32 devices in a mesh: dp: 32 (over z, y, x, core).
Axes of the slice: x: 2, y: 2, z: 4, core: 2. Of those that a mesh axis runs over, the one named last changes fastest.
Arguments:
- block_in: bfloat16 [131072, 384], P('dp'), may hold values from -6 to 6
- out_grad: bfloat16 [131072, 384], P('dp'), may hold values from -6 to 6
- live_counts: int32 [32], P('dp'), may hold values from 4 to 16, as said below
- qkv_weight: float32 [384, 1152], P(None, 'dp'), may hold values from -0.3125 to 0.3125
- proj_weight: float32 [384, 384], P(None, 'dp'), may hold values from -1.25 to 1.25
- up_weight: float32 [384, 1536], P(None, 'dp'), may hold values from -0.3125 to 0.3125
- down_weight: float32 [384, 1536], P(None, 'dp'), may hold values from -0.15625 to 0.15625
- feature_vectors: float32 [8, 384], replicated, may hold values from -0.6 to 1.5, as said below
- up_bias: float32 [1536], replicated, may hold values from -3 to 3
- qkv_moment: float32 [384, 1152], P(None, 'dp'), may hold values from -320 to 320
- proj_moment: float32 [384, 384], P(None, 'dp'), may hold values from -112 to 112
- up_moment: float32 [384, 1536], P(None, 'dp'), may hold values from -320 to 320
- down_moment: float32 [384, 1536], P(None, 'dp'), may hold values from -640 to 640
Outputs:
- block_out: float32 [131072, 384], P('dp')
- input_gradient: float32 [131072, 384], P('dp')
- qkv_gradient: float32 [384, 1152], P(None, 'dp')
- proj_gradient: float32 [384, 384], P(None, 'dp')
- up_gradient: float32 [384, 1536], P(None, 'dp')
- down_gradient: float32 [384, 1536], P(None, 'dp')
- vector_gradient: float32 [8, 384], replicated
- bias_gradient: float32 [1536], replicated
- qkv_updated: float32 [384, 1152], P(None, 'dp')
- proj_updated: float32 [384, 384], P(None, 'dp')
- up_updated: float32 [384, 1536], P(None, 'dp')
- down_updated: float32 [384, 1536], P(None, 'dp')
- qkv_state: float32 [384, 1152], P(None, 'dp')
- proj_state: float32 [384, 384], P(None, 'dp')
- up_state: float32 [384, 1536], P(None, 'dp')
- down_state: float32 [384, 1536], P(None, 'dp')
- vectors_updated: float32 [8, 384], replicated
- bias_updated: float32 [1536], replicated
The draws below stay inside these ranges and needn't reach their ends.
Inputs may be any that keep to these rules, and one draw needn't show every extreme that they name: The first live_counts[p] of the 16 image slots of index p are live; some index has all 16 live. `feature_vectors`: rows 0 and 5 lie in 0.5 to 1.5.
All inputs are finite; a program needn't handle non-finite values.
Results may differ from the reference program's by a relative error of at most 0.011.
Values may be sent and summed in bfloat16 or wider, within the bound.
No kernel may reach another device: no remote copies, remote signals or barrier semaphores. Data moves between devices by JAX's collectives and lax.ppermute only.
A program may use at most 192 MiB of HBM per device.

```python
import math
import jax
import jax.numpy as jnp
from jax import lax

D = 384
HEAD_DIM = 64
FF = 1536
SEQ = 256
IMG_DEV = 16
TOKENS = 131072
N_DP = 32


def draw_block_in(key, part):
    first = jax.random.fold_in(key, 0)
    base = jnp.clip(jax.random.normal(first, (TOKENS, D), jnp.float32), -6.0, 6.0)
    return base.astype(jnp.bfloat16)


def draw_live_counts(key, part):
    first, second = jax.random.split(key)
    counts = jax.random.randint(first, (N_DP,), max(1, IMG_DEV // 4), IMG_DEV + 1, dtype=jnp.int32)
    fullest = jax.random.randint(second, (), 0, N_DP, dtype=jnp.int32)
    return jnp.where(jnp.arange(N_DP, dtype=jnp.int32) == fullest, IMG_DEV, counts).astype(jnp.int32)


def draw_feature_vectors(key, part):
    first, second = jax.random.split(key)
    rows = jnp.arange(8, dtype=jnp.int32)[:, None]
    is_gain = (rows == 0) | (rows == 5)
    gains = 1.0 + 0.25 * jnp.clip(jax.random.normal(first, (8, D), jnp.float32), -2.0, 2.0)
    shifts = 0.3 * jnp.clip(jax.random.normal(second, (8, D), jnp.float32), -2.0, 2.0)
    return jnp.where(is_gain, gains, shifts).astype(jnp.float32)


def raised(values, rng, source, target, shards_of, factor):
    def block_of(position):
        return (jnp.arange(values.shape[position]) // (values.shape[position] // shards_of)).reshape((-1,) + (1,) * (values.ndim - 1 - position))

    one_side = jax.random.permutation(rng, shards_of)[block_of(target)]
    far = (block_of(target) + shards_of // 2) % shards_of
    return jnp.where((block_of(source) == one_side) | (block_of(source) == far), factor * values, values)


def block_levels(rng, dims, shards, low, largest):
    def one(axis_at, blocks):
        draws = jax.random.uniform(jax.random.fold_in(jax.random.fold_in(rng, 6), axis_at), (blocks,), jnp.float32, low / len(shards), largest / len(shards))
        return jnp.repeat(jnp.exp(draws), dims[axis_at] // blocks).reshape((-1,) + (1,) * (len(dims) - axis_at - 1))

    level = one(*shards[0])
    for cut in shards[1:]:
        level = level * one(*cut)
    return level


def gaussian(rng, extent, deviation, most, pieces=(), held_as=jnp.bfloat16):
    factor_of = block_levels(rng, extent, pieces, -0.22, 0.18) if pieces else 1.0
    values = jax.random.normal(rng, extent, jnp.float32) * deviation * factor_of
    return jnp.minimum(jnp.maximum(values, -most), most).astype(held_as)


def gaussian_with(rng, dims, deviation, most, shards, heavy, kind=jnp.bfloat16):
    values = deviation * jax.random.normal(rng, dims, jnp.float32)
    if shards:
        values = values * block_levels(rng, dims, shards, -0.22, 0.18)
    return jnp.clip(raised(values, jax.random.fold_in(rng, 3), *heavy), -most, most).astype(kind)


def setup_inputs(seed: int = 0) -> dict:
    streams_of = jax.random.split(jax.random.key(seed), 14)
    block_in = draw_block_in(jax.random.fold_in(streams_of[13], 71), 0)
    out_grad = gaussian_with(streams_of[1], (TOKENS, D), 1.0, 6.0, ((0, 32),), (0, 1, 32, 2.75))
    live_counts = draw_live_counts(jax.random.fold_in(streams_of[13], 71), 0)
    qkv_weight = gaussian(streams_of[3], (D, 3 * D), D ** -0.5, 0.3125, ((1, 32),), jnp.float32)
    proj_weight = gaussian(streams_of[4], (D, D), (D // 16) ** -0.5, 1.25, ((1, 32),), jnp.float32)
    up_weight = gaussian(streams_of[5], (D, FF), D ** -0.5, 0.3125, ((1, 32),), jnp.float32)
    down_weight = gaussian(streams_of[6], (D, FF), FF ** -0.5, 0.15625, ((1, 32),), jnp.float32)
    feature_vectors = draw_feature_vectors(jax.random.fold_in(streams_of[13], 71), 0)
    up_bias = gaussian(streams_of[8], (FF,), 0.5, 3.0, (), jnp.float32)
    qkv_moment = gaussian(streams_of[9], (D, 3 * D), (0.15 * TOKENS ** 0.5), 320.0, ((1, 32),), jnp.float32)
    proj_moment = gaussian(streams_of[10], (D, D), (0.05 * TOKENS ** 0.5), 112.0, ((1, 32),), jnp.float32)
    up_moment = gaussian(streams_of[11], (D, FF), (0.15 * TOKENS ** 0.5), 320.0, ((1, 32),), jnp.float32)
    down_moment = gaussian(streams_of[12], (D, FF), (0.3 * TOKENS ** 0.5), 640.0, ((1, 32),), jnp.float32)
    return dict(block_in=block_in, out_grad=out_grad, live_counts=live_counts, qkv_weight=qkv_weight, proj_weight=proj_weight, up_weight=up_weight, down_weight=down_weight, feature_vectors=feature_vectors, up_bias=up_bias, qkv_moment=qkv_moment, proj_moment=proj_moment, up_moment=up_moment, down_moment=down_moment)


norm_eps = 1e-06
newton_a = 3.4445
newton_b = -4.775
newton_c = 2.0315
momentum_decay = 0.9
matrix_rate = 0.15
vector_rate = 0.2

def layer_norm(inputs, gain, shift):
    center = inputs - lax.optimization_barrier(jnp.mean(inputs, axis=-1, keepdims=True))
    scale = lax.rsqrt(lax.optimization_barrier(jnp.mean(center * center, axis=-1, keepdims=True)) + norm_eps)
    normed = center * scale
    return (normed, scale, normed * gain + shift)

def norm_back(upstream, normed, scale, gain):
    inner = upstream * gain
    return scale * (inner - lax.optimization_barrier(jnp.mean(inner, axis=-1, keepdims=True)) - normed * lax.optimization_barrier(jnp.mean(inner * normed, axis=-1, keepdims=True)))

def gelu_exact(values):
    return 0.5 * values * (1.0 + lax.erf(values * (1.0 / math.sqrt(2.0))))

def gelu_slope(values):
    return 0.5 * (1.0 + lax.erf(values * (1.0 / math.sqrt(2.0)))) + values * jnp.exp(-0.5 * values * values) * (1.0 / math.sqrt(2.0 * math.pi))

def contract_rows(left, right):
    return lax.dot_general(left, right, (((0,), (0,)), ((), ())), preferred_element_type=jnp.float32)

def contract_cols(left, right):
    return lax.dot_general(left, right, (((1,), (1,)), ((), ())), preferred_element_type=jnp.float32)

def block_pass(inputs, cotangent, alive, qkv_b, proj_b, up_b, down_b, vectors, up_bias):
    count = inputs.shape[0]
    width = inputs.shape[2]
    rows = count * SEQ
    heads = width // HEAD_DIM
    scale_qk = 1.0 / math.sqrt(HEAD_DIM)

    def split(array):
        return array.reshape(count, SEQ, heads, HEAD_DIM).astype(jnp.float32)
    residual = inputs.reshape(rows, width).astype(jnp.float32)
    row_alive = jnp.repeat(alive, SEQ)[:, None]
    normed_one, scale_one, mixed_one = layer_norm(residual, vectors[0], vectors[1])
    normal_one = mixed_one.astype(jnp.bfloat16)
    projected = jnp.dot(normal_one, qkv_b, preferred_element_type=jnp.float32)
    query = (projected[:, :width] + vectors[2]).astype(jnp.bfloat16)
    keys = projected[:, width:2 * width].astype(jnp.bfloat16)
    values = (projected[:, 2 * width:] + vectors[3]).astype(jnp.bfloat16)
    query_h = split(query)
    keys_h = split(keys)
    values_h = split(values)
    scores = jnp.einsum('nqhd,nkhd->nhqk', query_h, keys_h) * scale_qk
    top = lax.optimization_barrier(jnp.max(scores, axis=-1, keepdims=True))
    log_total = top + jnp.log(lax.optimization_barrier(jnp.sum(jnp.exp(scores - top), axis=-1, keepdims=True)))
    attend = jnp.exp(scores - log_total)
    attend_b = attend.astype(jnp.bfloat16)
    heads_out = jnp.einsum('nhqk,nkhd->nqhd', attend_b.astype(jnp.float32), values_h)
    attn_b = heads_out.reshape(rows, width).astype(jnp.bfloat16)
    hidden_one = residual + jnp.dot(attn_b, proj_b, preferred_element_type=jnp.float32) + vectors[4]
    normed_two, scale_two, mixed_two = layer_norm(hidden_one, vectors[5], vectors[6])
    normal_two = mixed_two.astype(jnp.bfloat16)
    pre_act = jnp.dot(normal_two, up_b, preferred_element_type=jnp.float32) + up_bias
    active = gelu_exact(pre_act).astype(jnp.bfloat16)
    down_out = contract_cols(active, down_b)
    result = (hidden_one + down_out + vectors[7]) * row_alive
    cot_b = jnp.where(row_alive > 0.5, cotangent.reshape(rows, width), jnp.zeros((), jnp.bfloat16))
    cot_f = cot_b.astype(jnp.float32)
    down_grad = contract_rows(cot_b, active)
    pre_grad = jnp.dot(cot_b, down_b, preferred_element_type=jnp.float32) * gelu_slope(pre_act)
    pre_grad_b = pre_grad.astype(jnp.bfloat16)
    up_grad = contract_rows(normal_two, pre_grad_b)
    mixed_two_grad = contract_cols(pre_grad_b, up_b)
    hidden_grad = norm_back(mixed_two_grad, normed_two, scale_two, vectors[5]) + cot_f
    hidden_grad_b = hidden_grad.astype(jnp.bfloat16)
    proj_grad = contract_rows(attn_b, hidden_grad_b)
    attn_grad_b = contract_cols(hidden_grad_b, proj_b).astype(jnp.bfloat16)
    attn_grad_h = split(attn_grad_b)
    delta = jnp.transpose(lax.optimization_barrier(jnp.sum(attn_grad_h * split(attn_b), axis=-1)), (0, 2, 1))[..., None]
    values_grad = jnp.einsum('nhqk,nqhd->nkhd', attend_b.astype(jnp.float32), attn_grad_h)
    attend_grad = jnp.einsum('nqhd,nkhd->nhqk', attn_grad_h, values_h)
    score_grad = (attend * (attend_grad - delta) * scale_qk).astype(jnp.bfloat16).astype(jnp.float32)
    query_grad = jnp.einsum('nhqk,nkhd->nqhd', score_grad, keys_h).reshape(rows, width)
    keys_grad = jnp.einsum('nhqk,nqhd->nkhd', score_grad, query_h).reshape(rows, width)
    values_grad = values_grad.reshape(rows, width)
    packed_grad = jnp.concatenate([query_grad, keys_grad, values_grad], axis=1).astype(jnp.bfloat16)
    qkv_grad = contract_rows(normal_one, packed_grad)
    mixed_one_grad = contract_cols(packed_grad, qkv_b)
    input_grad = norm_back(mixed_one_grad, normed_one, scale_one, vectors[0]) + hidden_grad
    vector_grad = jnp.stack([lax.optimization_barrier(jnp.sum(mixed_one_grad * normed_one, axis=0)), lax.optimization_barrier(jnp.sum(mixed_one_grad, axis=0)), lax.optimization_barrier(jnp.sum(query_grad, axis=0)), lax.optimization_barrier(jnp.sum(values_grad, axis=0)), lax.optimization_barrier(jnp.sum(hidden_grad, axis=0)), lax.optimization_barrier(jnp.sum(mixed_two_grad * normed_two, axis=0)), lax.optimization_barrier(jnp.sum(mixed_two_grad, axis=0)), lax.optimization_barrier(jnp.sum(cot_f, axis=0))])
    bias_grad = lax.optimization_barrier(jnp.sum(pre_grad, axis=0))
    return (result, input_grad, (qkv_grad, proj_grad, up_grad, down_grad, vector_grad, bias_grad))

def orthogonalize(moment):
    ortho = moment * lax.rsqrt(jnp.sum(moment * moment) + norm_eps)
    for turn in range(5):
        gram = jnp.dot(ortho, ortho.T, precision=lax.Precision.HIGHEST)
        poly = newton_b * gram + newton_c * jnp.dot(gram, gram, precision=lax.Precision.HIGHEST)
        ortho = newton_a * ortho + jnp.dot(poly, ortho, precision=lax.Precision.HIGHEST)
    return ortho

def normalized_step(param, gradient):
    return param - vector_rate * gradient * lax.rsqrt(lax.optimization_barrier(jnp.mean(gradient * gradient, axis=-1, keepdims=True)) + norm_eps)

def reference(block_in, out_grad, live_counts, qkv_weight, proj_weight, up_weight, down_weight, feature_vectors, up_bias, qkv_moment, proj_moment, up_moment, down_moment):
    width = block_in.shape[1]
    groups = live_counts.shape[0]
    slots = block_in.shape[0] // (groups * SEQ)
    alive = (jnp.arange(slots, dtype=jnp.int32)[None, :] < live_counts[:, None]).astype(jnp.float32)
    matrices = (qkv_weight, proj_weight, up_weight, down_weight)
    rounded = tuple((matrix.astype(jnp.bfloat16) for matrix in matrices))
    inputs = block_in.reshape(groups, slots, SEQ, width)
    cotangents = out_grad.reshape(groups, slots, SEQ, width)
    initial = tuple((jnp.zeros(matrix.shape, jnp.float32) for matrix in matrices)) + (jnp.zeros(feature_vectors.shape, jnp.float32), jnp.zeros(up_bias.shape, jnp.float32))

    def visit(carry, piece):
        result, input_grad, grads = block_pass(piece[0], piece[1], piece[2], rounded[0], rounded[1], rounded[2], rounded[3], feature_vectors, up_bias)
        return (tuple((total + grad for total, grad in zip(carry, grads))), (result, input_grad))
    totals, (results, input_grads) = lax.scan(visit, initial, (inputs, cotangents, alive))
    moments = (qkv_moment, proj_moment, up_moment, down_moment)
    states = []
    updated = []
    for index in range(4):
        state = momentum_decay * moments[index] + totals[index]
        states.append(state)
        columns = matrices[index].shape[1]
        updated.append(matrices[index] - matrix_rate * 0.2 * math.sqrt(columns) * orthogonalize(state))
    return (results.reshape(block_in.shape), input_grads.reshape(block_in.shape), totals[0], totals[1], totals[2], totals[3], totals[4], totals[5], updated[0], updated[1], updated[2], updated[3], states[0], states[1], states[2], states[3], normalized_step(feature_vectors, totals[4]), normalized_step(up_bias, totals[5]))
```

```python
import functools
import math

import jax
import jax.numpy as jnp
from jax import lax
from jax.experimental import pallas as pl
from jax.experimental.pallas import tpu as pltpu
from jax.sharding import PartitionSpec as P

HEAD_DIM = 64
SEQ = 256
GROUP = 2
LANES = 128

norm_eps = 1e-06
newton_a = 3.4445
newton_b = -4.775
newton_c = 2.0315
momentum_decay = 0.9
matrix_rate = 0.15
vector_rate = 0.2

f32 = jnp.float32
bf16 = jnp.bfloat16


def nn(a, b):
    return lax.dot_general(a, b, (((1,), (0,)), ((), ())), preferred_element_type=f32)


def nt(a, b):
    return lax.dot_general(a, b, (((1,), (1,)), ((), ())), preferred_element_type=f32)


def tn(a, b):
    return lax.dot_general(a, b, (((0,), (0,)), ((), ())), preferred_element_type=f32)


def cols(index):
    return slice(index * LANES, (index + 1) * LANES)


def norm_parts(chunk):
    width = chunk.shape[0]
    center = chunk - jnp.sum(chunk, axis=0, keepdims=True) * (1.0 / width)
    scale = lax.rsqrt(jnp.sum(center * center, axis=0, keepdims=True) * (1.0 / width) + norm_eps)
    return center * scale, scale


def norm_back(inner, normed, scale):
    width = inner.shape[0]
    mean = jnp.sum(inner, axis=0, keepdims=True) * (1.0 / width)
    cross = jnp.sum(inner * normed, axis=0, keepdims=True) * (1.0 / width)
    return scale * (inner - mean - normed * cross)


def normal_parts(u):
    size = jnp.abs(u)
    density = jnp.exp(u * u * (-0.5))
    t = 1.0 / (1.0 + (0.3275911 / math.sqrt(2.0)) * size)
    poly = t * (
        0.5 * 0.254829592
        + t
        * (
            0.5 * -0.284496736
            + t * (0.5 * 1.421413741 + t * (0.5 * -1.453152027 + t * (0.5 * 1.061405429)))
        )
    )
    tail = poly * density
    return jnp.where(u >= 0.0, 1.0 - tail, tail), density * (1.0 / math.sqrt(2.0 * math.pi))


def split3(x):
    high = x.astype(bf16)
    return high, (x - high.astype(f32)).astype(bf16)


def mul3(a, b):
    ah, al = split3(a)
    bh, bl = split3(b)
    return nn(ah, bh) + (nn(ah, bl) + nn(al, bh))


def assemble(par, own_ref, other_ref, first, count, stage):
    for shard in range(2 * own_ref.shape[0]):
        mine = own_ref[shard // 2, first : first + count, :].astype(f32)
        theirs = other_ref[shard // 2, first : first + count, :].astype(f32)
        stage[shard * count : (shard + 1) * count, :] = jnp.where(par == shard % 2, mine, theirs)


def emit(par, pieces, vector, keep_ref, send_ref, stage):
    count = 2 * keep_ref.shape[0]
    sizes = [piece.shape[0] // count for piece in pieces]
    rows = sum(sizes)
    width = pieces[0].shape[1]
    stage[...] = jnp.zeros_like(stage)
    base = rows * (width // LANES)
    for index, row in enumerate(vector):
        stage[base + index : base + index + 1, :] = row.astype(bf16).astype(f32)
    for shard in range(count):
        for c in range(width // LANES):
            low = c * rows
            for piece, size in zip(pieces, sizes):
                stage[low : low + size, :] = piece[shard * size : (shard + 1) * size, cols(c)]
                low += size

        @pl.when(par == shard % 2)
        def _():
            keep_ref[shard // 2] = stage[...]

        @pl.when(par != shard % 2)
        def _():
            send_ref[shard // 2] = stage[...].astype(bf16)


def lane_rows(acc):
    out = []
    for c in range(acc.shape[0] // LANES):
        out.append(jnp.sum(acc[cols(c), :].T, axis=0, keepdims=True))
    return out


def prep_kernel(wq_ref, wp_ref, wu_ref, wd_ref, first_ref, second_ref):
    first = wq_ref[...].T.astype(bf16)
    second = jnp.concatenate([wu_ref[...].T, wd_ref[...].T, wp_ref[...].T], axis=0).astype(bf16)
    for index in range(first_ref.shape[0]):
        first_ref[index] = first
        second_ref[index] = second


def attend_kernel(
    info, x_ref, own_ref, other_ref, vec_ref, qkv_ref, att_ref, out_ref, wq_ref, z_scr, stage
):
    width, lanes = z_scr.shape
    heads = width // HEAD_DIM

    @pl.when(pl.program_id(0) == 0)
    def _():
        assemble(info[1], own_ref, other_ref, 0, own_ref.shape[1], stage)
        wq_ref[...] = stage[...].astype(bf16)

    @pl.when(pl.program_id(0) * GROUP < info[0])
    def _():
        for c in range(lanes // LANES):
            chunk = x_ref[cols(c), :].astype(f32).T
            normed, _ = norm_parts(chunk)
            z_scr[:, cols(c)] = (normed * vec_ref[0] + vec_ref[1]).astype(bf16)
        for part in range(3):
            rows = slice(part * width, (part + 1) * width)
            made = nn(wq_ref[rows, :], z_scr[...])
            for c in range(lanes // LANES):
                piece = made[:, cols(c)]
                if part == 0:
                    piece = (piece + vec_ref[2]) * (1.0 / math.sqrt(HEAD_DIM))
                elif part == 2:
                    piece = piece + vec_ref[3]
                qkv_ref[rows, cols(c)] = piece.astype(bf16)
        for image in range(lanes // SEQ):
            span = slice(image * SEQ, (image + 1) * SEQ)
            for head in range(heads):
                low = head * HEAD_DIM
                query = qkv_ref[low : low + HEAD_DIM, span]
                keys = qkv_ref[width + low : width + low + HEAD_DIM, span]
                values = qkv_ref[2 * width + low : 2 * width + low + HEAD_DIM, span]
                scores = tn(keys, query)
                top = jnp.max(scores, axis=0, keepdims=True)
                raised = jnp.exp(scores - top)
                total = jnp.sum(raised, axis=0, keepdims=True)
                attend = (raised * (1.0 / total)).astype(bf16)
                base = (image * heads + head) * SEQ
                att_ref[base : base + SEQ, :] = attend
                out_ref[low : low + HEAD_DIM, span] = nn(values, attend).astype(bf16)


def mlp_kernel(
    info, x_ref, cot_ref, att_ref, own_ref, other_ref, vec_ref, ub_ref,
    out_ref, dh_ref, gp_ref, wpn_ref, keep_ref, send_ref,
    wun_scr, wdn_scr, wp_scr, wu_scr, wd_scr, gu_scr, gd_scr, rows_scr, bias_scr,
    h_scr, n_scr, z_scr, m_scr, act_scr, du_scr, dhb_scr, s_scr, stage, wide,
):
    width, lanes = z_scr.shape
    ff = wu_scr.shape[0]
    devices = 2 * own_ref.shape[0]
    step = pl.program_id(0)
    block = 256

    @pl.when(step == 0)
    def _():
        gp_ref[...] = jnp.zeros_like(gp_ref)
        gu_scr[...] = jnp.zeros_like(gu_scr)
        gd_scr[...] = jnp.zeros_like(gd_scr)
        rows_scr[...] = jnp.zeros_like(rows_scr)
        bias_scr[...] = jnp.zeros_like(bias_scr)
        part = ff // devices
        assemble(info[1], own_ref, other_ref, 2 * part, width // devices, wide.at[:width])
        wp_scr[...] = wide[:width, :].astype(bf16)
        wpn_ref[...] = wide[:width, :].T.astype(bf16)
        assemble(info[1], own_ref, other_ref, 0, part, wide)
        wu_scr[...] = wide[...].astype(bf16)
        for c in range(ff // block):
            rows = slice(c * block, (c + 1) * block)
            wun_scr[:, rows] = wide[rows, :].T.astype(bf16)
        assemble(info[1], own_ref, other_ref, part, part, wide)
        wd_scr[...] = wide[...].astype(bf16)
        for c in range(ff // block):
            rows = slice(c * block, (c + 1) * block)
            wdn_scr[:, rows] = wide[rows, :].T.astype(bf16)

    @pl.when(step * GROUP >= info[0])
    def _():
        out_ref[...] = jnp.zeros_like(out_ref)

    @pl.when(step * GROUP < info[0])
    def _():
        made = nn(wp_scr[...], att_ref[...])
        total7 = jnp.zeros((width, LANES), f32)
        for c in range(lanes // LANES):
            chunk = x_ref[cols(c), :].astype(f32).T + made[:, cols(c)] + vec_ref[4]
            h_scr[:, cols(c)] = chunk
            normed, scale = norm_parts(chunk)
            n_scr[:, cols(c)] = normed
            s_scr[:, cols(c)] = scale
            z_scr[:, cols(c)] = (normed * vec_ref[5] + vec_ref[6]).astype(bf16)
            image = step * GROUP + c * LANES // SEQ
            cot = jnp.where(image < info[0], cot_ref[cols(c), :].astype(f32), 0.0).T
            m_scr[:, cols(c)] = cot.astype(bf16)
            total7 += cot
        rows_scr[3] += total7
        for c in range(ff // block):
            rows = slice(c * block, (c + 1) * block)
            u_all = nn(wu_scr[rows, :], z_scr[...])
            d_all = nn(wd_scr[rows, :], m_scr[...])
            bias = jnp.zeros((block, LANES), f32)
            for k in range(lanes // LANES):
                u = u_all[:, cols(k)] + ub_ref[rows, :]
                cdf, density = normal_parts(u)
                act_scr[rows, cols(k)] = (u * cdf).astype(bf16)
                du = d_all[:, cols(k)] * (cdf + u * density)
                du_scr[rows, cols(k)] = du.astype(bf16)
                bias += du
            bias_scr[rows, :] += bias
            gu_scr[rows, :] += nt(du_scr[rows, :], z_scr[...])
            gd_scr[rows, :] += nt(act_scr[rows, :], m_scr[...])
        down = nn(wdn_scr[...], act_scr[...])
        for c in range(lanes // LANES):
            image = step * GROUP + c * LANES // SEQ
            whole = down[:, cols(c)] + h_scr[:, cols(c)] + vec_ref[7]
            out_ref[cols(c), :] = jnp.where(image < info[0], whole, 0.0).T
        dz = nn(wun_scr[...], du_scr[...])
        total4 = jnp.zeros((width, LANES), f32)
        total5 = jnp.zeros((width, LANES), f32)
        total6 = jnp.zeros((width, LANES), f32)
        for c in range(lanes // LANES):
            piece = dz[:, cols(c)]
            normed = n_scr[:, cols(c)]
            dh = norm_back(piece * vec_ref[5], normed, s_scr[:, cols(c)]) + m_scr[:, cols(c)].astype(f32)
            dh_ref[:, cols(c)] = dh
            dhb_scr[:, cols(c)] = dh.astype(bf16)
            total4 += dh
            total5 += piece * normed
            total6 += piece
        rows_scr[0] += total4
        rows_scr[1] += total5
        rows_scr[2] += total6
        gp_ref[...] += nt(dhb_scr[...], att_ref[...])

    @pl.when(step == pl.num_programs(0) - 1)
    def _():
        vector = []
        for index in range(4):
            vector += lane_rows(rows_scr[index])
        vector += lane_rows(bias_scr)
        emit(info[1], (gu_scr, gd_scr), vector, keep_ref, send_ref, stage)


def back_kernel(
    info, x_ref, qkv_ref, att_ref, dh_ref, wpn_ref, wq_ref, gp_ref, vec_ref,
    out_ref, keep_ref, send_ref,
    wqn_scr, n_scr, z_scr, s_scr, da_scr, dqkv_scr, gq_scr, rows_scr, stage,
):
    width, lanes = z_scr.shape
    heads = width // HEAD_DIM
    step = pl.program_id(0)

    @pl.when(step == 0)
    def _():
        gq_scr[...] = jnp.zeros_like(gq_scr)
        rows_scr[...] = jnp.zeros_like(rows_scr)
        for c in range(3):
            rows = slice(c * width, (c + 1) * width)
            wqn_scr[:, rows] = wq_ref[rows, :].T

    @pl.when(step * GROUP >= info[0])
    def _():
        out_ref[...] = jnp.zeros_like(out_ref)

    @pl.when(step * GROUP < info[0])
    def _():
        da_scr[...] = nn(wpn_ref[...], dh_ref[...].astype(bf16)).astype(bf16)
        for c in range(lanes // LANES):
            chunk = x_ref[cols(c), :].astype(f32).T
            normed, scale = norm_parts(chunk)
            n_scr[:, cols(c)] = normed
            s_scr[:, cols(c)] = scale
            z_scr[:, cols(c)] = (normed * vec_ref[0] + vec_ref[1]).astype(bf16)
        for image in range(lanes // SEQ):
            span = slice(image * SEQ, (image + 1) * SEQ)
            for head in range(heads):
                low = head * HEAD_DIM
                high = low + HEAD_DIM
                query = qkv_ref[low:high, span]
                keys = qkv_ref[width + low : width + high, span]
                values = qkv_ref[2 * width + low : 2 * width + high, span]
                grad = da_scr[low:high, span]
                base = (image * heads + head) * SEQ
                attend = att_ref[base : base + SEQ, :]
                attend_f = attend.astype(f32)
                upstream = tn(values, grad)
                delta = jnp.sum(attend_f * upstream, axis=0, keepdims=True)
                dscore = (attend_f * (upstream - delta)).astype(bf16)
                dquery = nn(keys, dscore) * (1.0 / math.sqrt(HEAD_DIM))
                dkey = nt(query, dscore)
                dvalue = nt(grad, attend)
                dqkv_scr[low:high, span] = dquery.astype(bf16)
                dqkv_scr[width + low : width + high, span] = dkey.astype(bf16)
                dqkv_scr[2 * width + low : 2 * width + high, span] = dvalue.astype(bf16)
                rows_scr[2, low:high, :] += dquery[:, :LANES] + dquery[:, LANES:]
                rows_scr[3, low:high, :] += dvalue[:, :LANES] + dvalue[:, LANES:]
        for part in range(3):
            rows = slice(part * width, (part + 1) * width)
            gq_scr[rows, :] += nt(dqkv_scr[rows, :], z_scr[...])
        dz = nn(wqn_scr[...], dqkv_scr[...])
        total0 = jnp.zeros((width, LANES), f32)
        total1 = jnp.zeros((width, LANES), f32)
        for c in range(lanes // LANES):
            piece = dz[:, cols(c)]
            normed = n_scr[:, cols(c)]
            dx = norm_back(piece * vec_ref[0], normed, s_scr[:, cols(c)]) + dh_ref[:, cols(c)]
            out_ref[cols(c), :] = dx.T
            total0 += piece * normed
            total1 += piece
        rows_scr[0] += total0
        rows_scr[1] += total1

    @pl.when(step == pl.num_programs(0) - 1)
    def _():
        vector = []
        for index in range(4):
            vector += lane_rows(rows_scr[index])
        emit(info[1], (gq_scr, gp_ref), vector, keep_ref, send_ref, stage)


def state_kernel(got_ref, ma_ref, mb_ref, ga_ref, gb_ref, sa_ref, sb_ref, spread_ref, state_ref, vec_ref):
    width, first = ma_ref.shape
    second = mb_ref.shape[1]
    rows = first + second
    total = got_ref[0].astype(f32)
    for index in range(1, got_ref.shape[0]):
        total += got_ref[index].astype(f32)
    blocks = width // LANES
    grad = jnp.concatenate([total[c * rows : (c + 1) * rows] for c in range(blocks)], axis=1)
    vec_ref[...] = total[blocks * rows : blocks * rows + vec_ref.shape[0]]
    natural = grad.T
    ga_ref[...] = natural[:, :first]
    gb_ref[...] = natural[:, first:]
    state_a = momentum_decay * ma_ref[...] + natural[:, :first]
    state_b = momentum_decay * mb_ref[...] + natural[:, first:]
    sa_ref[...] = state_a
    sb_ref[...] = state_b
    state = jnp.concatenate([state_a, state_b], axis=1).T
    state_ref[...] = state
    for index in range(spread_ref.shape[0]):
        spread_ref[index] = state.astype(bf16)


def newton_kernel(columns, own_ref, other_ref, state_ref, wa_ref, wb_ref, ua_ref, ub_ref):
    count, rows, width = own_ref.shape
    first = wa_ref.shape[1]
    spans = ((0, first), (first, rows))
    grams = []
    for low, high in spans:
        gram = jnp.zeros((width, width), f32)
        for ref in (own_ref, other_ref):
            part = jnp.concatenate(
                [ref[index, low:high, :].astype(f32) for index in range(count)], axis=0
            ).astype(bf16)
            gram += tn(part, part)
        grams.append(gram)
    eye = (
        lax.broadcasted_iota(jnp.int32, (width, width), 0)
        == lax.broadcasted_iota(jnp.int32, (width, width), 1)
    ).astype(f32)
    for gram, (low, high), w_ref, u_ref, wide in zip(
        grams, spans, (wa_ref, wb_ref), (ua_ref, ub_ref), columns
    ):
        norm = lax.rsqrt(jnp.sum(gram * eye) + norm_eps)
        gram = gram * (norm * norm)
        whole = None
        for turn in range(5):
            poly = newton_a * eye + newton_b * gram + newton_c * mul3(gram, gram)
            whole = poly if whole is None else mul3(poly, whole)
            if turn < 4:
                gram = mul3(mul3(poly, gram), poly)
        sh, sl = split3(state_ref[low:high, :] * norm)
        ph, pl_ = split3(whole)
        ortho = nt(ph, sh) + (nt(ph, sl) + nt(pl_, sh))
        u_ref[...] = w_ref[...] - (matrix_rate * 0.2 * math.sqrt(wide)) * ortho


def fixed(shape):
    return pl.BlockSpec(shape, lambda i, info: (0,) * len(shape))


def params(grid=True):
    return pltpu.CompilerParams(
        dimension_semantics=("arbitrary",) if grid else None, vmem_limit_bytes=60 * 1024 * 1024
    )


def shape_of(shape, dtype):
    return jax.ShapeDtypeStruct(shape, dtype)


def small_call(kernel, outs, name):
    return pl.pallas_call(
        kernel,
        out_shape=[shape_of(*out) for out in outs],
        compiler_params=params(False),
        name=name,
    )


def padded(rows):
    return -(-rows // 16) * 16


def body(
    block_in,
    out_grad,
    live_counts,
    qkv_weight,
    proj_weight,
    up_weight,
    down_weight,
    feature_vectors,
    up_bias,
    qkv_moment,
    proj_moment,
    up_moment,
    down_moment,
):
    devices = lax.axis_size("dp")
    half = devices // 2
    par = lax.axis_index("dp") % 2
    width = block_in.shape[1]
    heads = width // HEAD_DIM
    slots = block_in.shape[0] // SEQ
    groups = slots // GROUP
    lanes = GROUP * SEQ
    cq, cp, cu, cd = (w.shape[1] for w in (qkv_weight, proj_weight, up_weight, down_weight))
    ff = cu * devices
    blocks = width // LANES
    pairs = [(i, i ^ 1) for i in range(devices)]
    planes = [[2 * i + c for i in range(half)] for c in range(2)]
    info = jnp.stack([live_counts[0], par.astype(jnp.int32)])
    vec = jnp.broadcast_to(feature_vectors[:, :, None], feature_vectors.shape + (LANES,))
    ub = jnp.broadcast_to(up_bias[:, None], up_bias.shape + (LANES,))

    def exchange(x):
        return lax.all_to_all(x, "dp", 0, 0, axis_index_groups=planes, tiled=True)

    def swap(x):
        return lax.ppermute(x, "dp", pairs)

    first, second = small_call(
        prep_kernel,
        [((half, cq, width), bf16), ((half, cu + cd + cp, width), bf16)],
        "prep",
    )(qkv_weight, proj_weight, up_weight, down_weight)
    wq_own = exchange(first)
    wq_other = swap(wq_own)
    second, wq_own = lax.optimization_barrier((second, wq_own))
    rest_own = exchange(second)
    rest_other = swap(rest_own)

    tokens = lambda i, info: (i, 0)
    deep = lambda i, info: (i, 0, 0)
    token_spec = pl.BlockSpec((lanes, width), tokens)
    deep_spec = pl.BlockSpec((None, width, lanes), deep)
    qkv_spec = pl.BlockSpec((None, 3 * width, lanes), deep)
    att_spec = pl.BlockSpec((None, GROUP * heads * SEQ, SEQ), deep)

    qkv, att, attn, wq = pl.pallas_call(
        attend_kernel,
        grid_spec=pltpu.PrefetchScalarGridSpec(
            num_scalar_prefetch=1,
            grid=(groups,),
            in_specs=[token_spec, fixed(wq_own.shape), fixed(wq_own.shape), fixed(vec.shape)],
            out_specs=[qkv_spec, att_spec, deep_spec, fixed((3 * width, width))],
            scratch_shapes=[pltpu.VMEM((width, lanes), bf16), pltpu.VMEM((3 * width, width), f32)],
        ),
        out_shape=[
            shape_of((groups, 3 * width, lanes), bf16),
            shape_of((groups, GROUP * heads * SEQ, SEQ), bf16),
            shape_of((groups, width, lanes), bf16),
            shape_of((3 * width, width), bf16),
        ],
        compiler_params=params(),
        cost_estimate=pl.CostEstimate(flops=40_000_000_000, bytes_accessed=30_000_000, transcendentals=0),
        name="attend",
    )(info, block_in, wq_own, wq_other, vec)

    rows_b = padded(blocks * (cu + cd) + 4 * blocks + ff // LANES)
    out, dh, gp, wpn, keep_b, send_b = pl.pallas_call(
        mlp_kernel,
        grid_spec=pltpu.PrefetchScalarGridSpec(
            num_scalar_prefetch=1,
            grid=(groups,),
            in_specs=[
                token_spec, token_spec, deep_spec,
                fixed(rest_own.shape), fixed(rest_own.shape), fixed(vec.shape), fixed(ub.shape),
            ],
            out_specs=[
                token_spec, deep_spec, fixed((width, width)), fixed((width, width)),
                fixed((half, rows_b, LANES)), fixed((half, rows_b, LANES)),
            ],
            scratch_shapes=[
                pltpu.VMEM((width, ff), bf16),
                pltpu.VMEM((width, ff), bf16),
                pltpu.VMEM((width, width), bf16),
                pltpu.VMEM((ff, width), bf16),
                pltpu.VMEM((ff, width), bf16),
                pltpu.VMEM((ff, width), f32),
                pltpu.VMEM((ff, width), f32),
                pltpu.VMEM((4, width, LANES), f32),
                pltpu.VMEM((ff, LANES), f32),
                pltpu.VMEM((width, lanes), f32),
                pltpu.VMEM((width, lanes), f32),
                pltpu.VMEM((width, lanes), bf16),
                pltpu.VMEM((width, lanes), bf16),
                pltpu.VMEM((ff, lanes), bf16),
                pltpu.VMEM((ff, lanes), bf16),
                pltpu.VMEM((width, lanes), bf16),
                pltpu.VMEM((1, lanes), f32),
                pltpu.VMEM((rows_b, LANES), f32),
                pltpu.VMEM((ff, width), f32),
            ],
        ),
        out_shape=[
            shape_of(block_in.shape, f32),
            shape_of((groups, width, lanes), f32),
            shape_of((width, width), f32),
            shape_of((width, width), bf16),
            shape_of((half, rows_b, LANES), f32),
            shape_of((half, rows_b, LANES), bf16),
        ],
        compiler_params=params(),
        cost_estimate=pl.CostEstimate(flops=80_000_000_000, bytes_accessed=30_000_000, transcendentals=0),
        name="mlp",
    )(info, block_in, out_grad, attn, rest_own, rest_other, vec, ub)

    def gather_sums(keep, send):
        return exchange((keep + swap(send).astype(f32)).astype(bf16))

    got_b = gather_sums(keep_b, send_b)

    rows_a = padded(blocks * (cq + cp) + 4 * blocks)
    dx, keep_a, send_a = pl.pallas_call(
        back_kernel,
        grid_spec=pltpu.PrefetchScalarGridSpec(
            num_scalar_prefetch=1,
            grid=(groups,),
            in_specs=[
                token_spec, qkv_spec, att_spec, deep_spec,
                fixed(wpn.shape), fixed(wq.shape), fixed(gp.shape), fixed(vec.shape),
            ],
            out_specs=[token_spec, fixed((half, rows_a, LANES)), fixed((half, rows_a, LANES))],
            scratch_shapes=[
                pltpu.VMEM((width, 3 * width), bf16),
                pltpu.VMEM((width, lanes), f32),
                pltpu.VMEM((width, lanes), bf16),
                pltpu.VMEM((1, lanes), f32),
                pltpu.VMEM((width, lanes), bf16),
                pltpu.VMEM((3 * width, lanes), bf16),
                pltpu.VMEM((3 * width, width), f32),
                pltpu.VMEM((4, width, LANES), f32),
                pltpu.VMEM((rows_a, LANES), f32),
            ],
        ),
        out_shape=[
            shape_of(block_in.shape, f32),
            shape_of((half, rows_a, LANES), f32),
            shape_of((half, rows_a, LANES), bf16),
        ],
        compiler_params=params(),
        cost_estimate=pl.CostEstimate(flops=60_000_000_000, bytes_accessed=40_000_000, transcendentals=0),
        name="back",
    )(info, block_in, qkv, att, dh, wpn, wq, gp, vec)
    got_a = gather_sums(keep_a, send_a)

    def muon(got, moment_a, moment_b, weight_a, weight_b, vectors, name):
        ca, cb = moment_a.shape[1], moment_b.shape[1]
        ga, gb, sa, sb, spread, state, vector = small_call(
            state_kernel,
            [
                (moment_a.shape, f32), (moment_b.shape, f32), (moment_a.shape, f32), (moment_b.shape, f32),
                ((half, ca + cb, width), bf16), ((ca + cb, width), f32), ((vectors, LANES), f32),
            ],
            name + "_state",
        )(got, moment_a, moment_b)
        own = exchange(spread)
        other = swap(own)
        ua, ub_ = small_call(
            functools.partial(newton_kernel, (ca * devices, cb * devices)),
            [(moment_a.shape, f32), (moment_b.shape, f32)],
            name + "_newton",
        )(own, other, state, weight_a, weight_b)
        return ga, gb, sa, sb, ua, ub_, vector

    gu, gd, su, sd, uu, ud, vector_b = muon(
        got_b, up_moment, down_moment, up_weight, down_weight, 4 * blocks + ff // LANES, "mlp"
    )
    gq, gpr, sq, sp, uq, up, vector_a = muon(
        got_a, qkv_moment, proj_moment, qkv_weight, proj_weight, 4 * blocks, "att"
    )
    vector_grad = jnp.concatenate(
        [vector_a.reshape(4, width), vector_b[: 4 * blocks].reshape(4, width)], axis=0
    )
    bias_grad = vector_b[4 * blocks :].reshape(ff)

    def normalized_step(param, gradient):
        return param - vector_rate * gradient * lax.rsqrt(
            jnp.mean(gradient * gradient, axis=-1, keepdims=True) + norm_eps
        )

    return (
        out, dx, gq, gpr, gu, gd, vector_grad, bias_grad, uq, up, uu, ud, sq, sp, su, sd,
        normalized_step(feature_vectors, vector_grad),
        normalized_step(up_bias, bias_grad),
    )


def solution(mesh):
    rows, columns, whole = P("dp", None), P(None, "dp"), P()
    return jax.shard_map(
        body,
        mesh=mesh,
        in_specs=(rows, rows, P("dp")) + (columns,) * 4 + (whole,) * 2 + (columns,) * 4,
        out_specs=(rows, rows) + (columns,) * 4 + (whole,) * 2 + (columns,) * 8 + (whole,) * 2,
        check_vma=False,
    )
```

```python
import functools
import math

import jax
import jax.numpy as jnp
from jax import lax
from jax.experimental import pallas as pl
from jax.experimental.pallas import tpu as pltpu
from jax.sharding import PartitionSpec as P

HEAD_DIM = 64
SEQ = 256
GROUP = 2
LANES = 128

norm_eps = 1e-06
newton_a = 3.4445
newton_b = -4.775
newton_c = 2.0315
momentum_decay = 0.9
matrix_rate = 0.15
vector_rate = 0.2

f32 = jnp.float32
bf16 = jnp.bfloat16


def nn(a, b):
    return lax.dot_general(a, b, (((1,), (0,)), ((), ())), preferred_element_type=f32)


def nt(a, b):
    return lax.dot_general(a, b, (((1,), (1,)), ((), ())), preferred_element_type=f32)


def tn(a, b):
    return lax.dot_general(a, b, (((0,), (0,)), ((), ())), preferred_element_type=f32)


def cols(index):
    return slice(index * LANES, (index + 1) * LANES)


def norm_parts(chunk):
    width = chunk.shape[0]
    center = chunk - jnp.sum(chunk, axis=0, keepdims=True) * (1.0 / width)
    scale = lax.rsqrt(jnp.sum(center * center, axis=0, keepdims=True) * (1.0 / width) + norm_eps)
    return center * scale, scale


def norm_back(inner, normed, scale):
    width = inner.shape[0]
    mean = jnp.sum(inner, axis=0, keepdims=True) * (1.0 / width)
    cross = jnp.sum(inner * normed, axis=0, keepdims=True) * (1.0 / width)
    return scale * (inner - mean - normed * cross)


def split_parts(x):
    high = x.astype(bf16)
    return high, (x - high.astype(f32)).astype(bf16)


def shard_rows(par, shard, own_ref, other_ref, first, count):
    span = slice(first, first + count)
    return jnp.where(par == shard % 2, own_ref[shard // 2, span, :], other_ref[shard // 2, span, :])


def lane_rows(acc):
    return [jnp.sum(acc[cols(c), :].T, axis=0, keepdims=True) for c in range(acc.shape[0] // LANES)]


def wide_rows(acc, width):
    rows = lane_rows(acc)
    per = width // LANES
    return [jnp.concatenate(rows[i : i + per], axis=1) for i in range(0, len(rows), per)]


def rounded(x):
    return x.astype(bf16).astype(f32)


def prep_kernel(wq_ref, wp_ref, wu_ref, wd_ref, first_ref, second_ref):
    first = wq_ref[...].astype(bf16)
    second = jnp.concatenate([wu_ref[...], wd_ref[...], wp_ref[...]], axis=0).astype(bf16)
    for index in range(first_ref.shape[0]):
        first_ref[index] = first
        second_ref[index, : second.shape[0], :] = second
        second_ref[index, second.shape[0] :, :] = jnp.zeros_like(second_ref[index, second.shape[0] :, :])


def attend_kernel(start, info, x_ref, vec_ref, *refs):
    if start == 0:
        own_ref, other_ref, qkv_ref, att_ref, out_ref, wq_ref, z_scr, qkv_scr, s_scr, p_scr, stage = refs
    else:
        wq_ref, _, _, _, qkv_ref, att_ref, out_ref, z_scr, qkv_scr, s_scr, p_scr = refs
    width, lanes = z_scr.shape
    heads = width // HEAD_DIM
    group = start + pl.program_id(0)

    if start == 0:

        @pl.when(pl.program_id(0) == 0)
        def _():
            count = own_ref.shape[1]
            for shard in range(2 * own_ref.shape[0]):
                rows = shard_rows(info[1], shard, own_ref, other_ref, 0, count)
                stage[shard * count : (shard + 1) * count, :] = rows.astype(f32)
            wq_ref[...] = stage[...].astype(bf16)

    @pl.when(group * GROUP < info[0])
    def _():
        for c in range(lanes // LANES):
            chunk = x_ref[cols(c), :].astype(f32).T
            normed, _ = norm_parts(chunk)
            z_scr[:, cols(c)] = (normed * vec_ref[0] + vec_ref[1]).astype(bf16)
        for part in range(3):
            rows = slice(part * width, (part + 1) * width)
            made = nn(wq_ref[rows, :], z_scr[...])
            for c in range(lanes // LANES):
                piece = made[:, cols(c)]
                if part == 0:
                    piece = (piece + vec_ref[2]) * (1.0 / math.sqrt(HEAD_DIM))
                elif part == 2:
                    piece = piece + vec_ref[3]
                piece = piece.astype(bf16)
                qkv_scr[rows, cols(c)] = piece
                qkv_ref[rows, cols(c)] = piece
        for image in range(lanes // SEQ):
            span = slice(image * SEQ, (image + 1) * SEQ)
            for head in range(heads):
                low = head * HEAD_DIM
                query = qkv_scr[low : low + HEAD_DIM, span]
                keys = qkv_scr[width + low : width + low + HEAD_DIM, span]
                s_scr[image * heads + head] = tn(keys, query)
        for image in range(lanes // SEQ):
            span = slice(image * SEQ, (image + 1) * SEQ)
            for head in range(heads):
                low = head * HEAD_DIM
                slot = image * heads + head
                for c in range(SEQ // LANES):
                    scores = s_scr[slot, :, cols(c)]
                    top = jnp.max(scores, axis=0, keepdims=True)
                    raised = jnp.exp(scores - top)
                    total = jnp.sum(raised, axis=0, keepdims=True)
                    attend = (raised * (1.0 / total)).astype(bf16)
                    p_scr[slot, :, cols(c)] = attend
                    att_ref[slot * SEQ : (slot + 1) * SEQ, cols(c)] = attend
                values = qkv_scr[2 * width + low : 2 * width + low + HEAD_DIM, span]
                out_ref[low : low + HEAD_DIM, span] = nn(values, p_scr[slot]).astype(bf16)


def mlp_kernel(
    info, x_ref, cot_ref, att_ref, own_ref, other_ref, vec_ref, ub_ref,
    out_ref, dh_ref, gp_ref, wpn_ref, keep_ref, send_ref,
    wun_scr, wdn_scr, wp_scr, wu_scr, wd_scr, gu_scr, gd_scr, rows_scr, bias_scr,
    h_scr, n_scr, z_scr, m_scr, act_scr, du_scr, dhb_scr, s_scr, stage, u_scr, d_scr,
):
    width, lanes = z_scr.shape
    ff = wu_scr.shape[0]
    half = own_ref.shape[0]
    part = ff // (2 * half)
    step = pl.program_id(0)
    block = u_scr.shape[1]

    @pl.when(step == 0)
    def _():
        gp_ref[...] = jnp.zeros_like(gp_ref)
        gu_scr[...] = jnp.zeros_like(gu_scr)
        gd_scr[...] = jnp.zeros_like(gd_scr)
        rows_scr[...] = jnp.zeros_like(rows_scr)
        bias_scr[...] = jnp.zeros_like(bias_scr)
        count = width // (2 * half)
        for shard in range(2 * half):
            rows = shard_rows(info[1], shard, own_ref, other_ref, 2 * part, count)
            stage[shard * count : (shard + 1) * count, :] = rows.astype(f32)
        wp_scr[...] = stage[:width, :].astype(bf16)
        wpn_ref[...] = stage[:width, :].T.astype(bf16)
        for low, wide_scr in ((0, wu_scr), (part, wd_scr)):
            if part % 16 == 0:
                for side, ref in enumerate((own_ref, other_ref)):
                    for index in range(half):
                        at = (side * half + index) * part
                        wide_scr[at : at + part, :] = ref[index, low : low + part, :]
            else:
                for side, ref in enumerate((own_ref, other_ref)):
                    for index in range(half):
                        at = (side * half + index) * part
                        stage[at : at + part, :] = ref[index, low : low + part, :].astype(f32)
                wide_scr[...] = stage[...].astype(bf16)
        for c in range(ff // block):
            rows = slice(c * block, (c + 1) * block)
            wun_scr[:, rows] = wu_scr[rows, :].T
            wdn_scr[:, rows] = wd_scr[rows, :].T

    @pl.when(step * GROUP >= info[0])
    def _():
        out_ref[...] = jnp.zeros_like(out_ref)

    @pl.when(step * GROUP < info[0])
    def _():
        made = nn(wp_scr[...], att_ref[...])
        total7 = jnp.zeros((width, LANES), f32)
        for c in range(lanes // LANES):
            chunk = x_ref[cols(c), :].astype(f32).T + made[:, cols(c)] + vec_ref[4]
            h_scr[:, cols(c)] = chunk
            normed, scale = norm_parts(chunk)
            n_scr[:, cols(c)] = normed
            s_scr[:, cols(c)] = scale
            z_scr[:, cols(c)] = (normed * vec_ref[5] + vec_ref[6]).astype(bf16)
            image = step * GROUP + c * LANES // SEQ
            cot = jnp.where(image < info[0], cot_ref[cols(c), :].astype(f32), 0.0).T
            m_scr[:, cols(c)] = cot.astype(bf16)
            total7 += cot
        rows_scr[3] += total7

        def first(c):
            rows = slice(c * block, (c + 1) * block)
            u_scr[c % 2] = nn(wu_scr[rows, :], z_scr[...])
            d_scr[c % 2] = nn(wd_scr[rows, :], m_scr[...])

        def second(c):
            for low in range(c * block, (c + 1) * block, 128):
                rows = slice(low, low + 128)
                here = slice(low - c * block, low - c * block + 128)
                bias = jnp.zeros((128, LANES), f32)
                for k in range(lanes // LANES):
                    u = u_scr[c % 2, here, cols(k)] + ub_ref[rows, :]
                    v = u * (1.0 / math.sqrt(2.0))
                    cdf = 0.5 + 0.5 * lax.erf(v)
                    act_scr[rows, cols(k)] = (u * cdf).astype(bf16)
                    slope = cdf + (v * (1.0 / math.sqrt(math.pi))) * jnp.exp(-(v * v))
                    du = d_scr[c % 2, here, cols(k)] * slope
                    du_scr[rows, cols(k)] = du.astype(bf16)
                    bias += du
                bias_scr[rows, :] += bias

        def third(c):
            rows = slice(c * block, (c + 1) * block)
            gu_scr[rows, :] += nt(du_scr[rows, :], z_scr[...])
            gd_scr[rows, :] += nt(act_scr[rows, :], m_scr[...])

        chunks = ff // block
        first(0)
        for c in range(chunks):
            if c + 1 < chunks:
                first(c + 1)
            second(c)
            third(c)
        down = nn(wdn_scr[...], act_scr[...])
        for c in range(lanes // LANES):
            image = step * GROUP + c * LANES // SEQ
            whole = down[:, cols(c)] + h_scr[:, cols(c)] + vec_ref[7]
            out_ref[cols(c), :] = jnp.where(image < info[0], whole, 0.0).T
        dz = nn(wun_scr[...], du_scr[...])
        total4 = jnp.zeros((width, LANES), f32)
        total5 = jnp.zeros((width, LANES), f32)
        total6 = jnp.zeros((width, LANES), f32)
        for c in range(lanes // LANES):
            piece = dz[:, cols(c)]
            normed = n_scr[:, cols(c)]
            dh = norm_back(piece * vec_ref[5], normed, s_scr[:, cols(c)]) + m_scr[:, cols(c)].astype(f32)
            dh_ref[:, cols(c)] = dh
            dhb_scr[:, cols(c)] = dh.astype(bf16)
            total4 += dh
            total5 += piece * normed
            total6 += piece
        rows_scr[0] += total4
        rows_scr[1] += total5
        rows_scr[2] += total6
        gp_ref[...] += nt(dhb_scr[...], att_ref[...])

    @pl.when(step == pl.num_programs(0) - 1)
    def _():
        vector = []
        for index in range(4):
            vector += wide_rows(rows_scr[index], width)
        hidden = wide_rows(bias_scr, width)
        side = len(hidden) // 2
        for index in range(len(hidden)):
            swapped = hidden[(index + side) % len(hidden)]
            vector.append(jnp.where(info[1] == 0, hidden[index], swapped))
        vector = jnp.concatenate(vector, axis=0)
        total = 2 * part + vector.shape[0]
        for index in range(half):
            keep_ref[index, :part, :] = gu_scr[index * part : (index + 1) * part, :]
            keep_ref[index, part : 2 * part, :] = gd_scr[index * part : (index + 1) * part, :]
            keep_ref[index, 2 * part : total, :] = rounded(vector)
            at = half * part + index * part
            if part % 16 == 0:
                send_ref[index, :part, :] = gu_scr[at : at + part, :].astype(bf16)
                send_ref[index, part : 2 * part, :] = gd_scr[at : at + part, :].astype(bf16)
                send_ref[index, 2 * part : total, :] = vector.astype(bf16)
            else:
                stage[:part, :] = gu_scr[at : at + part, :]
                stage[part : 2 * part, :] = gd_scr[at : at + part, :]
                stage[2 * part : total, :] = vector
                send_ref[index] = stage[: send_ref.shape[1], :].astype(bf16)


def back_kernel(start, last, info, x_ref, qkv_ref, att_ref, dh_ref, wpn_ref, wq_ref, gp_ref, vec_ref, *refs):
    if start:
        _, gq_in, rows_in = refs[:3]
        refs = refs[3:]
    if last:
        out_ref, keep_ref, send_ref, gq_ref, rows_ref, stage = refs[:6]
        refs = refs[6:]
    else:
        out_ref, gq_ref, rows_ref = refs[:3]
        refs = refs[3:]
    wqn_scr, n_scr, z_scr, s_scr, da_scr, dqkv_scr, up_scr, ds_scr = refs
    width, lanes = z_scr.shape
    heads = width // HEAD_DIM
    step = pl.program_id(0)
    group = start + step

    @pl.when(step == 0)
    def _():
        if start == 0:
            gq_ref[...] = jnp.zeros_like(gq_ref)
            rows_ref[...] = jnp.zeros_like(rows_ref)
        else:
            gq_ref[...] = gq_in[...]
            rows_ref[...] = rows_in[...]
        for c in range(3):
            rows = slice(c * width, (c + 1) * width)
            wqn_scr[:, rows] = wq_ref[rows, :].T

    @pl.when(group * GROUP >= info[0])
    def _():
        out_ref[...] = jnp.zeros_like(out_ref)

    @pl.when(group * GROUP < info[0])
    def _():
        da_scr[...] = nn(wpn_ref[...], dh_ref[...].astype(bf16)).astype(bf16)
        for image in range(lanes // SEQ):
            span = slice(image * SEQ, (image + 1) * SEQ)
            for head in range(heads):
                low = head * HEAD_DIM
                values = qkv_ref[2 * width + low : 2 * width + low + HEAD_DIM, span]
                up_scr[image * heads + head] = tn(values, da_scr[low : low + HEAD_DIM, span])
        for c in range(lanes // LANES):
            chunk = x_ref[cols(c), :].astype(f32).T
            normed, scale = norm_parts(chunk)
            n_scr[:, cols(c)] = normed
            s_scr[:, cols(c)] = scale
            z_scr[:, cols(c)] = (normed * vec_ref[0] + vec_ref[1]).astype(bf16)
        for image in range(lanes // SEQ):
            span = slice(image * SEQ, (image + 1) * SEQ)
            for head in range(heads):
                low = head * HEAD_DIM
                high = low + HEAD_DIM
                slot = image * heads + head
                base = slot * SEQ
                for c in range(SEQ // LANES):
                    attend = att_ref[base : base + SEQ, cols(c)].astype(f32)
                    upstream = up_scr[slot, :, cols(c)]
                    delta = jnp.sum(attend * upstream, axis=0, keepdims=True)
                    ds_scr[slot, :, cols(c)] = (attend * (upstream - delta)).astype(bf16)
                query = qkv_ref[low:high, span]
                keys = qkv_ref[width + low : width + high, span]
                dscore = ds_scr[slot]
                dquery = nn(keys, dscore) * (1.0 / math.sqrt(HEAD_DIM))
                dkey = nt(query, dscore)
                dvalue = nt(da_scr[low:high, span], att_ref[base : base + SEQ, :])
                dqkv_scr[low:high, span] = dquery.astype(bf16)
                dqkv_scr[width + low : width + high, span] = dkey.astype(bf16)
                dqkv_scr[2 * width + low : 2 * width + high, span] = dvalue.astype(bf16)
                rows_ref[2, low:high, :] += dquery[:, :LANES] + dquery[:, LANES:]
                rows_ref[3, low:high, :] += dvalue[:, :LANES] + dvalue[:, LANES:]
        for part in range(3):
            rows = slice(part * width, (part + 1) * width)
            gq_ref[rows, :] += nt(dqkv_scr[rows, :], z_scr[...])
        dz = nn(wqn_scr[...], dqkv_scr[...])
        total0 = jnp.zeros((width, LANES), f32)
        total1 = jnp.zeros((width, LANES), f32)
        for c in range(lanes // LANES):
            piece = dz[:, cols(c)]
            normed = n_scr[:, cols(c)]
            dx = norm_back(piece * vec_ref[0], normed, s_scr[:, cols(c)]) + dh_ref[:, cols(c)]
            out_ref[cols(c), :] = dx.T
            total0 += piece * normed
            total1 += piece
        rows_ref[0] += total0
        rows_ref[1] += total1

    if not last:
        return

    @pl.when(step == pl.num_programs(0) - 1)
    def _():
        count = 2 * keep_ref.shape[0]
        blocks = width // LANES
        sizes = (3 * width // count, width // count)
        rows = sum(sizes)
        stage[...] = jnp.zeros_like(stage)
        vector = []
        for index in range(4):
            vector += lane_rows(rows_ref[index])
        for index, row in enumerate(vector):
            stage[blocks * rows + index : blocks * rows + index + 1, :] = rounded(row)
        for shard in range(count):
            for c in range(blocks):
                low = c * rows
                for piece, size in zip((gq_ref, gp_ref), sizes):
                    stage[low : low + size, :] = piece[shard * size : (shard + 1) * size, cols(c)]
                    low += size

            @pl.when(info[1] == shard % 2)
            def _():
                keep_ref[shard // 2] = stage[...]

            @pl.when(info[1] != shard % 2)
            def _():
                send_ref[shard // 2] = stage[...].astype(bf16)


def unpack_att(total, rows, width, vectors):
    blocks = width // LANES
    grad = jnp.concatenate([total[c * rows : (c + 1) * rows] for c in range(blocks)], axis=1)
    return grad, total[blocks * rows : blocks * rows + vectors]


def state_kernel(got_ref, ma_ref, mb_ref, ga_ref, gb_ref, sa_ref, sb_ref, spread_ref, state_ref, vec_ref):
    first, width = ma_ref.shape
    rows = first + mb_ref.shape[0]
    total = got_ref[0].astype(f32)
    for index in range(1, got_ref.shape[0]):
        total += got_ref[index].astype(f32)
    if got_ref.shape[2] == width:
        grad, vec_ref[...] = total[:rows], total[rows : rows + vec_ref.shape[0]]
    else:
        grad, vec_ref[...] = unpack_att(total, rows, width, vec_ref.shape[0])
    ga_ref[...] = grad[:first]
    gb_ref[...] = grad[first:]
    state = grad + momentum_decay * jnp.concatenate([ma_ref[...], mb_ref[...]], axis=0)
    sa_ref[...] = state[:first]
    sb_ref[...] = state[first:]
    state_ref[...] = state
    for index in range(spread_ref.shape[0]):
        spread_ref[index] = state.astype(bf16)


def store_parts(x, left_ref, right_ref):
    width = x.shape[0]
    high, low = split_parts(x)
    left_ref[:, :width] = high
    left_ref[:, width : 2 * width] = high
    left_ref[:, 2 * width :] = low
    right_ref[:, :width] = high
    right_ref[:, width : 2 * width] = low
    right_ref[:, 2 * width :] = high


def newton_kernel(info, own_ref, other_ref, out_ref, whole_ref, gram_scr, poly_scr, pa, pb, sa, sb):
    count, rows, width = own_ref.shape
    first = info[1]
    eye = (
        lax.broadcasted_iota(jnp.int32, (width, width), 0)
        == lax.broadcasted_iota(jnp.int32, (width, width), 1)
    ).astype(f32)
    gram = jnp.zeros((width, width), f32)
    place = lax.broadcasted_iota(jnp.int32, (rows, width), 0)
    mine = (place < first) == (info[0] == 0)
    for ref in (own_ref, other_ref):
        part = jnp.concatenate(
            [jnp.where(mine, ref[index].astype(f32), 0.0) for index in range(count)], axis=0
        ).astype(bf16)
        gram += tn(part, part)
    norm = lax.rsqrt(jnp.sum(gram * eye) + norm_eps)
    out_ref[width:, :] = jnp.full((8, width), norm, f32)
    gram_scr[...] = gram * (norm * norm)
    whole_ref[...] = eye

    def turn(index, carry):
        store_parts(gram_scr[...], sa, sb)
        gram = gram_scr[...]
        poly = newton_a * eye + newton_b * gram + newton_c * nt(sa[...], sb[...])
        store_parts(poly, pa, pb)
        poly_scr[...] = nt(pa[...], sb[...])
        store_parts(whole_ref[...], sa, sb)
        whole_ref[...] = nt(pa[...], sb[...])

        @pl.when(index < 4)
        def _():
            store_parts(poly_scr[...], sa, sb)
            gram_scr[...] = nt(sa[...], pb[...])

        return carry

    lax.fori_loop(0, 5, turn, 0)
    out_ref[:width, :] = whole_ref[...]


def update_kernel(
    wide, info, mine_ref, theirs_ref, state_ref, wa_ref, wb_ref, ua_ref, ub_ref
):
    first = wa_ref.shape[0]
    rows = state_ref.shape[0]
    ours = info[0] == 0
    for low, high, w_ref, u_ref, columns, is_first in (
        (0, first, wa_ref, ua_ref, wide[0], True),
        (first, rows, wb_ref, ub_ref, wide[1], False),
    ):
        pick = ours if is_first else jnp.logical_not(ours)
        width = mine_ref.shape[1]
        whole = jnp.where(pick, mine_ref[:width, :], theirs_ref[:width, :])
        norm = jnp.where(pick, mine_ref[width : width + 1, :], theirs_ref[width : width + 1, :])
        state = state_ref[low:high, :] * norm
        sh, sl = split_parts(state)
        ph, pl_ = split_parts(whole)
        ortho = nt(sh, ph) + (nt(sl, ph) + nt(sh, pl_))
        u_ref[...] = w_ref[...] - (matrix_rate * 0.2 * math.sqrt(columns)) * ortho


def fixed(shape):
    return pl.BlockSpec(shape, lambda i, info: (0,) * len(shape))


ANY = pl.BlockSpec(memory_space=pl.ANY)


def params(grid=True):
    return pltpu.CompilerParams(
        dimension_semantics=("arbitrary",) if grid else None, vmem_limit_bytes=60 * 1024 * 1024
    )


def shape_of(shape, dtype):
    return jax.ShapeDtypeStruct(shape, dtype)


def cost(flops, read):
    return pl.CostEstimate(flops=int(flops), bytes_accessed=int(read), transcendentals=0)


def small_call(kernel, outs, name, scalars=0, scratch=()):
    vmem = pl.BlockSpec(memory_space=pltpu.VMEM)
    smem = pl.BlockSpec(memory_space=pltpu.SMEM)

    def call(*args):
        return pl.pallas_call(
            kernel,
            in_specs=[smem] * scalars + [vmem] * (len(args) - scalars),
            out_specs=[vmem] * len(outs),
            out_shape=[shape_of(*out) for out in outs],
            scratch_shapes=scratch,
            compiler_params=params(False),
            name=name,
        )(*args)

    return call


def group_specs(width, start):
    heads = width // HEAD_DIM
    lanes = GROUP * SEQ
    deep = lambda i, info: (start + i, 0, 0)
    return (
        pl.BlockSpec((lanes, width), lambda i, info: (start + i, 0)),
        pl.BlockSpec((None, 3 * width, lanes), deep),
        pl.BlockSpec((None, GROUP * heads * SEQ, SEQ), deep),
        pl.BlockSpec((None, width, lanes), deep),
    )


def attend_call(info, x, vec, start, stop, weights, before=()):
    width = x.shape[1]
    heads = width // HEAD_DIM
    lanes = GROUP * SEQ
    groups = x.shape[0] // lanes
    tokens, qkv_spec, att_spec, deep_spec = group_specs(width, start)
    fresh = start == 0
    return pl.pallas_call(
        functools.partial(attend_kernel, start),
        grid_spec=pltpu.PrefetchScalarGridSpec(
            num_scalar_prefetch=1,
            grid=(stop - start,),
            in_specs=[tokens, fixed(vec.shape)] + [fixed(w.shape) for w in weights] + [ANY] * len(before),
            out_specs=[qkv_spec, att_spec, deep_spec] + [fixed((3 * width, width))] * fresh,
            scratch_shapes=[
                pltpu.VMEM((width, lanes), bf16),
                pltpu.VMEM((3 * width, lanes), bf16),
                pltpu.VMEM((GROUP * heads, SEQ, SEQ), f32),
                pltpu.VMEM((GROUP * heads, SEQ, SEQ), bf16),
            ] + [pltpu.VMEM((3 * width, width), f32)] * fresh,
        ),
        out_shape=[
            shape_of((groups, 3 * width, lanes), bf16),
            shape_of((groups, GROUP * heads * SEQ, SEQ), bf16),
            shape_of((groups, width, lanes), bf16),
        ] + [shape_of((3 * width, width), bf16)] * fresh,
        input_output_aliases={3 + len(weights) + i: i for i in range(len(before))},
        compiler_params=params(),
        cost_estimate=cost(4e9 * (stop - start), 3e6 * (stop - start)),
        name="attend",
    )(info, x, vec, *weights, *before)


def mlp_call(info, x, cot, attn, own, other, vec, ub):
    width = x.shape[1]
    ff = ub.shape[0]
    half = own.shape[0]
    lanes = GROUP * SEQ
    groups = x.shape[0] // lanes
    block = 256
    tokens, _, _, deep_spec = group_specs(width, 0)
    rows = 2 * (ff // (2 * half)) + 4 + ff // width
    return pl.pallas_call(
        mlp_kernel,
        grid_spec=pltpu.PrefetchScalarGridSpec(
            num_scalar_prefetch=1,
            grid=(groups,),
            in_specs=[
                tokens, tokens, deep_spec,
                fixed(own.shape), fixed(own.shape), fixed(vec.shape), fixed(ub.shape),
            ],
            out_specs=[
                tokens, deep_spec, fixed((width, width)), fixed((width, width)),
                fixed((half, rows, width)), fixed((half, rows, width)),
            ],
            scratch_shapes=[
                pltpu.VMEM((width, ff), bf16),
                pltpu.VMEM((width, ff), bf16),
                pltpu.VMEM((width, width), bf16),
                pltpu.VMEM((ff, width), bf16),
                pltpu.VMEM((ff, width), bf16),
                pltpu.VMEM((ff, width), f32),
                pltpu.VMEM((ff, width), f32),
                pltpu.VMEM((4, width, LANES), f32),
                pltpu.VMEM((ff, LANES), f32),
                pltpu.VMEM((width, lanes), f32),
                pltpu.VMEM((width, lanes), f32),
                pltpu.VMEM((width, lanes), bf16),
                pltpu.VMEM((width, lanes), bf16),
                pltpu.VMEM((ff, lanes), bf16),
                pltpu.VMEM((ff, lanes), bf16),
                pltpu.VMEM((width, lanes), bf16),
                pltpu.VMEM((1, lanes), f32),
                pltpu.VMEM((ff, width), f32),
                pltpu.VMEM((2, block, lanes), f32),
                pltpu.VMEM((2, block, lanes), f32),
            ],
        ),
        out_shape=[
            shape_of(x.shape, f32),
            shape_of((groups, width, lanes), f32),
            shape_of((width, width), f32),
            shape_of((width, width), bf16),
            shape_of((half, rows, width), f32),
            shape_of((half, rows, width), bf16),
        ],
        compiler_params=params(),
        cost_estimate=cost(10e9 * groups, 4e6 * groups),
        name="mlp",
    )(info, x, cot, attn, own, other, vec, ub)


def back_call(info, x, qkv, att, dh, wpn, wq, gp, vec, half, start, stop, before=()):
    width = x.shape[1]
    heads = width // HEAD_DIM
    lanes = GROUP * SEQ
    groups = x.shape[0] // lanes
    tokens, qkv_spec, att_spec, deep_spec = group_specs(width, start)
    blocks = width // LANES
    rows = -(-(blocks * (4 * width // (2 * half)) + 4 * blocks) // 16) * 16
    last = stop == groups
    sums = [(3 * width, width), (4, width, LANES)]
    shards = (half, rows, LANES)
    scratch = [
        pltpu.VMEM((width, 3 * width), bf16),
        pltpu.VMEM((width, lanes), f32),
        pltpu.VMEM((width, lanes), bf16),
        pltpu.VMEM((1, lanes), f32),
        pltpu.VMEM((width, lanes), bf16),
        pltpu.VMEM((3 * width, lanes), bf16),
        pltpu.VMEM((GROUP * heads, SEQ, SEQ), f32),
        pltpu.VMEM((GROUP * heads, SEQ, SEQ), bf16),
    ]
    if last:
        outs = [(shards, f32), (shards, bf16)]
        scratch = [pltpu.VMEM(shape, f32) for shape in sums + [(rows, LANES)]] + scratch
    else:
        outs = [(shape, f32) for shape in sums]
    return pl.pallas_call(
        functools.partial(back_kernel, start, last),
        grid_spec=pltpu.PrefetchScalarGridSpec(
            num_scalar_prefetch=1,
            grid=(stop - start,),
            in_specs=[
                tokens, qkv_spec, att_spec, deep_spec,
                fixed(wpn.shape), fixed(wq.shape), fixed(gp.shape), fixed(vec.shape),
            ] + ([ANY] + [fixed(shape) for shape in sums] if before else []),
            out_specs=[tokens] + [fixed(shape) for shape, _ in outs],
            scratch_shapes=scratch,
        ),
        out_shape=[shape_of(x.shape, f32)] + [shape_of(*out) for out in outs],
        input_output_aliases={9: 0} if before else {},
        compiler_params=params(),
        cost_estimate=cost(7e9 * (stop - start), 5e6 * (stop - start)),
        name="back",
    )(info, x, qkv, att, dh, wpn, wq, gp, vec, *before)


def order_ff(up_bias, par, half):
    parts = up_bias.reshape(half, 2, -1)
    return jnp.where(
        par == 0,
        jnp.concatenate([parts[:, 0], parts[:, 1]]),
        jnp.concatenate([parts[:, 1], parts[:, 0]]),
    ).reshape(-1)


def natural_ff(bias, half):
    return jnp.swapaxes(bias.reshape(2, half, -1), 0, 1).reshape(-1)


def spread_lanes(array):
    return jnp.broadcast_to(array[..., None], array.shape + (LANES,))


def body(
    block_in,
    out_grad,
    live_counts,
    qkv_weight,
    proj_weight,
    up_weight,
    down_weight,
    feature_vectors,
    up_bias,
    qkv_moment,
    proj_moment,
    up_moment,
    down_moment,
):
    devices = lax.axis_size("dp")
    half = devices // 2
    par = (lax.axis_index("dp") % 2).astype(jnp.int32)
    width = block_in.shape[1]
    groups = block_in.shape[0] // (GROUP * SEQ)
    ff = up_bias.shape[0]
    blocks = width // LANES
    turned = [w.T for w in (qkv_weight, proj_weight, up_weight, down_weight)]
    wq_s, wp_s, wu_s, wd_s = turned
    mq_s, mp_s, mu_s, md_s = [m.T for m in (qkv_moment, proj_moment, up_moment, down_moment)]
    cq, cp, cu, cd = (w.shape[0] for w in turned)
    pairs = [(i, i ^ 1) for i in range(devices)]
    planes = [[2 * i + c for i in range(half)] for c in range(2)]
    info = jnp.stack([live_counts[0], par])
    vec = spread_lanes(feature_vectors)
    ub = spread_lanes(order_ff(up_bias, par, half))

    def exchange(x):
        return lax.all_to_all(x, "dp", 0, 0, axis_index_groups=planes, tiled=True)

    def swap(x):
        return lax.ppermute(x, "dp", pairs)

    def after(x, *others):
        return lax.optimization_barrier((x,) + others)[0]

    first, second = small_call(
        prep_kernel,
        [((half, cq, width), bf16), ((half, -(-(cu + cd + cp) // 16) * 16, width), bf16)],
        "prep",
    )(wq_s, wp_s, wu_s, wd_s)
    wq_own = exchange(first)
    wq_other = swap(wq_own)
    rest_own = exchange(after(second, wq_own))

    early = groups - 2 if groups > 2 else groups
    qkv, att, attn, wq = attend_call(info, block_in, vec, 0, early, (wq_own, wq_other))
    rest_own = after(rest_own, attn)
    rest_other = swap(rest_own)
    if early < groups:
        qkv, att, attn = attend_call(info, block_in, vec, early, groups, (wq,), (qkv, att, attn))
    out, dh, gp, wpn, keep_b, send_b = mlp_call(
        info, block_in, out_grad, attn, rest_own, rest_other, vec, ub
    )

    def fold(keep, received):
        return exchange((keep + received.astype(f32)).astype(bf16))

    swapped = swap(send_b)
    one = 1 if groups > 2 else groups
    most = groups - 1 if groups > 2 else groups
    done = back_call(info, block_in, qkv, att, dh, wpn, wq, gp, vec, half, 0, one)
    got_b = fold(keep_b, after(swapped, done[1]))
    if one < groups:
        done = back_call(info, block_in, qkv, att, dh, wpn, wq, gp, vec, half, one, most, done)
    got_b = after(got_b, done[1])

    def sums(got, moment_a, moment_b, vectors, lanes, name):
        rows = moment_a.shape[0] + moment_b.shape[0]
        return small_call(
            state_kernel,
            [
                (moment_a.shape, f32), (moment_b.shape, f32), (moment_a.shape, f32), (moment_b.shape, f32),
                ((half, rows, width), bf16), ((rows, width), f32), ((vectors, lanes), f32),
            ],
            name + "_state",
        )(got, moment_a, moment_b)

    def polynomials(own, other, first, name):
        square = pltpu.VMEM((width, width), f32)
        parts = pltpu.VMEM((width, 3 * width), bf16)
        return small_call(
            newton_kernel,
            [((width + 8, width), f32)],
            name + "_newton",
            scalars=1,
            scratch=[square, square, square, parts, parts, parts, parts],
        )(jnp.stack([par, jnp.full((), first, jnp.int32)]), own, other)[0]

    def updates(mine, theirs, state, weight_a, weight_b, name):
        wide = (weight_a.shape[0] * devices, weight_b.shape[0] * devices)
        return small_call(
            functools.partial(update_kernel, wide),
            [(weight_a.shape, f32), (weight_b.shape, f32)],
            name + "_update",
            scalars=1,
        )(par.reshape(1), mine, theirs, state, weight_a, weight_b)

    gu, gd, su, sd, spread_b, state_b, vector_b = sums(
        got_b, mu_s, md_s, 4 + ff // width, width, "mlp"
    )
    own_b = exchange(spread_b)
    if most < groups:
        done = back_call(info, block_in, qkv, att, dh, wpn, wq, gp, vec, half, most, groups, done)
    dx, keep_a, send_a = done
    got_a = fold(keep_a, swap(send_a))
    other_b = swap(own_b)
    gq, gpr, sq, sp, spread_a, state_a, vector_a = sums(got_a, mq_s, mp_s, 4 * blocks, LANES, "att")
    own_a = exchange(spread_a)
    other_a = swap(own_a)
    mine_b = polynomials(own_b, other_b, cu, "mlp")
    uu, ud = updates(mine_b, swap(mine_b), state_b, wu_s, wd_s, "mlp")
    mine_a = polynomials(own_a, other_a, cq, "att")
    uq, up = updates(mine_a, swap(mine_a), state_a, wq_s, wp_s, "att")

    vector_grad = jnp.concatenate([vector_a.reshape(4, width), vector_b[:4]], axis=0)
    bias_grad = natural_ff(vector_b[4:].reshape(ff), half)

    def normalized_step(param, gradient):
        return param - vector_rate * gradient * lax.rsqrt(
            jnp.mean(gradient * gradient, axis=-1, keepdims=True) + norm_eps
        )

    return (
        out, dx, gq.T, gpr.T, gu.T, gd.T, vector_grad, bias_grad, uq.T, up.T, uu.T, ud.T,
        sq.T, sp.T, su.T, sd.T,
        normalized_step(feature_vectors, vector_grad),
        normalized_step(up_bias, bias_grad),
    )


def solution(mesh):
    rows, columns, whole = P("dp", None), P(None, "dp"), P()
    return jax.shard_map(
        body,
        mesh=mesh,
        in_specs=(rows, rows, P("dp")) + (columns,) * 4 + (whole,) * 2 + (columns,) * 4,
        out_specs=(rows, rows) + (columns,) * 4 + (whole,) * 2 + (columns,) * 8 + (whole,) * 2,
        check_vma=False,
    )
```

```python
import functools
import math

import jax
import jax.numpy as jnp
from jax import lax
from jax.experimental import pallas as pl
from jax.experimental.pallas import tpu as pltpu
from jax.sharding import PartitionSpec as P

HEAD_DIM = 64
SEQ = 256
GROUP = 2
LANES = 128

norm_eps = 1e-06
newton_a = 3.4445
newton_b = -4.775
newton_c = 2.0315
momentum_decay = 0.9
matrix_rate = 0.15
vector_rate = 0.2

f32 = jnp.float32
bf16 = jnp.bfloat16


def nn(a, b):
    return lax.dot_general(a, b, (((1,), (0,)), ((), ())), preferred_element_type=f32)


def nt(a, b):
    return lax.dot_general(a, b, (((1,), (1,)), ((), ())), preferred_element_type=f32)


def tn(a, b):
    return lax.dot_general(a, b, (((0,), (0,)), ((), ())), preferred_element_type=f32)


def cols(index):
    return slice(index * LANES, (index + 1) * LANES)


def norm_parts(chunk):
    width = chunk.shape[0]
    center = chunk - jnp.sum(chunk, axis=0, keepdims=True) * (1.0 / width)
    scale = lax.rsqrt(jnp.sum(center * center, axis=0, keepdims=True) * (1.0 / width) + norm_eps)
    return center * scale, scale


def norm_back(inner, normed, scale):
    width = inner.shape[0]
    mean = jnp.sum(inner, axis=0, keepdims=True) * (1.0 / width)
    cross = jnp.sum(inner * normed, axis=0, keepdims=True) * (1.0 / width)
    return scale * (inner - mean - normed * cross)


def split_parts(x):
    high = x.astype(bf16)
    return high, (x - high.astype(f32)).astype(bf16)


def shard_rows(par, shard, own_ref, other_ref, first, count):
    span = slice(first, first + count)
    return jnp.where(par == shard % 2, own_ref[shard // 2, span, :], other_ref[shard // 2, span, :])


def lane_rows(acc):
    return [jnp.sum(acc[cols(c), :].T, axis=0, keepdims=True) for c in range(acc.shape[0] // LANES)]


def wide_rows(acc, width):
    rows = lane_rows(acc)
    per = width // LANES
    return [jnp.concatenate(rows[i : i + per], axis=1) for i in range(0, len(rows), per)]


def rounded(x):
    return x.astype(bf16).astype(f32)


def prep_kernel(wq_ref, wp_ref, wu_ref, wd_ref, first_ref, second_ref):
    first = wq_ref[...].astype(bf16)
    second = jnp.concatenate([wu_ref[...], wd_ref[...], wp_ref[...]], axis=0).astype(bf16)
    for index in range(first_ref.shape[0]):
        first_ref[index] = first
        second_ref[index, : second.shape[0], :] = second
        second_ref[index, second.shape[0] :, :] = jnp.zeros_like(second_ref[index, second.shape[0] :, :])


def normal_kernel(info, x_ref, vec_ref, z_ref):
    @pl.when(pl.program_id(0) * GROUP < info[0])
    def _():
        for c in range(z_ref.shape[1] // LANES):
            normed, _ = norm_parts(x_ref[cols(c), :].astype(f32).T)
            z_ref[:, cols(c)] = (normed * vec_ref[0] + vec_ref[1]).astype(bf16)


def attend_kernel(start, info, z_ref, vec_ref, *refs):
    if start == 0:
        own_ref, other_ref, qkv_ref, att_ref, out_ref, wq_ref, qkv_scr, s_scr, p_scr, stage = refs
    else:
        wq_ref, _, _, _, qkv_ref, att_ref, out_ref, qkv_scr, s_scr, p_scr = refs
    width, lanes = z_ref.shape
    heads = width // HEAD_DIM
    group = start + pl.program_id(0)

    if start == 0:

        @pl.when(pl.program_id(0) == 0)
        def _():
            count = own_ref.shape[1]
            for shard in range(2 * own_ref.shape[0]):
                rows = shard_rows(info[1], shard, own_ref, other_ref, 0, count)
                stage[shard * count : (shard + 1) * count, :] = rows.astype(f32)
            wq_ref[...] = stage[...].astype(bf16)

    @pl.when(group * GROUP < info[0])
    def _():
        for part in range(3):
            rows = slice(part * width, (part + 1) * width)
            made = nn(wq_ref[rows, :], z_ref[...])
            for c in range(lanes // LANES):
                piece = made[:, cols(c)]
                if part == 0:
                    piece = (piece + vec_ref[2]) * (1.0 / math.sqrt(HEAD_DIM))
                elif part == 2:
                    piece = piece + vec_ref[3]
                piece = piece.astype(bf16)
                qkv_scr[rows, cols(c)] = piece
                qkv_ref[rows, cols(c)] = piece
        for image in range(lanes // SEQ):
            span = slice(image * SEQ, (image + 1) * SEQ)
            for head in range(heads):
                low = head * HEAD_DIM
                query = qkv_scr[low : low + HEAD_DIM, span]
                keys = qkv_scr[width + low : width + low + HEAD_DIM, span]
                s_scr[image * heads + head] = tn(keys, query)
        for image in range(lanes // SEQ):
            span = slice(image * SEQ, (image + 1) * SEQ)
            for head in range(heads):
                low = head * HEAD_DIM
                slot = image * heads + head
                for c in range(SEQ // LANES):
                    scores = s_scr[slot, :, cols(c)]
                    top = jnp.max(scores, axis=0, keepdims=True)
                    raised = jnp.exp(scores - top)
                    total = jnp.sum(raised, axis=0, keepdims=True)
                    attend = (raised * (1.0 / total)).astype(bf16)
                    p_scr[slot, :, cols(c)] = attend
                    att_ref[slot * SEQ : (slot + 1) * SEQ, cols(c)] = attend
                values = qkv_scr[2 * width + low : 2 * width + low + HEAD_DIM, span]
                out_ref[low : low + HEAD_DIM, span] = nn(values, p_scr[slot]).astype(bf16)


def mlp_kernel(
    info, x_ref, cot_ref, att_ref, own_ref, other_ref, vec_ref, ub_ref,
    h_ref, act_ref, dh_ref, gp_ref, wpn_ref, wdn_ref, keep_ref, send_ref,
    wun_scr, wp_scr, wu_scr, wd_scr, gu_scr, gd_scr, rows_scr, bias_scr,
    n_scr, z_scr, m_scr, act_scr, du_scr, dhb_scr, s_scr, stage, u_scr, d_scr,
):
    width, lanes = z_scr.shape
    ff = wu_scr.shape[0]
    half = own_ref.shape[0]
    part = ff // (2 * half)
    step = pl.program_id(0)
    block = u_scr.shape[1]

    @pl.when(step == 0)
    def _():
        gp_ref[...] = jnp.zeros_like(gp_ref)
        rows_scr[...] = jnp.zeros_like(rows_scr)

        def clear(index, carry):
            rows = pl.ds(pl.multiple_of(index * LANES, LANES), LANES)
            gu_scr[rows, :] = jnp.zeros((LANES, width), f32)
            gd_scr[rows, :] = jnp.zeros((LANES, width), f32)
            bias_scr[rows, :] = jnp.zeros((LANES, LANES), f32)
            return carry

        lax.fori_loop(0, ff // LANES, clear, 0)
        count = width // (2 * half)
        for shard in range(2 * half):
            rows = shard_rows(info[1], shard, own_ref, other_ref, 2 * part, count)
            stage[shard * count : (shard + 1) * count, :] = rows.astype(f32)
        wp_scr[...] = stage[:width, :].astype(bf16)
        wpn_ref[...] = stage[:width, :].T.astype(bf16)
        for low, wide_scr in ((0, wu_scr), (part, wd_scr)):
            if part % 16 == 0:
                for side, ref in enumerate((own_ref, other_ref)):
                    for index in range(half):
                        at = (side * half + index) * part
                        wide_scr[at : at + part, :] = ref[index, low : low + part, :]
            else:
                for side, ref in enumerate((own_ref, other_ref)):
                    for index in range(half):
                        at = (side * half + index) * part
                        stage[at : at + part, :] = ref[index, low : low + part, :].astype(f32)
                wide_scr[...] = stage[...].astype(bf16)

        def turn(index, carry):
            rows = pl.ds(pl.multiple_of(index * block, block), block)
            wun_scr[:, rows] = wu_scr[rows, :].T
            wdn_ref[:, rows] = wd_scr[rows, :].T
            return carry

        lax.fori_loop(0, ff // block, turn, 0)

    @pl.when(step * GROUP < info[0])
    def _():
        made = nn(wp_scr[...], att_ref[...])
        total7 = jnp.zeros((width, LANES), f32)
        for c in range(lanes // LANES):
            chunk = x_ref[cols(c), :].astype(f32).T + made[:, cols(c)] + vec_ref[4]
            h_ref[:, cols(c)] = chunk
            normed, scale = norm_parts(chunk)
            n_scr[:, cols(c)] = normed
            s_scr[:, cols(c)] = scale
            z_scr[:, cols(c)] = (normed * vec_ref[5] + vec_ref[6]).astype(bf16)
            image = step * GROUP + c * LANES // SEQ
            cot = jnp.where(image < info[0], cot_ref[cols(c), :].astype(f32), 0.0).T
            m_scr[:, cols(c)] = cot.astype(bf16)
            total7 += cot
        rows_scr[3] += total7

        def first(c):
            rows = slice(c * block, (c + 1) * block)
            u_scr[c % 2] = nn(wu_scr[rows, :], z_scr[...])
            d_scr[c % 2] = nn(wd_scr[rows, :], m_scr[...])

        def second(c):
            for low in range(c * block, (c + 1) * block, 128):
                rows = slice(low, low + 128)
                here = slice(low - c * block, low - c * block + 128)
                bias = jnp.zeros((128, LANES), f32)
                for k in range(lanes // LANES):
                    u = u_scr[c % 2, here, cols(k)] + ub_ref[rows, :]
                    v = u * (1.0 / math.sqrt(2.0))
                    cdf = 0.5 + 0.5 * lax.erf(v)
                    act = (u * cdf).astype(bf16)
                    act_scr[rows, cols(k)] = act
                    act_ref[rows, cols(k)] = act
                    slope = cdf + (v * (1.0 / math.sqrt(math.pi))) * jnp.exp(-(v * v))
                    du = d_scr[c % 2, here, cols(k)] * slope
                    du_scr[rows, cols(k)] = du.astype(bf16)
                    bias += du
                bias_scr[rows, :] += bias

        def third(c):
            rows = slice(c * block, (c + 1) * block)
            gu_scr[rows, :] += nt(du_scr[rows, :], z_scr[...])
            gd_scr[rows, :] += nt(act_scr[rows, :], m_scr[...])

        chunks = ff // block
        first(0)
        for c in range(chunks):
            if c + 1 < chunks:
                first(c + 1)
            second(c)
            third(c)
        dz = nn(wun_scr[...], du_scr[...])
        total4 = jnp.zeros((width, LANES), f32)
        total5 = jnp.zeros((width, LANES), f32)
        total6 = jnp.zeros((width, LANES), f32)
        for c in range(lanes // LANES):
            piece = dz[:, cols(c)]
            normed = n_scr[:, cols(c)]
            dh = norm_back(piece * vec_ref[5], normed, s_scr[:, cols(c)]) + m_scr[:, cols(c)].astype(f32)
            dh_ref[:, cols(c)] = dh
            dhb_scr[:, cols(c)] = dh.astype(bf16)
            total4 += dh
            total5 += piece * normed
            total6 += piece
        rows_scr[0] += total4
        rows_scr[1] += total5
        rows_scr[2] += total6
        gp_ref[...] += nt(dhb_scr[...], att_ref[...])

    @pl.when(step == pl.num_programs(0) - 1)
    def _():
        vector = []
        for index in range(4):
            vector += wide_rows(rows_scr[index], width)
        hidden = wide_rows(bias_scr, width)
        side = len(hidden) // 2
        for index in range(len(hidden)):
            swapped = hidden[(index + side) % len(hidden)]
            vector.append(jnp.where(info[1] == 0, hidden[index], swapped))
        vector = jnp.concatenate(vector, axis=0)
        total = 2 * part + vector.shape[0]
        for index in range(half):
            keep_ref[index, :part, :] = gu_scr[index * part : (index + 1) * part, :]
            keep_ref[index, part : 2 * part, :] = gd_scr[index * part : (index + 1) * part, :]
            keep_ref[index, 2 * part : total, :] = rounded(vector)
            at = half * part + index * part
            if part % 16 == 0:
                send_ref[index, :part, :] = gu_scr[at : at + part, :].astype(bf16)
                send_ref[index, part : 2 * part, :] = gd_scr[at : at + part, :].astype(bf16)
                send_ref[index, 2 * part : total, :] = vector.astype(bf16)
            else:
                stage[:part, :] = gu_scr[at : at + part, :]
                stage[part : 2 * part, :] = gd_scr[at : at + part, :]
                stage[2 * part : total, :] = vector
                send_ref[index] = stage[: send_ref.shape[1], :].astype(bf16)


def out_kernel(start, info, h_ref, act_ref, wdn_ref, vec_ref, *refs):
    out_ref = refs[-1]
    group = start + pl.program_id(0)

    @pl.when(group * GROUP >= info[0])
    def _():
        out_ref[...] = jnp.zeros_like(out_ref)

    @pl.when(group * GROUP < info[0])
    def _():
        down = nn(wdn_ref[...], act_ref[...])
        for c in range(h_ref.shape[1] // LANES):
            image = group * GROUP + c * LANES // SEQ
            whole = down[:, cols(c)] + h_ref[:, cols(c)] + vec_ref[7]
            out_ref[cols(c), :] = jnp.where(image < info[0], whole, 0.0).T


def back_kernel(start, last, info, z_ref, qkv_ref, att_ref, dh_ref, wpn_ref, wq_ref, gp_ref, row_ref, *refs):
    if start:
        gq_in, rows_in, _ = refs[:3]
        refs = refs[3:]
    if last:
        dqkv_ref, keep_ref, send_ref, gq_ref, rows_ref, stage = refs[:6]
        refs = refs[6:]
    else:
        dqkv_ref, gq_ref, rows_ref = refs[:3]
        refs = refs[3:]
    da_scr, dqkv_scr, up_scr, ds_scr = refs
    width, lanes = z_ref.shape
    heads = width // HEAD_DIM
    step = pl.program_id(0)
    group = start + step

    @pl.when(step == 0)
    def _():
        if start == 0:
            gq_ref[...] = jnp.zeros_like(gq_ref)
            rows_ref[...] = jnp.zeros_like(rows_ref)
        else:
            gq_ref[...] = gq_in[...]
            rows_ref[...] = rows_in[...]

    @pl.when(group * GROUP < info[0])
    def _():
        da_scr[...] = nn(wpn_ref[...], dh_ref[...].astype(bf16)).astype(bf16)
        for image in range(lanes // SEQ):
            span = slice(image * SEQ, (image + 1) * SEQ)
            for head in range(heads):
                low = head * HEAD_DIM
                values = qkv_ref[2 * width + low : 2 * width + low + HEAD_DIM, span]
                up_scr[image * heads + head] = tn(values, da_scr[low : low + HEAD_DIM, span])
        for image in range(lanes // SEQ):
            span = slice(image * SEQ, (image + 1) * SEQ)
            for head in range(heads):
                low = head * HEAD_DIM
                high = low + HEAD_DIM
                slot = image * heads + head
                base = slot * SEQ
                for c in range(SEQ // LANES):
                    attend = att_ref[base : base + SEQ, cols(c)].astype(f32)
                    upstream = up_scr[slot, :, cols(c)]
                    delta = jnp.sum(attend * upstream, axis=0, keepdims=True)
                    ds_scr[slot, :, cols(c)] = (attend * (upstream - delta)).astype(bf16)
                query = qkv_ref[low:high, span]
                keys = qkv_ref[width + low : width + high, span]
                dscore = ds_scr[slot]
                dquery = nn(keys, dscore) * (1.0 / math.sqrt(HEAD_DIM))
                dkey = nt(query, dscore)
                dvalue = nt(da_scr[low:high, span], att_ref[base : base + SEQ, :])
                for part, value in enumerate((dquery, dkey, dvalue)):
                    rows = slice(part * width + low, part * width + high)
                    made = value.astype(bf16)
                    dqkv_scr[rows, span] = made
                    dqkv_ref[rows, span] = made
                    rows_ref[part, low:high, :] += value[:, :LANES] + value[:, LANES:]
        for part in range(3):
            rows = slice(part * width, (part + 1) * width)
            gq_ref[rows, :] += nt(dqkv_scr[rows, :], z_ref[...])

    if not last:
        return

    @pl.when(step == pl.num_programs(0) - 1)
    def _():
        count = 2 * keep_ref.shape[0]
        blocks = width // LANES
        sizes = (3 * width // count, width // count)
        rows = sum(sizes)
        stage[...] = jnp.zeros_like(stage)
        cross, plain = jnp.zeros((1, width), f32), jnp.zeros((1, width), f32)
        for part in range(3):
            rows_of = slice(part * width, (part + 1) * width)
            weight = wq_ref[rows_of, :].astype(f32)
            total = jnp.sum(rows_ref[part], axis=1, keepdims=True)
            cross += jnp.sum(weight * gq_ref[rows_of, :], axis=0, keepdims=True)
            plain += jnp.sum(weight * total, axis=0, keepdims=True)
        cross = (cross - row_ref[1:2, :] * plain) / row_ref[0:1, :]
        vector = [value[:, cols(c)] for value in (cross, plain) for c in range(blocks)]
        vector += lane_rows(rows_ref[0]) + lane_rows(rows_ref[2])
        for index, row in enumerate(vector):
            stage[blocks * rows + index : blocks * rows + index + 1, :] = rounded(row)
        for shard in range(count):
            for c in range(blocks):
                low = c * rows
                for piece, size in zip((gq_ref, gp_ref), sizes):
                    stage[low : low + size, :] = piece[shard * size : (shard + 1) * size, cols(c)]
                    low += size

            @pl.when(info[1] == shard % 2)
            def _():
                keep_ref[shard // 2] = stage[...]

            @pl.when(info[1] != shard % 2)
            def _():
                send_ref[shard // 2] = stage[...].astype(bf16)


def input_kernel(start, info, x_ref, dqkv_ref, dh_ref, wq_ref, vec_ref, *refs):
    out_ref, wqn_scr, s_scr, n_scr = refs[-4:]
    width, lanes = n_scr.shape
    step = pl.program_id(0)
    group = start + step

    @pl.when(step == 0)
    def _():
        for c in range(3):
            rows = slice(c * width, (c + 1) * width)
            wqn_scr[:, rows] = wq_ref[rows, :].T

    @pl.when(group * GROUP >= info[0])
    def _():
        out_ref[...] = jnp.zeros_like(out_ref)

    @pl.when(group * GROUP < info[0])
    def _():
        dz = nn(wqn_scr[...], dqkv_ref[...])
        for c in range(lanes // LANES):
            normed, scale = norm_parts(x_ref[cols(c), :].astype(f32).T)
            n_scr[:, cols(c)] = normed
            s_scr[:, cols(c)] = scale
        for c in range(lanes // LANES):
            inner = dz[:, cols(c)] * vec_ref[0]
            dx = norm_back(inner, n_scr[:, cols(c)], s_scr[:, cols(c)]) + dh_ref[:, cols(c)]
            out_ref[cols(c), :] = dx.T


def unpack_att(total, rows, width, vectors):
    blocks = width // LANES
    grad = jnp.concatenate([total[c * rows : (c + 1) * rows] for c in range(blocks)], axis=1)
    return grad, total[blocks * rows : blocks * rows + vectors]


def state_kernel(info, got_ref, ma_ref, mb_ref, ga_ref, gb_ref, sa_ref, sb_ref, spread_ref, state_ref, vec_ref):
    first, width = ma_ref.shape
    rows = first + mb_ref.shape[0]
    total = got_ref[0].astype(f32)
    for index in range(1, got_ref.shape[0]):
        total += got_ref[index].astype(f32)
    if got_ref.shape[2] == width:
        grad, vec_ref[...] = total[:rows], total[rows : rows + vec_ref.shape[0]]
    else:
        grad, vec_ref[...] = unpack_att(total, rows, width, vec_ref.shape[0])
    ga_ref[...] = grad[:first]
    gb_ref[...] = grad[first:]
    state = grad + momentum_decay * jnp.concatenate([ma_ref[...], mb_ref[...]], axis=0)
    sa_ref[...] = state[:first]
    sb_ref[...] = state[first:]
    state_ref[...] = state
    if got_ref.shape[2] == width:
        ours = info[0] == 0
        high, low = state[:first].astype(bf16), state[first:].astype(bf16)
        spread_ref[0] = jnp.where(ours, high, low)
        spread_ref[1] = jnp.where(ours, low, high)
    else:
        for index in range(spread_ref.shape[0]):
            spread_ref[index] = state.astype(bf16)


def store_parts(x, left_ref, right_ref):
    width = x.shape[0]
    high, low = split_parts(x)
    left_ref[:, :width] = high
    left_ref[:, width : 2 * width] = high
    left_ref[:, 2 * width :] = low
    right_ref[:, :width] = high
    right_ref[:, width : 2 * width] = low
    right_ref[:, 2 * width :] = high


def newton_kernel(info, own_ref, other_ref, out_ref, whole_ref, gram_scr, poly_scr, pa, pb, sa, sb):
    width = own_ref.shape[-1]
    eye = (
        lax.broadcasted_iota(jnp.int32, (width, width), 0)
        == lax.broadcasted_iota(jnp.int32, (width, width), 1)
    ).astype(f32)
    gram = jnp.zeros((width, width), f32)
    for ref in (own_ref, other_ref):
        if len(ref.shape) == 2:
            part = ref[...]
        else:
            place = lax.broadcasted_iota(jnp.int32, ref.shape[1:], 0)
            mine = (place < info[1]) == (info[0] == 0)
            part = jnp.concatenate(
                [jnp.where(mine, ref[index].astype(f32), 0.0) for index in range(ref.shape[0])], axis=0
            ).astype(bf16)
        gram += tn(part, part)
    norm = lax.rsqrt(jnp.sum(gram * eye) + norm_eps)
    out_ref[width:, :] = jnp.full((8, width), norm, f32)
    gram_scr[...] = gram * (norm * norm)
    whole_ref[...] = eye

    def turn(index, carry):
        store_parts(gram_scr[...], sa, sb)
        gram = gram_scr[...]
        poly = newton_a * eye + newton_b * gram + newton_c * nt(sa[...], sb[...])
        store_parts(poly, pa, pb)
        poly_scr[...] = nt(pa[...], sb[...])
        store_parts(whole_ref[...], sa, sb)
        whole_ref[...] = nt(pa[...], sb[...])

        @pl.when(index < 4)
        def _():
            store_parts(poly_scr[...], sa, sb)
            gram_scr[...] = nt(sa[...], pb[...])

        return carry

    lax.fori_loop(0, 5, turn, 0)
    out_ref[:width, :] = whole_ref[...]


def update_kernel(
    wide, info, mine_ref, theirs_ref, state_ref, wa_ref, wb_ref, ua_ref, ub_ref
):
    first = wa_ref.shape[0]
    rows = state_ref.shape[0]
    ours = info[0] == 0
    for low, high, w_ref, u_ref, columns, is_first in (
        (0, first, wa_ref, ua_ref, wide[0], True),
        (first, rows, wb_ref, ub_ref, wide[1], False),
    ):
        pick = ours if is_first else jnp.logical_not(ours)
        width = mine_ref.shape[1]
        whole = jnp.where(pick, mine_ref[:width, :], theirs_ref[:width, :])
        norm = jnp.where(pick, mine_ref[width : width + 1, :], theirs_ref[width : width + 1, :])
        state = state_ref[low:high, :] * norm
        sh, sl = split_parts(state)
        ph, pl_ = split_parts(whole)
        ortho = nt(sh, ph) + (nt(sl, ph) + nt(sh, pl_))
        u_ref[...] = w_ref[...] - (matrix_rate * 0.2 * math.sqrt(columns)) * ortho


def fixed(shape):
    return pl.BlockSpec(shape, lambda i, info: (0,) * len(shape))


ANY = pl.BlockSpec(memory_space=pl.ANY)


def params(grid=True):
    return pltpu.CompilerParams(
        dimension_semantics=("arbitrary",) if grid else None, vmem_limit_bytes=60 * 1024 * 1024
    )


def shape_of(shape, dtype):
    return jax.ShapeDtypeStruct(shape, dtype)


def cost(flops, read):
    return pl.CostEstimate(flops=int(flops), bytes_accessed=int(read), transcendentals=0)


def small_call(kernel, outs, name, scalars=0, scratch=()):
    vmem = pl.BlockSpec(memory_space=pltpu.VMEM)
    smem = pl.BlockSpec(memory_space=pltpu.SMEM)

    def call(*args):
        return pl.pallas_call(
            kernel,
            in_specs=[smem] * scalars + [vmem] * (len(args) - scalars),
            out_specs=[vmem] * len(outs),
            out_shape=[shape_of(*out) for out in outs],
            scratch_shapes=scratch,
            compiler_params=params(False),
            name=name,
        )(*args)

    return call


def group_specs(width, ff, start):
    heads = width // HEAD_DIM
    lanes = GROUP * SEQ
    deep = lambda i, info: (start + i, 0, 0)
    return (
        pl.BlockSpec((lanes, width), lambda i, info: (start + i, 0)),
        pl.BlockSpec((None, 3 * width, lanes), deep),
        pl.BlockSpec((None, GROUP * heads * SEQ, SEQ), deep),
        pl.BlockSpec((None, width, lanes), deep),
        pl.BlockSpec((None, ff, lanes), deep),
    )


def grid_call(kernel, info, start, stop, ins, outs, scratch, name, flops, before=()):
    return pl.pallas_call(
        kernel,
        grid_spec=pltpu.PrefetchScalarGridSpec(
            num_scalar_prefetch=1,
            grid=(stop - start,),
            in_specs=[spec or fixed(array.shape) for spec, array in ins] + [ANY] * len(before),
            out_specs=[spec or fixed(shape) for spec, shape, _ in outs],
            scratch_shapes=[pltpu.VMEM(*one) for one in scratch],
        ),
        out_shape=[shape_of(shape, dtype) for _, shape, dtype in outs],
        input_output_aliases={1 + len(ins) + i: i for i in range(len(before))},
        compiler_params=params(),
        cost_estimate=cost(flops * (stop - start), 4e6 * (stop - start)),
        name=name,
    )(info, *[array for _, array in ins], *before)


def order_ff(up_bias, par, half):
    parts = up_bias.reshape(half, 2, -1)
    return jnp.where(
        par == 0,
        jnp.concatenate([parts[:, 0], parts[:, 1]]),
        jnp.concatenate([parts[:, 1], parts[:, 0]]),
    ).reshape(-1)


def natural_ff(bias, half):
    return jnp.swapaxes(bias.reshape(2, half, -1), 0, 1).reshape(-1)


def spread_lanes(array):
    return jnp.broadcast_to(array[..., None], array.shape + (LANES,))


def body(
    block_in,
    out_grad,
    live_counts,
    qkv_weight,
    proj_weight,
    up_weight,
    down_weight,
    feature_vectors,
    up_bias,
    qkv_moment,
    proj_moment,
    up_moment,
    down_moment,
):
    devices = lax.axis_size("dp")
    half = devices // 2
    par = (lax.axis_index("dp") % 2).astype(jnp.int32)
    width = block_in.shape[1]
    groups = block_in.shape[0] // (GROUP * SEQ)
    ff = up_bias.shape[0]
    blocks = width // LANES
    turned = [w.T for w in (qkv_weight, proj_weight, up_weight, down_weight)]
    wq_s, wp_s, wu_s, wd_s = turned
    mq_s, mp_s, mu_s, md_s = [m.T for m in (qkv_moment, proj_moment, up_moment, down_moment)]
    cq, cp, cu, cd = (w.shape[0] for w in turned)
    pairs = [(i, i ^ 1) for i in range(devices)]
    planes = [[2 * i + c for i in range(half)] for c in range(2)]
    info = jnp.stack([live_counts[0], par])
    vec = spread_lanes(feature_vectors)
    ub = spread_lanes(order_ff(up_bias, par, half))

    def exchange(x):
        return lax.all_to_all(x, "dp", 0, 0, axis_index_groups=planes, tiled=True)

    def swap(x):
        return lax.ppermute(x, "dp", pairs)

    def after(x, *others):
        return lax.optimization_barrier((x,) + others)[0]

    first, second = small_call(
        prep_kernel,
        [((half, cq, width), bf16), ((half, -(-(cu + cd + cp) // 16) * 16, width), bf16)],
        "prep",
    )(wq_s, wp_s, wu_s, wd_s)
    lanes = GROUP * SEQ
    heads = width // HEAD_DIM
    tokens, qkv_spec, att_spec, deep_spec, ff_spec = group_specs(width, ff, 0)
    wide = (groups, width, lanes)
    z1 = grid_call(
        normal_kernel, info, 0, groups, [(tokens, block_in), (None, vec)], [(deep_spec, wide, bf16)], [],
        "normal", 1e9,
    )[0]
    wq_own = exchange(first)
    wq_other = swap(wq_own)
    rest_own = exchange(after(second, wq_own))

    def attend(start, stop, weights, before=()):
        _, qkv_at, att_at, deep_at, _ = group_specs(width, ff, start)
        fresh = start == 0
        return grid_call(
            functools.partial(attend_kernel, start), info, start, stop,
            [(deep_at, z1), (None, vec)] + [(None, w) for w in weights],
            [
                (qkv_at, (groups, 3 * width, lanes), bf16),
                (att_at, (groups, GROUP * heads * SEQ, SEQ), bf16),
                (deep_at, wide, bf16),
            ] + [(None, (3 * width, width), bf16)] * fresh,
            [
                ((3 * width, lanes), bf16),
                ((GROUP * heads, SEQ, SEQ), f32),
                ((GROUP * heads, SEQ, SEQ), bf16),
            ] + [((3 * width, width), f32)] * fresh,
            "attend", 4e9, before,
        )

    early = groups - 2 if groups > 2 else groups
    qkv, att, attn, wq = attend(0, early, (wq_own, wq_other))
    rest_own = after(rest_own, attn)
    rest_other = swap(rest_own)
    if early < groups:
        qkv, att, attn = attend(early, groups, (wq,), (qkv, att, attn))

    block = 256
    rows_b = 2 * cu + 4 + ff // width
    h1, act, dh, gp, wpn, wdn, keep_b, send_b = grid_call(
        mlp_kernel, info, 0, groups,
        [(tokens, block_in), (tokens, out_grad), (deep_spec, attn)]
        + [(None, array) for array in (rest_own, rest_other, vec, ub)],
        [
            (deep_spec, wide, f32),
            (ff_spec, (groups, ff, lanes), bf16),
            (deep_spec, wide, f32),
            (None, (width, width), f32),
            (None, (width, width), bf16),
            (None, (width, ff), bf16),
            (None, (half, rows_b, width), f32),
            (None, (half, rows_b, width), bf16),
        ],
        [
            ((width, ff), bf16),
            ((width, width), bf16),
            ((ff, width), bf16),
            ((ff, width), bf16),
            ((ff, width), f32),
            ((ff, width), f32),
            ((4, width, LANES), f32),
            ((ff, LANES), f32),
            ((width, lanes), f32),
            ((width, lanes), bf16),
            ((width, lanes), bf16),
            ((ff, lanes), bf16),
            ((ff, lanes), bf16),
            ((width, lanes), bf16),
            ((1, lanes), f32),
            ((ff, width), f32),
            ((2, block, lanes), f32),
            ((2, block, lanes), f32),
        ],
        "mlp", 10e9,
    )

    def back(start, stop, before=()):
        _, qkv_at, att_at, deep_at, _ = group_specs(width, ff, start)
        last = stop == groups
        rows = -(-(blocks * (cq + cp) + 4 * blocks) // 16) * 16
        totals = [(3 * width, width), (3, width, LANES)]
        scratch = [
            ((width, lanes), bf16),
            ((3 * width, lanes), bf16),
            ((GROUP * heads, SEQ, SEQ), f32),
            ((GROUP * heads, SEQ, SEQ), bf16),
        ]
        ins = [
            (deep_at, z1), (qkv_at, qkv), (att_at, att), (deep_at, dh),
            (None, wpn), (None, wq), (None, gp), (None, feature_vectors),
        ]
        outs = [(qkv_at, (groups, 3 * width, lanes), bf16)]
        if last:
            outs += [(None, (half, rows, LANES), f32), (None, (half, rows, LANES), bf16)]
            scratch = [(shape, f32) for shape in totals + [(rows, LANES)]] + scratch
        else:
            outs += [(None, shape, f32) for shape in totals]
        kernel = functools.partial(back_kernel, start, last)
        if not before:
            return grid_call(kernel, info, start, stop, ins, outs, scratch, "back", 6e9)
        ins += [(None, array) for array in before[1:]]
        return grid_call(kernel, info, start, stop, ins, outs, scratch, "back", 6e9, before[:1])

    def out_part(start, stop, before=()):
        tokens, _, _, deep_at, ff_at = group_specs(width, ff, start)
        return grid_call(
            functools.partial(out_kernel, start), info, start, stop,
            [(deep_at, h1), (ff_at, act), (None, wdn), (None, vec)],
            [(tokens, block_in.shape, f32)], [], "out", 1.5e9, before,
        )

    def input_part(start, stop, dqkv, before=()):
        tokens, qkv_at, _, deep_at, _ = group_specs(width, ff, start)
        return grid_call(
            functools.partial(input_kernel, start), info, start, stop,
            [(tokens, block_in), (qkv_at, dqkv), (deep_at, dh), (None, wq), (None, vec)],
            [(tokens, block_in.shape, f32)],
            [((width, 3 * width), bf16), ((1, lanes), f32), ((width, lanes), f32)], "input", 2e9, before,
        )

    def fold(keep, received):
        return (keep + received.astype(f32)).astype(bf16)

    def sums(got, moment_a, moment_b, vectors, spread, name):
        rows = moment_a.shape[0] + moment_b.shape[0]
        return small_call(
            state_kernel,
            [
                (moment_a.shape, f32), (moment_b.shape, f32), (moment_a.shape, f32), (moment_b.shape, f32),
                (spread, bf16), ((rows, width), f32), (vectors, f32),
            ],
            name + "_state",
            scalars=1,
        )(par.reshape(1), got, moment_a, moment_b)

    def polynomials(own, other, first, name):
        square = pltpu.VMEM((width, width), f32)
        parts = pltpu.VMEM((width, 3 * width), bf16)
        return small_call(
            newton_kernel,
            [((width + 8, width), f32)],
            name + "_newton",
            scalars=1,
            scratch=[square, square, square, parts, parts, parts, parts],
        )(jnp.stack([par, jnp.full((), first, jnp.int32)]), own, other)[0]

    def updates(mine, theirs, state, weight_a, weight_b, name):
        wide = (weight_a.shape[0] * devices, weight_b.shape[0] * devices)
        return small_call(
            functools.partial(update_kernel, wide),
            [(weight_a.shape, f32), (weight_b.shape, f32)],
            name + "_update",
            scalars=1,
        )(par.reshape(1), mine, theirs, state, weight_a, weight_b)

    swapped = swap(send_b)
    one = 1 if groups > 2 else groups
    done = back(0, one)
    swapped = after(swapped, done[1])
    got_b = exchange(fold(keep_b, swapped))
    if one < groups:
        done = back(one, groups, done)
    dqkv, keep_a, send_a = done
    summed_a = fold(keep_a, swap(send_a))
    got_b = after(got_b, summed_a)
    gu, gd, su, sd, spread_b, state_b, vector_b = sums(
        got_b, mu_s, md_s, (4 + ff // width, width), (2, cu, width), "mlp"
    )
    got_a = exchange(summed_a)

    bits = [1 << k for k in range(1, devices.bit_length() - 1)][::-1]
    pool = jnp.concatenate([spread_b[0], swap(spread_b[1])], axis=0)
    mid = groups // 2
    for index, bit in enumerate(bits):
        moved = lax.ppermute(pool, "dp", [(i, i ^ bit) for i in range(devices)])
        if index == 0:
            out = out_part(0, mid)
            moved = after(moved, out[0])
        elif index == 1:
            out = out_part(mid, groups, out)
            moved = after(moved, out[0])
        elif index == 2:
            dx = input_part(0, mid, dqkv)
            moved = after(moved, dx[0])
        if index + 1 < len(bits):
            pool = jnp.concatenate([pool, moved], axis=0)
    gq, gpr, sq, sp, spread_a, state_a, vector_a = sums(
        got_a, mq_s, mp_s, (4 * blocks, LANES), (half, cq + cp, width), "att"
    )
    own_a = exchange(spread_a)
    dx = input_part(mid, groups, dqkv, dx)
    mine_b = polynomials(pool, moved, cu, "mlp")
    other_a = swap(own_a)
    uu, ud = updates(mine_b, swap(mine_b), state_b, wu_s, wd_s, "mlp")
    mine_a = polynomials(own_a, other_a, cq, "att")
    uq, up = updates(mine_a, swap(mine_a), state_a, wq_s, wp_s, "att")
    out, dx = out[0], dx[0]

    vector_grad = jnp.concatenate([vector_a.reshape(4, width), vector_b[:4]], axis=0)
    bias_grad = natural_ff(vector_b[4:].reshape(ff), half)

    def normalized_step(param, gradient):
        return param - vector_rate * gradient * lax.rsqrt(
            jnp.mean(gradient * gradient, axis=-1, keepdims=True) + norm_eps
        )

    return (
        out, dx, gq.T, gpr.T, gu.T, gd.T, vector_grad, bias_grad, uq.T, up.T, uu.T, ud.T,
        sq.T, sp.T, su.T, sd.T,
        normalized_step(feature_vectors, vector_grad),
        normalized_step(up_bias, bias_grad),
    )


def solution(mesh):
    rows, columns, whole = P("dp", None), P(None, "dp"), P()
    return jax.shard_map(
        body,
        mesh=mesh,
        in_specs=(rows, rows, P("dp")) + (columns,) * 4 + (whole,) * 2 + (columns,) * 4,
        out_specs=(rows, rows) + (columns,) * 4 + (whole,) * 2 + (columns,) * 8 + (whole,) * 2,
        check_vma=False,
    )
```

```python
import functools
import math

import jax
import jax.numpy as jnp
from jax import lax
from jax.experimental import pallas as pl
from jax.experimental.pallas import tpu as pltpu
from jax.sharding import PartitionSpec as P

HEAD_DIM = 64
SEQ = 256
GROUP = 2
LANES = 128

norm_eps = 1e-06
newton_a = 3.4445
newton_b = -4.775
newton_c = 2.0315
momentum_decay = 0.9
matrix_rate = 0.15
vector_rate = 0.2

f32 = jnp.float32
bf16 = jnp.bfloat16


def nn(a, b):
    return lax.dot_general(a, b, (((1,), (0,)), ((), ())), preferred_element_type=f32)


def nt(a, b):
    return lax.dot_general(a, b, (((1,), (1,)), ((), ())), preferred_element_type=f32)


def tn(a, b):
    return lax.dot_general(a, b, (((0,), (0,)), ((), ())), preferred_element_type=f32)


def cols(index):
    return slice(index * LANES, (index + 1) * LANES)


def norm_parts(chunk):
    width = chunk.shape[0]
    center = chunk - jnp.sum(chunk, axis=0, keepdims=True) * (1.0 / width)
    scale = lax.rsqrt(jnp.sum(center * center, axis=0, keepdims=True) * (1.0 / width) + norm_eps)
    return center * scale, scale


def norm_back(inner, normed, scale):
    width = inner.shape[0]
    mean = jnp.sum(inner, axis=0, keepdims=True) * (1.0 / width)
    cross = jnp.sum(inner * normed, axis=0, keepdims=True) * (1.0 / width)
    return scale * (inner - mean - normed * cross)


def split_parts(x):
    high = x.astype(bf16)
    return high, (x - high.astype(f32)).astype(bf16)


def shard_rows(par, shard, own_ref, other_ref, first, count):
    span = slice(first, first + count)
    return jnp.where(par == shard % 2, own_ref[shard // 2, span, :], other_ref[shard // 2, span, :])


def lane_rows(acc):
    return [jnp.sum(acc[cols(c), :].T, axis=0, keepdims=True) for c in range(acc.shape[0] // LANES)]


def wide_rows(acc, width):
    rows = lane_rows(acc)
    per = width // LANES
    return [jnp.concatenate(rows[i : i + per], axis=1) for i in range(0, len(rows), per)]


def rounded(x):
    return x.astype(bf16).astype(f32)


def prep_kernel(wq_ref, wp_ref, wu_ref, wd_ref, first_ref, second_ref):
    first = wq_ref[...].astype(bf16)
    second = jnp.concatenate([wu_ref[...], wd_ref[...], wp_ref[...]], axis=0).astype(bf16)
    for index in range(first_ref.shape[0]):
        first_ref[index] = first
        second_ref[index, : second.shape[0], :] = second
        second_ref[index, second.shape[0] :, :] = jnp.zeros_like(second_ref[index, second.shape[0] :, :])


def normal_kernel(info, x_ref, vec_ref, z_ref):
    @pl.when(pl.program_id(0) * GROUP < info[0])
    def _():
        for c in range(z_ref.shape[1] // LANES):
            normed, _ = norm_parts(x_ref[cols(c), :].astype(f32).T)
            z_ref[:, cols(c)] = (normed * vec_ref[0] + vec_ref[1]).astype(bf16)


def attend_kernel(start, info, z_ref, vec_ref, *refs):
    if start == 0:
        own_ref, other_ref, qkv_ref, att_ref, out_ref, wq_ref, qkv_scr, s_scr, p_scr, stage = refs
    else:
        wq_ref, _, _, _, qkv_ref, att_ref, out_ref, qkv_scr, s_scr, p_scr = refs
    width, lanes = z_ref.shape
    heads = width // HEAD_DIM
    group = start + pl.program_id(0)

    if start == 0:

        @pl.when(pl.program_id(0) == 0)
        def _():
            count = own_ref.shape[1]
            for shard in range(2 * own_ref.shape[0]):
                rows = shard_rows(info[1], shard, own_ref, other_ref, 0, count)
                stage[shard * count : (shard + 1) * count, :] = rows.astype(f32)
            wq_ref[...] = stage[...].astype(bf16)

    @pl.when(group * GROUP < info[0])
    def _():
        for part in range(3):
            rows = slice(part * width, (part + 1) * width)
            made = nn(wq_ref[rows, :], z_ref[...])
            for c in range(lanes // LANES):
                piece = made[:, cols(c)]
                if part == 0:
                    piece = (piece + vec_ref[2]) * (1.0 / math.sqrt(HEAD_DIM))
                elif part == 2:
                    piece = piece + vec_ref[3]
                piece = piece.astype(bf16)
                qkv_scr[rows, cols(c)] = piece
                qkv_ref[rows, cols(c)] = piece
        for image in range(lanes // SEQ):
            span = slice(image * SEQ, (image + 1) * SEQ)
            for head in range(heads):
                low = head * HEAD_DIM
                query = qkv_scr[low : low + HEAD_DIM, span]
                keys = qkv_scr[width + low : width + low + HEAD_DIM, span]
                s_scr[image * heads + head] = tn(keys, query)
        for image in range(lanes // SEQ):
            span = slice(image * SEQ, (image + 1) * SEQ)
            for head in range(heads):
                low = head * HEAD_DIM
                slot = image * heads + head
                for c in range(SEQ // LANES):
                    scores = s_scr[slot, :, cols(c)]
                    top = jnp.max(scores, axis=0, keepdims=True)
                    raised = jnp.exp(scores - top)
                    total = jnp.sum(raised, axis=0, keepdims=True)
                    attend = (raised * (1.0 / total)).astype(bf16)
                    p_scr[slot, :, cols(c)] = attend
                    att_ref[slot * SEQ : (slot + 1) * SEQ, cols(c)] = attend
                values = qkv_scr[2 * width + low : 2 * width + low + HEAD_DIM, span]
                out_ref[low : low + HEAD_DIM, span] = nn(values, p_scr[slot]).astype(bf16)


def mlp_kernel(
    info, x_ref, cot_ref, att_ref, own_ref, other_ref, vec_ref, ub_ref,
    h_ref, act_ref, dh_ref, gp_ref, wpn_ref, wdn_ref, keep_ref, send_ref,
    wun_scr, wp_scr, wu_scr, wd_scr, gu_scr, gd_scr, rows_scr, bias_scr,
    n_scr, z_scr, m_scr, act_scr, du_scr, dhb_scr, s_scr, stage, u_scr, d_scr,
):
    width, lanes = z_scr.shape
    ff = wu_scr.shape[0]
    half = own_ref.shape[0]
    part = ff // (2 * half)
    step = pl.program_id(0)
    block = u_scr.shape[1]

    @pl.when(step == 0)
    def _():
        gp_ref[...] = jnp.zeros_like(gp_ref)
        rows_scr[...] = jnp.zeros_like(rows_scr)

        def clear(index, carry):
            rows = pl.ds(pl.multiple_of(index * LANES, LANES), LANES)
            gu_scr[rows, :] = jnp.zeros((LANES, width), f32)
            gd_scr[rows, :] = jnp.zeros((LANES, width), f32)
            bias_scr[rows, :] = jnp.zeros((LANES, LANES), f32)
            return carry

        lax.fori_loop(0, ff // LANES, clear, 0)
        count = width // (2 * half)
        for shard in range(2 * half):
            rows = shard_rows(info[1], shard, own_ref, other_ref, 2 * part, count)
            stage[shard * count : (shard + 1) * count, :] = rows.astype(f32)
        wp_scr[...] = stage[:width, :].astype(bf16)
        wpn_ref[...] = stage[:width, :].T.astype(bf16)
        for low, wide_scr in ((0, wu_scr), (part, wd_scr)):
            if part % 16 == 0:
                for side, ref in enumerate((own_ref, other_ref)):
                    for index in range(half):
                        at = (side * half + index) * part
                        wide_scr[at : at + part, :] = ref[index, low : low + part, :]
            else:
                for side, ref in enumerate((own_ref, other_ref)):
                    for index in range(half):
                        at = (side * half + index) * part
                        stage[at : at + part, :] = ref[index, low : low + part, :].astype(f32)
                wide_scr[...] = stage[...].astype(bf16)

        def turn(index, carry):
            rows = pl.ds(pl.multiple_of(index * block, block), block)
            wun_scr[:, rows] = wu_scr[rows, :].T
            wdn_ref[:, rows] = wd_scr[rows, :].T
            return carry

        lax.fori_loop(0, ff // block, turn, 0)

    @pl.when(step * GROUP < info[0])
    def _():
        made = nn(wp_scr[...], att_ref[...])
        total7 = jnp.zeros((width, LANES), f32)
        for c in range(lanes // LANES):
            chunk = x_ref[cols(c), :].astype(f32).T + made[:, cols(c)] + vec_ref[4]
            h_ref[:, cols(c)] = chunk
            normed, scale = norm_parts(chunk)
            n_scr[:, cols(c)] = normed
            s_scr[:, cols(c)] = scale
            z_scr[:, cols(c)] = (normed * vec_ref[5] + vec_ref[6]).astype(bf16)
            image = step * GROUP + c * LANES // SEQ
            cot = jnp.where(image < info[0], cot_ref[cols(c), :].astype(f32), 0.0).T
            m_scr[:, cols(c)] = cot.astype(bf16)
            total7 += cot
        rows_scr[3] += total7

        def first(c):
            rows = slice(c * block, (c + 1) * block)
            u_scr[c % 2] = nn(wu_scr[rows, :], z_scr[...])
            d_scr[c % 2] = nn(wd_scr[rows, :], m_scr[...])

        def second(c):
            for low in range(c * block, (c + 1) * block, 128):
                rows = slice(low, low + 128)
                here = slice(low - c * block, low - c * block + 128)
                bias = jnp.zeros((128, LANES), f32)
                for k in range(lanes // LANES):
                    u = u_scr[c % 2, here, cols(k)] + ub_ref[rows, :]
                    v = u * (1.0 / math.sqrt(2.0))
                    cdf = 0.5 + 0.5 * lax.erf(v)
                    act = (u * cdf).astype(bf16)
                    act_scr[rows, cols(k)] = act
                    act_ref[rows, cols(k)] = act
                    slope = cdf + (v * (1.0 / math.sqrt(math.pi))) * jnp.exp(-(v * v))
                    du = d_scr[c % 2, here, cols(k)] * slope
                    du_scr[rows, cols(k)] = du.astype(bf16)
                    bias += du
                bias_scr[rows, :] += bias

        def third(c):
            rows = slice(c * block, (c + 1) * block)
            gu_scr[rows, :] += nt(du_scr[rows, :], z_scr[...])
            gd_scr[rows, :] += nt(act_scr[rows, :], m_scr[...])

        chunks = ff // block
        first(0)
        for c in range(chunks):
            if c + 1 < chunks:
                first(c + 1)
            second(c)
            third(c)
        dz = nn(wun_scr[...], du_scr[...])
        total4 = jnp.zeros((width, LANES), f32)
        total5 = jnp.zeros((width, LANES), f32)
        total6 = jnp.zeros((width, LANES), f32)
        for c in range(lanes // LANES):
            piece = dz[:, cols(c)]
            normed = n_scr[:, cols(c)]
            dh = norm_back(piece * vec_ref[5], normed, s_scr[:, cols(c)]) + m_scr[:, cols(c)].astype(f32)
            dh_ref[:, cols(c)] = dh
            dhb_scr[:, cols(c)] = dh.astype(bf16)
            total4 += dh
            total5 += piece * normed
            total6 += piece
        rows_scr[0] += total4
        rows_scr[1] += total5
        rows_scr[2] += total6
        gp_ref[...] += nt(dhb_scr[...], att_ref[...])

    @pl.when(step == pl.num_programs(0) - 1)
    def _():
        vector = []
        for index in range(4):
            vector += wide_rows(rows_scr[index], width)
        hidden = wide_rows(bias_scr, width)
        side = len(hidden) // 2
        for index in range(len(hidden)):
            swapped = hidden[(index + side) % len(hidden)]
            vector.append(jnp.where(info[1] == 0, hidden[index], swapped))
        vector = jnp.concatenate(vector, axis=0)
        total = 2 * part + vector.shape[0]
        for index in range(half):
            keep_ref[index, :part, :] = gu_scr[index * part : (index + 1) * part, :]
            keep_ref[index, part : 2 * part, :] = gd_scr[index * part : (index + 1) * part, :]
            keep_ref[index, 2 * part : total, :] = rounded(vector)
            at = half * part + index * part
            if part % 16 == 0:
                send_ref[index, :part, :] = gu_scr[at : at + part, :].astype(bf16)
                send_ref[index, part : 2 * part, :] = gd_scr[at : at + part, :].astype(bf16)
                send_ref[index, 2 * part : total, :] = vector.astype(bf16)
            else:
                stage[:part, :] = gu_scr[at : at + part, :]
                stage[part : 2 * part, :] = gd_scr[at : at + part, :]
                stage[2 * part : total, :] = vector
                send_ref[index] = stage[: send_ref.shape[1], :].astype(bf16)


def out_kernel(start, info, h_ref, act_ref, wdn_ref, vec_ref, *refs):
    out_ref = refs[-1]
    group = start + pl.program_id(0)

    @pl.when(group * GROUP >= info[0])
    def _():
        out_ref[...] = jnp.zeros_like(out_ref)

    @pl.when(group * GROUP < info[0])
    def _():
        down = nn(wdn_ref[...], act_ref[...])
        for c in range(h_ref.shape[1] // LANES):
            image = group * GROUP + c * LANES // SEQ
            whole = down[:, cols(c)] + h_ref[:, cols(c)] + vec_ref[7]
            out_ref[cols(c), :] = jnp.where(image < info[0], whole, 0.0).T


def back_kernel(start, last, info, z_ref, qkv_ref, att_ref, dh_ref, wpn_ref, wq_ref, gp_ref, row_ref, *refs):
    if start:
        gq_in, rows_in, _ = refs[:3]
        refs = refs[3:]
    if last:
        dqkv_ref, keep_ref, send_ref, gq_ref, rows_ref, stage = refs[:6]
        refs = refs[6:]
    else:
        dqkv_ref, gq_ref, rows_ref = refs[:3]
        refs = refs[3:]
    da_scr, dqkv_scr, up_scr, ds_scr = refs
    width, lanes = z_ref.shape
    heads = width // HEAD_DIM
    step = pl.program_id(0)
    group = start + step

    @pl.when(step == 0)
    def _():
        if start == 0:
            gq_ref[...] = jnp.zeros_like(gq_ref)
            rows_ref[...] = jnp.zeros_like(rows_ref)
        else:
            gq_ref[...] = gq_in[...]
            rows_ref[...] = rows_in[...]

    @pl.when(group * GROUP < info[0])
    def _():
        da_scr[...] = nn(wpn_ref[...], dh_ref[...].astype(bf16)).astype(bf16)
        for image in range(lanes // SEQ):
            span = slice(image * SEQ, (image + 1) * SEQ)
            for head in range(heads):
                low = head * HEAD_DIM
                values = qkv_ref[2 * width + low : 2 * width + low + HEAD_DIM, span]
                up_scr[image * heads + head] = tn(values, da_scr[low : low + HEAD_DIM, span])
        for image in range(lanes // SEQ):
            span = slice(image * SEQ, (image + 1) * SEQ)
            for head in range(heads):
                low = head * HEAD_DIM
                high = low + HEAD_DIM
                slot = image * heads + head
                base = slot * SEQ
                for c in range(SEQ // LANES):
                    attend = att_ref[base : base + SEQ, cols(c)].astype(f32)
                    upstream = up_scr[slot, :, cols(c)]
                    delta = jnp.sum(attend * upstream, axis=0, keepdims=True)
                    ds_scr[slot, :, cols(c)] = (attend * (upstream - delta)).astype(bf16)
                query = qkv_ref[low:high, span]
                keys = qkv_ref[width + low : width + high, span]
                dscore = ds_scr[slot]
                dquery = nn(keys, dscore) * (1.0 / math.sqrt(HEAD_DIM))
                dkey = nt(query, dscore)
                dvalue = nt(da_scr[low:high, span], att_ref[base : base + SEQ, :])
                for part, value in enumerate((dquery, dkey, dvalue)):
                    rows = slice(part * width + low, part * width + high)
                    made = value.astype(bf16)
                    dqkv_scr[rows, span] = made
                    dqkv_ref[rows, span] = made
                    rows_ref[part, low:high, :] += value[:, :LANES] + value[:, LANES:]
        for part in range(3):
            rows = slice(part * width, (part + 1) * width)
            gq_ref[rows, :] += nt(dqkv_scr[rows, :], z_ref[...])

    if not last:
        return

    @pl.when(step == pl.num_programs(0) - 1)
    def _():
        count = 2 * keep_ref.shape[0]
        blocks = width // LANES
        sizes = (3 * width // count, width // count)
        rows = sum(sizes)
        stage[...] = jnp.zeros_like(stage)
        cross, plain = jnp.zeros((1, width), f32), jnp.zeros((1, width), f32)
        for part in range(3):
            rows_of = slice(part * width, (part + 1) * width)
            weight = wq_ref[rows_of, :].astype(f32)
            total = jnp.sum(rows_ref[part], axis=1, keepdims=True)
            cross += jnp.sum(weight * gq_ref[rows_of, :], axis=0, keepdims=True)
            plain += jnp.sum(weight * total, axis=0, keepdims=True)
        cross = (cross - row_ref[1:2, :] * plain) / row_ref[0:1, :]
        vector = [value[:, cols(c)] for value in (cross, plain) for c in range(blocks)]
        vector += lane_rows(rows_ref[0]) + lane_rows(rows_ref[2])
        for index, row in enumerate(vector):
            stage[blocks * rows + index : blocks * rows + index + 1, :] = rounded(row)
        for shard in range(count):
            for c in range(blocks):
                low = c * rows
                for piece, size in zip((gq_ref, gp_ref), sizes):
                    stage[low : low + size, :] = piece[shard * size : (shard + 1) * size, cols(c)]
                    low += size

            @pl.when(info[1] == shard % 2)
            def _():
                keep_ref[shard // 2] = stage[...]

            @pl.when(info[1] != shard % 2)
            def _():
                send_ref[shard // 2] = stage[...].astype(bf16)


def input_kernel(start, info, x_ref, dqkv_ref, dh_ref, wq_ref, vec_ref, *refs):
    out_ref, wqn_scr, s_scr, n_scr = refs[-4:]
    width, lanes = n_scr.shape
    step = pl.program_id(0)
    group = start + step

    @pl.when(step == 0)
    def _():
        for c in range(3):
            rows = slice(c * width, (c + 1) * width)
            wqn_scr[:, rows] = wq_ref[rows, :].T

    @pl.when(group * GROUP >= info[0])
    def _():
        out_ref[...] = jnp.zeros_like(out_ref)

    @pl.when(group * GROUP < info[0])
    def _():
        dz = nn(wqn_scr[...], dqkv_ref[...])
        for c in range(lanes // LANES):
            normed, scale = norm_parts(x_ref[cols(c), :].astype(f32).T)
            n_scr[:, cols(c)] = normed
            s_scr[:, cols(c)] = scale
        for c in range(lanes // LANES):
            inner = dz[:, cols(c)] * vec_ref[0]
            dx = norm_back(inner, n_scr[:, cols(c)], s_scr[:, cols(c)]) + dh_ref[:, cols(c)]
            out_ref[cols(c), :] = dx.T


def unpack_att(total, rows, width, vectors):
    blocks = width // LANES
    grad = jnp.concatenate([total[c * rows : (c + 1) * rows] for c in range(blocks)], axis=1)
    return grad, total[blocks * rows : blocks * rows + vectors]


def state_kernel(info, got_ref, ma_ref, mb_ref, ga_ref, gb_ref, sa_ref, sb_ref, spread_ref, state_ref, vec_ref):
    first, width = ma_ref.shape
    rows = first + mb_ref.shape[0]
    total = got_ref[0].astype(f32)
    for index in range(1, got_ref.shape[0]):
        total += got_ref[index].astype(f32)
    if got_ref.shape[2] == width:
        grad, vec_ref[...] = total[:rows], total[rows : rows + vec_ref.shape[0]]
    else:
        grad, vec_ref[...] = unpack_att(total, rows, width, vec_ref.shape[0])
    ga_ref[...] = grad[:first]
    gb_ref[...] = grad[first:]
    state = grad + momentum_decay * jnp.concatenate([ma_ref[...], mb_ref[...]], axis=0)
    sa_ref[...] = state[:first]
    sb_ref[...] = state[first:]
    state_ref[...] = state
    if got_ref.shape[2] == width:
        ours = info[0] == 0
        high, low = state[:first].astype(bf16), state[first:].astype(bf16)
        spread_ref[0] = jnp.where(ours, high, low)
        spread_ref[1] = jnp.where(ours, low, high)
    else:
        for index in range(spread_ref.shape[0]):
            spread_ref[index] = state.astype(bf16)


def store_parts(x, left_ref, right_ref):
    width = x.shape[0]
    high, low = split_parts(x)
    left_ref[:, :width] = high
    left_ref[:, width : 2 * width] = high
    left_ref[:, 2 * width :] = low
    right_ref[:, :width] = high
    right_ref[:, width : 2 * width] = low
    right_ref[:, 2 * width :] = high


def newton_kernel(info, own_ref, other_ref, out_ref, whole_ref, gram_scr, poly_scr, pa, pb, sa, sb):
    width = own_ref.shape[-1]
    eye = (
        lax.broadcasted_iota(jnp.int32, (width, width), 0)
        == lax.broadcasted_iota(jnp.int32, (width, width), 1)
    ).astype(f32)
    gram = jnp.zeros((width, width), f32)
    for ref in (own_ref, other_ref):
        if len(ref.shape) == 2:
            part = ref[...]
        else:
            place = lax.broadcasted_iota(jnp.int32, ref.shape[1:], 0)
            mine = (place < info[1]) == (info[0] == 0)
            part = jnp.concatenate(
                [jnp.where(mine, ref[index].astype(f32), 0.0) for index in range(ref.shape[0])], axis=0
            ).astype(bf16)
        gram += tn(part, part)
    norm = lax.rsqrt(jnp.sum(gram * eye) + norm_eps)
    out_ref[width:, :] = jnp.full((8, width), norm, f32)
    gram_scr[...] = gram * (norm * norm)
    whole_ref[...] = eye

    def turn(index, carry):
        store_parts(gram_scr[...], sa, sb)
        gram = gram_scr[...]
        poly = newton_a * eye + newton_b * gram + newton_c * nt(sa[...], sb[...])
        store_parts(poly, pa, pb)
        poly_scr[...] = nt(pa[...], sb[...])
        store_parts(whole_ref[...], sa, sb)
        whole_ref[...] = nt(pa[...], sb[...])

        @pl.when(index < 4)
        def _():
            store_parts(poly_scr[...], sa, sb)
            gram_scr[...] = nt(sa[...], pb[...])

        return carry

    lax.fori_loop(0, 5, turn, 0)
    out_ref[:width, :] = whole_ref[...]


def update_kernel(
    wide, info, mine_ref, theirs_ref, state_ref, wa_ref, wb_ref, ua_ref, ub_ref
):
    first = wa_ref.shape[0]
    rows = state_ref.shape[0]
    ours = info[0] == 0
    for low, high, w_ref, u_ref, columns, is_first in (
        (0, first, wa_ref, ua_ref, wide[0], True),
        (first, rows, wb_ref, ub_ref, wide[1], False),
    ):
        pick = ours if is_first else jnp.logical_not(ours)
        width = mine_ref.shape[1]
        whole = jnp.where(pick, mine_ref[:width, :], theirs_ref[:width, :])
        norm = jnp.where(pick, mine_ref[width : width + 1, :], theirs_ref[width : width + 1, :])
        state = state_ref[low:high, :] * norm
        sh, sl = split_parts(state)
        ph, pl_ = split_parts(whole)
        ortho = nt(sh, ph) + (nt(sl, ph) + nt(sh, pl_))
        u_ref[...] = w_ref[...] - (matrix_rate * 0.2 * math.sqrt(columns)) * ortho


def fixed(shape):
    return pl.BlockSpec(shape, lambda i, info: (0,) * len(shape))


ANY = pl.BlockSpec(memory_space=pl.ANY)


def params(grid=True):
    return pltpu.CompilerParams(
        dimension_semantics=("arbitrary",) if grid else None, vmem_limit_bytes=60 * 1024 * 1024
    )


def shape_of(shape, dtype):
    return jax.ShapeDtypeStruct(shape, dtype)


def cost(flops, read):
    return pl.CostEstimate(flops=int(flops), bytes_accessed=int(read), transcendentals=0)


def small_call(kernel, outs, name, scalars=0, scratch=()):
    vmem = pl.BlockSpec(memory_space=pltpu.VMEM)
    smem = pl.BlockSpec(memory_space=pltpu.SMEM)

    def call(*args):
        return pl.pallas_call(
            kernel,
            in_specs=[smem] * scalars + [vmem] * (len(args) - scalars),
            out_specs=[vmem] * len(outs),
            out_shape=[shape_of(*out) for out in outs],
            scratch_shapes=scratch,
            compiler_params=params(False),
            name=name,
        )(*args)

    return call


def group_specs(width, ff, start):
    heads = width // HEAD_DIM
    lanes = GROUP * SEQ
    deep = lambda i, info: (start + i, 0, 0)
    return (
        pl.BlockSpec((lanes, width), lambda i, info: (start + i, 0)),
        pl.BlockSpec((None, 3 * width, lanes), deep),
        pl.BlockSpec((None, GROUP * heads * SEQ, SEQ), deep),
        pl.BlockSpec((None, width, lanes), deep),
        pl.BlockSpec((None, ff, lanes), deep),
    )


def grid_call(kernel, info, start, stop, ins, outs, scratch, name, flops, before=()):
    return pl.pallas_call(
        kernel,
        grid_spec=pltpu.PrefetchScalarGridSpec(
            num_scalar_prefetch=1,
            grid=(stop - start,),
            in_specs=[spec or fixed(array.shape) for spec, array in ins] + [ANY] * len(before),
            out_specs=[spec or fixed(shape) for spec, shape, _ in outs],
            scratch_shapes=[pltpu.VMEM(*one) for one in scratch],
        ),
        out_shape=[shape_of(shape, dtype) for _, shape, dtype in outs],
        input_output_aliases={1 + len(ins) + i: i for i in range(len(before))},
        compiler_params=params(),
        cost_estimate=cost(flops * (stop - start), 4e6 * (stop - start)),
        name=name,
    )(info, *[array for _, array in ins], *before)


def order_ff(up_bias, par, half):
    parts = up_bias.reshape(half, 2, -1)
    return jnp.where(
        par == 0,
        jnp.concatenate([parts[:, 0], parts[:, 1]]),
        jnp.concatenate([parts[:, 1], parts[:, 0]]),
    ).reshape(-1)


def natural_ff(bias, half):
    return jnp.swapaxes(bias.reshape(2, half, -1), 0, 1).reshape(-1)


def spread_lanes(array):
    return jnp.broadcast_to(array[..., None], array.shape + (LANES,))


def body(
    block_in,
    out_grad,
    live_counts,
    qkv_weight,
    proj_weight,
    up_weight,
    down_weight,
    feature_vectors,
    up_bias,
    qkv_moment,
    proj_moment,
    up_moment,
    down_moment,
):
    devices = lax.axis_size("dp")
    half = devices // 2
    par = (lax.axis_index("dp") % 2).astype(jnp.int32)
    width = block_in.shape[1]
    groups = block_in.shape[0] // (GROUP * SEQ)
    ff = up_bias.shape[0]
    blocks = width // LANES
    turned = [w.T for w in (qkv_weight, proj_weight, up_weight, down_weight)]
    wq_s, wp_s, wu_s, wd_s = turned
    mq_s, mp_s, mu_s, md_s = [m.T for m in (qkv_moment, proj_moment, up_moment, down_moment)]
    cq, cp, cu, cd = (w.shape[0] for w in turned)
    pairs = [(i, i ^ 1) for i in range(devices)]
    planes = [[2 * i + c for i in range(half)] for c in range(2)]
    info = jnp.stack([live_counts[0], par])
    vec = spread_lanes(feature_vectors)
    ub = spread_lanes(order_ff(up_bias, par, half))

    def exchange(x):
        return lax.all_to_all(x, "dp", 0, 0, axis_index_groups=planes, tiled=True)

    def swap(x):
        return lax.ppermute(x, "dp", pairs)

    def after(x, *others):
        return lax.optimization_barrier((x,) + others)[0]

    first, second = small_call(
        prep_kernel,
        [((half, cq, width), bf16), ((half, -(-(cu + cd + cp) // 16) * 16, width), bf16)],
        "prep",
    )(wq_s, wp_s, wu_s, wd_s)
    lanes = GROUP * SEQ
    heads = width // HEAD_DIM
    tokens, qkv_spec, att_spec, deep_spec, ff_spec = group_specs(width, ff, 0)
    wide = (groups, width, lanes)
    z1 = grid_call(
        normal_kernel, info, 0, groups, [(tokens, block_in), (None, vec)], [(deep_spec, wide, bf16)], [],
        "normal", 1e9,
    )[0]
    wq_own = exchange(first)
    wq_other = swap(wq_own)
    rest_own = exchange(after(second, wq_own))

    def attend(start, stop, weights, before=()):
        _, qkv_at, att_at, deep_at, _ = group_specs(width, ff, start)
        fresh = start == 0
        return grid_call(
            functools.partial(attend_kernel, start), info, start, stop,
            [(deep_at, z1), (None, vec)] + [(None, w) for w in weights],
            [
                (qkv_at, (groups, 3 * width, lanes), bf16),
                (att_at, (groups, GROUP * heads * SEQ, SEQ), bf16),
                (deep_at, wide, bf16),
            ] + [(None, (3 * width, width), bf16)] * fresh,
            [
                ((3 * width, lanes), bf16),
                ((GROUP * heads, SEQ, SEQ), f32),
                ((GROUP * heads, SEQ, SEQ), bf16),
            ] + [((3 * width, width), f32)] * fresh,
            "attend", 4e9, before,
        )

    early = groups - 2 if groups > 2 else groups
    qkv, att, attn, wq = attend(0, early, (wq_own, wq_other))
    rest_own = after(rest_own, attn)
    rest_other = swap(rest_own)
    if early < groups:
        qkv, att, attn = attend(early, groups, (wq,), (qkv, att, attn))

    block = 256
    rows_b = 2 * cu + 4 + ff // width
    h1, act, dh, gp, wpn, wdn, keep_b, send_b = grid_call(
        mlp_kernel, info, 0, groups,
        [(tokens, block_in), (tokens, out_grad), (deep_spec, attn)]
        + [(None, array) for array in (rest_own, rest_other, vec, ub)],
        [
            (deep_spec, wide, f32),
            (ff_spec, (groups, ff, lanes), bf16),
            (deep_spec, wide, f32),
            (None, (width, width), f32),
            (None, (width, width), bf16),
            (None, (width, ff), bf16),
            (None, (half, rows_b, width), f32),
            (None, (half, rows_b, width), bf16),
        ],
        [
            ((width, ff), bf16),
            ((width, width), bf16),
            ((ff, width), bf16),
            ((ff, width), bf16),
            ((ff, width), f32),
            ((ff, width), f32),
            ((4, width, LANES), f32),
            ((ff, LANES), f32),
            ((width, lanes), f32),
            ((width, lanes), bf16),
            ((width, lanes), bf16),
            ((ff, lanes), bf16),
            ((ff, lanes), bf16),
            ((width, lanes), bf16),
            ((1, lanes), f32),
            ((ff, width), f32),
            ((2, block, lanes), f32),
            ((2, block, lanes), f32),
        ],
        "mlp", 10e9,
    )

    def back(start, stop, before=(), info=info):
        _, qkv_at, att_at, deep_at, _ = group_specs(width, ff, start)
        last = stop == groups
        rows = -(-(blocks * (cq + cp) + 4 * blocks) // 16) * 16
        totals = [(3 * width, width), (3, width, LANES)]
        scratch = [
            ((width, lanes), bf16),
            ((3 * width, lanes), bf16),
            ((GROUP * heads, SEQ, SEQ), f32),
            ((GROUP * heads, SEQ, SEQ), bf16),
        ]
        ins = [
            (deep_at, z1), (qkv_at, qkv), (att_at, att), (deep_at, dh),
            (None, wpn), (None, wq), (None, gp), (None, feature_vectors),
        ]
        outs = [(qkv_at, (groups, 3 * width, lanes), bf16)]
        if last:
            outs += [(None, (half, rows, LANES), f32), (None, (half, rows, LANES), bf16)]
            scratch = [(shape, f32) for shape in totals + [(rows, LANES)]] + scratch
        else:
            outs += [(None, shape, f32) for shape in totals]
        kernel = functools.partial(back_kernel, start, last)
        if not before:
            return grid_call(kernel, info, start, stop, ins, outs, scratch, "back", 6e9)
        ins += [(None, array) for array in before[1:]]
        return grid_call(kernel, info, start, stop, ins, outs, scratch, "back", 6e9, before[:1])

    def out_part(start, stop, info, before=()):
        tokens, _, _, deep_at, ff_at = group_specs(width, ff, start)
        return grid_call(
            functools.partial(out_kernel, start), info, start, stop,
            [(deep_at, h1), (ff_at, act), (None, wdn), (None, vec)],
            [(tokens, block_in.shape, f32)], [], "out", 1.5e9, before,
        )

    def input_part(start, stop, dqkv, info, before=()):
        tokens, qkv_at, _, deep_at, _ = group_specs(width, ff, start)
        return grid_call(
            functools.partial(input_kernel, start), info, start, stop,
            [(tokens, block_in), (qkv_at, dqkv), (deep_at, dh), (None, wq), (None, vec)],
            [(tokens, block_in.shape, f32)],
            [((width, 3 * width), bf16), ((1, lanes), f32), ((width, lanes), f32)], "input", 2e9, before,
        )

    def fold(keep, received):
        return (keep + received.astype(f32)).astype(bf16)

    def sums(got, moment_a, moment_b, vectors, spread, name):
        rows = moment_a.shape[0] + moment_b.shape[0]
        return small_call(
            state_kernel,
            [
                (moment_a.shape, f32), (moment_b.shape, f32), (moment_a.shape, f32), (moment_b.shape, f32),
                (spread, bf16), ((rows, width), f32), (vectors, f32),
            ],
            name + "_state",
            scalars=1,
        )(par.reshape(1), got, moment_a, moment_b)

    def polynomials(own, other, first, name):
        square = pltpu.VMEM((width, width), f32)
        parts = pltpu.VMEM((width, 3 * width), bf16)
        return small_call(
            newton_kernel,
            [((width + 8, width), f32)],
            name + "_newton",
            scalars=1,
            scratch=[square, square, square, parts, parts, parts, parts],
        )(jnp.stack([par, jnp.full((), first, jnp.int32)]), own, other)[0]

    def updates(mine, theirs, state, weight_a, weight_b, name):
        wide = (weight_a.shape[0] * devices, weight_b.shape[0] * devices)
        return small_call(
            functools.partial(update_kernel, wide),
            [(weight_a.shape, f32), (weight_b.shape, f32)],
            name + "_update",
            scalars=1,
        )(par.reshape(1), mine, theirs, state, weight_a, weight_b)

    swapped = swap(send_b)
    one = 1 if groups > 2 else groups
    done = back(0, one)
    summed_b = fold(keep_b, after(swapped, done[1]))
    got_b = exchange(summed_b)
    if one < groups:
        done = back(one, groups, done, after(info, summed_b))
    dqkv, keep_a, send_a = done
    send_a, got_b = lax.optimization_barrier((send_a, got_b))
    summed_a = fold(keep_a, swap(send_a))
    got_a = exchange(summed_a)
    gate = after(info, summed_a)
    gu, gd, su, sd, spread_b, state_b, vector_b = sums(
        after(got_b, summed_a), mu_s, md_s, (4 + ff // width, width), (2, cu, width), "mlp"
    )

    bits = [1 << k for k in range(1, devices.bit_length() - 1)][::-1]

    def gather_step(pool, bit):
        return lax.ppermute(pool, "dp", [(i, i ^ bit) for i in range(devices)])

    def joined(pool, moved):
        return jnp.concatenate([pool, moved], axis=0)

    mid = groups // 2
    pool = joined(spread_b[0], swap(spread_b[1]))
    moved = gather_step(pool, bits[0])
    out = out_part(0, mid, after(gate, pool))
    for bit in bits[1:-2]:
        pool = joined(pool, after(moved, out[0]))
        moved = gather_step(pool, bit)
    out = out_part(mid, groups, after(gate, pool), out)
    got_a = after(got_a, out[0])
    gq, gpr, sq, sp, spread_a, state_a, vector_a = sums(
        got_a, mq_s, mp_s, (4 * blocks, LANES), (half, cq + cp, width), "att"
    )
    own_a = exchange(spread_a)
    pool = joined(pool, after(moved, spread_a))
    moved = gather_step(pool, bits[-2])
    dx = input_part(0, mid, dqkv, after(info, pool))
    pool = joined(pool, after(moved, dx[0]))
    moved = gather_step(pool, bits[-1])
    dx = input_part(mid, groups, dqkv, after(info, pool), dx)
    own_a = after(own_a, dx[0])
    other_a = swap(own_a)
    mine_a = polynomials(own_a, other_a, cq, "att")
    theirs_a = swap(mine_a)
    mine_b = polynomials(pool, after(moved, mine_a), cu, "mlp")
    uq, up = updates(mine_a, after(theirs_a, mine_b), state_a, wq_s, wp_s, "att")
    uu, ud = updates(mine_b, swap(mine_b), state_b, wu_s, wd_s, "mlp")
    out, dx = out[0], dx[0]

    vector_grad = jnp.concatenate([vector_a.reshape(4, width), vector_b[:4]], axis=0)
    bias_grad = natural_ff(vector_b[4:].reshape(ff), half)

    def normalized_step(param, gradient):
        return param - vector_rate * gradient * lax.rsqrt(
            jnp.mean(gradient * gradient, axis=-1, keepdims=True) + norm_eps
        )

    return (
        out, dx, gq.T, gpr.T, gu.T, gd.T, vector_grad, bias_grad, uq.T, up.T, uu.T, ud.T,
        sq.T, sp.T, su.T, sd.T,
        normalized_step(feature_vectors, vector_grad),
        normalized_step(up_bias, bias_grad),
    )


def solution(mesh):
    rows, columns, whole = P("dp", None), P(None, "dp"), P()
    return jax.shard_map(
        body,
        mesh=mesh,
        in_specs=(rows, rows, P("dp")) + (columns,) * 4 + (whole,) * 2 + (columns,) * 4,
        out_specs=(rows, rows) + (columns,) * 4 + (whole,) * 2 + (columns,) * 8 + (whole,) * 2,
        check_vma=False,
    )
```

```python
import functools
import math

import jax
import jax.numpy as jnp
from jax import lax
from jax.experimental import pallas as pl
from jax.experimental.pallas import tpu as pltpu
from jax.sharding import PartitionSpec as P

HEAD_DIM = 64
SEQ = 256
GROUP = 2
LANES = 128

norm_eps = 1e-06
newton_a = 3.4445
newton_b = -4.775
newton_c = 2.0315
momentum_decay = 0.9
matrix_rate = 0.15
vector_rate = 0.2

f32 = jnp.float32
bf16 = jnp.bfloat16


def nn(a, b):
    return lax.dot_general(a, b, (((1,), (0,)), ((), ())), preferred_element_type=f32)


def nt(a, b):
    return lax.dot_general(a, b, (((1,), (1,)), ((), ())), preferred_element_type=f32)


def tn(a, b):
    return lax.dot_general(a, b, (((0,), (0,)), ((), ())), preferred_element_type=f32)


def cols(index):
    return slice(index * LANES, (index + 1) * LANES)


def norm_parts(chunk):
    width = chunk.shape[0]
    center = chunk - jnp.sum(chunk, axis=0, keepdims=True) * (1.0 / width)
    scale = lax.rsqrt(jnp.sum(center * center, axis=0, keepdims=True) * (1.0 / width) + norm_eps)
    return center * scale, scale


def norm_back(inner, normed, scale):
    width = inner.shape[0]
    mean = jnp.sum(inner, axis=0, keepdims=True) * (1.0 / width)
    cross = jnp.sum(inner * normed, axis=0, keepdims=True) * (1.0 / width)
    return scale * (inner - mean - normed * cross)


def split_parts(x):
    high = x.astype(bf16)
    return high, (x - high.astype(f32)).astype(bf16)


def shard_rows(par, shard, own_ref, other_ref, first, count):
    span = slice(first, first + count)
    return jnp.where(par == shard % 2, own_ref[shard // 2, span, :], other_ref[shard // 2, span, :])


def lane_rows(acc):
    return [jnp.sum(acc[cols(c), :].T, axis=0, keepdims=True) for c in range(acc.shape[0] // LANES)]


def wide_rows(acc, width):
    rows = lane_rows(acc)
    per = width // LANES
    return [jnp.concatenate(rows[i : i + per], axis=1) for i in range(0, len(rows), per)]


def rounded(x):
    return x.astype(bf16).astype(f32)


def prep_kernel(wq_ref, wp_ref, wu_ref, wd_ref, first_ref, second_ref):
    first = wq_ref[...].astype(bf16)
    second = jnp.concatenate([wu_ref[...], wd_ref[...], wp_ref[...]], axis=0).astype(bf16)
    for index in range(first_ref.shape[0]):
        first_ref[index] = first
        second_ref[index, : second.shape[0], :] = second
        second_ref[index, second.shape[0] :, :] = jnp.zeros_like(second_ref[index, second.shape[0] :, :])


def normal_kernel(info, x_ref, vec_ref, z_ref):
    @pl.when(pl.program_id(0) * GROUP < info[0])
    def _():
        for c in range(z_ref.shape[1] // LANES):
            normed, _ = norm_parts(x_ref[cols(c), :].astype(f32).T)
            z_ref[:, cols(c)] = (normed * vec_ref[0] + vec_ref[1]).astype(bf16)


def attend_kernel(start, info, z_ref, vec_ref, *refs):
    if start == 0:
        own_ref, other_ref, qkv_ref, att_ref, out_ref, wq_ref, qkv_scr, s_scr, p_scr, stage = refs
    else:
        wq_ref, _, _, _, qkv_ref, att_ref, out_ref, qkv_scr, s_scr, p_scr = refs
    width, lanes = z_ref.shape
    heads = width // HEAD_DIM
    group = start + pl.program_id(0)

    if start == 0:

        @pl.when(pl.program_id(0) == 0)
        def _():
            count = own_ref.shape[1]
            for shard in range(2 * own_ref.shape[0]):
                rows = shard_rows(info[1], shard, own_ref, other_ref, 0, count)
                stage[shard * count : (shard + 1) * count, :] = rows.astype(f32)
            wq_ref[...] = stage[...].astype(bf16)

    @pl.when(group * GROUP < info[0])
    def _():
        for part in range(3):
            rows = slice(part * width, (part + 1) * width)
            made = nn(wq_ref[rows, :], z_ref[...])
            for c in range(lanes // LANES):
                piece = made[:, cols(c)]
                if part == 0:
                    piece = (piece + vec_ref[2]) * (1.0 / math.sqrt(HEAD_DIM))
                elif part == 2:
                    piece = piece + vec_ref[3]
                piece = piece.astype(bf16)
                qkv_scr[rows, cols(c)] = piece
                qkv_ref[rows, cols(c)] = piece
        for image in range(lanes // SEQ):
            span = slice(image * SEQ, (image + 1) * SEQ)
            for head in range(heads):
                low = head * HEAD_DIM
                query = qkv_scr[low : low + HEAD_DIM, span]
                keys = qkv_scr[width + low : width + low + HEAD_DIM, span]
                s_scr[image * heads + head] = tn(keys, query)
        for image in range(lanes // SEQ):
            span = slice(image * SEQ, (image + 1) * SEQ)
            for head in range(heads):
                low = head * HEAD_DIM
                slot = image * heads + head
                for c in range(SEQ // LANES):
                    scores = s_scr[slot, :, cols(c)]
                    top = jnp.max(scores, axis=0, keepdims=True)
                    raised = jnp.exp(scores - top)
                    total = jnp.sum(raised, axis=0, keepdims=True)
                    attend = (raised * (1.0 / total)).astype(bf16)
                    p_scr[slot, :, cols(c)] = attend
                    att_ref[slot * SEQ : (slot + 1) * SEQ, cols(c)] = attend
                values = qkv_scr[2 * width + low : 2 * width + low + HEAD_DIM, span]
                out_ref[low : low + HEAD_DIM, span] = nn(values, p_scr[slot]).astype(bf16)


def mlp_kernel(
    info, x_ref, cot_ref, att_ref, own_ref, other_ref, vec_ref, ub_ref,
    h_ref, act_ref, dh_ref, gp_ref, wpn_ref, wdn_ref, keep_ref, send_ref,
    wun_scr, wp_scr, wu_scr, wd_scr, gu_scr, gd_scr, rows_scr, bias_scr,
    n_scr, z_scr, m_scr, act_scr, du_scr, dhb_scr, s_scr, stage, u_scr, d_scr,
):
    width, lanes = z_scr.shape
    ff = wu_scr.shape[0]
    half = own_ref.shape[0]
    part = ff // (2 * half)
    step = pl.program_id(0)
    block = u_scr.shape[1]

    @pl.when(step == 0)
    def _():
        gp_ref[...] = jnp.zeros_like(gp_ref)
        rows_scr[...] = jnp.zeros_like(rows_scr)

        def clear(index, carry):
            rows = pl.ds(pl.multiple_of(index * LANES, LANES), LANES)
            gu_scr[rows, :] = jnp.zeros((LANES, width), f32)
            gd_scr[rows, :] = jnp.zeros((LANES, width), f32)
            bias_scr[rows, :] = jnp.zeros((LANES, LANES), f32)
            return carry

        lax.fori_loop(0, ff // LANES, clear, 0)
        count = width // (2 * half)
        for shard in range(2 * half):
            rows = shard_rows(info[1], shard, own_ref, other_ref, 2 * part, count)
            stage[shard * count : (shard + 1) * count, :] = rows.astype(f32)
        wp_scr[...] = stage[:width, :].astype(bf16)
        wpn_ref[...] = stage[:width, :].T.astype(bf16)
        for low, wide_scr in ((0, wu_scr), (part, wd_scr)):
            if part % 16 == 0:
                for side, ref in enumerate((own_ref, other_ref)):
                    for index in range(half):
                        at = (side * half + index) * part
                        wide_scr[at : at + part, :] = ref[index, low : low + part, :]
            else:
                for side, ref in enumerate((own_ref, other_ref)):
                    for index in range(half):
                        at = (side * half + index) * part
                        stage[at : at + part, :] = ref[index, low : low + part, :].astype(f32)
                wide_scr[...] = stage[...].astype(bf16)

        def turn(index, carry):
            rows = pl.ds(pl.multiple_of(index * block, block), block)
            wun_scr[:, rows] = wu_scr[rows, :].T
            wdn_ref[:, rows] = wd_scr[rows, :].T
            return carry

        lax.fori_loop(0, ff // block, turn, 0)

    @pl.when(step * GROUP < info[0])
    def _():
        made = nn(wp_scr[...], att_ref[...])
        total7 = jnp.zeros((width, LANES), f32)
        for c in range(lanes // LANES):
            chunk = x_ref[cols(c), :].astype(f32).T + made[:, cols(c)] + vec_ref[4]
            h_ref[:, cols(c)] = chunk
            normed, scale = norm_parts(chunk)
            n_scr[:, cols(c)] = normed
            s_scr[:, cols(c)] = scale
            z_scr[:, cols(c)] = (normed * vec_ref[5] + vec_ref[6]).astype(bf16)
            image = step * GROUP + c * LANES // SEQ
            cot = jnp.where(image < info[0], cot_ref[cols(c), :].astype(f32), 0.0).T
            m_scr[:, cols(c)] = cot.astype(bf16)
            total7 += cot
        rows_scr[3] += total7

        def first(c):
            rows = slice(c * block, (c + 1) * block)
            u_scr[c % 2] = nn(wu_scr[rows, :], z_scr[...])
            d_scr[c % 2] = nn(wd_scr[rows, :], m_scr[...])

        def second(c):
            for low in range(c * block, (c + 1) * block, 128):
                rows = slice(low, low + 128)
                here = slice(low - c * block, low - c * block + 128)
                bias = jnp.zeros((128, LANES), f32)
                for k in range(lanes // LANES):
                    u = u_scr[c % 2, here, cols(k)] + ub_ref[rows, :]
                    v = u * (1.0 / math.sqrt(2.0))
                    cdf = 0.5 + 0.5 * lax.erf(v)
                    act = (u * cdf).astype(bf16)
                    act_scr[rows, cols(k)] = act
                    act_ref[rows, cols(k)] = act
                    slope = cdf + (v * (1.0 / math.sqrt(math.pi))) * jnp.exp(-(v * v))
                    du = d_scr[c % 2, here, cols(k)] * slope
                    du_scr[rows, cols(k)] = du.astype(bf16)
                    bias += du
                bias_scr[rows, :] += bias

        def third(c):
            rows = slice(c * block, (c + 1) * block)
            gu_scr[rows, :] += nt(du_scr[rows, :], z_scr[...])
            gd_scr[rows, :] += nt(act_scr[rows, :], m_scr[...])

        chunks = ff // block
        first(0)
        for c in range(chunks):
            if c + 1 < chunks:
                first(c + 1)
            second(c)
            third(c)
        dz = nn(wun_scr[...], du_scr[...])
        total4 = jnp.zeros((width, LANES), f32)
        total5 = jnp.zeros((width, LANES), f32)
        total6 = jnp.zeros((width, LANES), f32)
        for c in range(lanes // LANES):
            piece = dz[:, cols(c)]
            normed = n_scr[:, cols(c)]
            dh = norm_back(piece * vec_ref[5], normed, s_scr[:, cols(c)]) + m_scr[:, cols(c)].astype(f32)
            dh_ref[:, cols(c)] = dh
            dhb_scr[:, cols(c)] = dh.astype(bf16)
            total4 += dh
            total5 += piece * normed
            total6 += piece
        rows_scr[0] += total4
        rows_scr[1] += total5
        rows_scr[2] += total6
        gp_ref[...] += nt(dhb_scr[...], att_ref[...])

    @pl.when(step == pl.num_programs(0) - 1)
    def _():
        vector = []
        for index in range(4):
            vector += wide_rows(rows_scr[index], width)
        hidden = wide_rows(bias_scr, width)
        side = len(hidden) // 2
        for index in range(len(hidden)):
            swapped = hidden[(index + side) % len(hidden)]
            vector.append(jnp.where(info[1] == 0, hidden[index], swapped))
        vector = jnp.concatenate(vector, axis=0)
        total = 2 * part + vector.shape[0]
        for index in range(half):
            keep_ref[index, :part, :] = gu_scr[index * part : (index + 1) * part, :]
            keep_ref[index, part : 2 * part, :] = gd_scr[index * part : (index + 1) * part, :]
            keep_ref[index, 2 * part : total, :] = rounded(vector)
            at = half * part + index * part
            if part % 16 == 0:
                send_ref[index, :part, :] = gu_scr[at : at + part, :].astype(bf16)
                send_ref[index, part : 2 * part, :] = gd_scr[at : at + part, :].astype(bf16)
                send_ref[index, 2 * part : total, :] = vector.astype(bf16)
            else:
                stage[:part, :] = gu_scr[at : at + part, :]
                stage[part : 2 * part, :] = gd_scr[at : at + part, :]
                stage[2 * part : total, :] = vector
                send_ref[index] = stage[: send_ref.shape[1], :].astype(bf16)


def out_kernel(start, info, h_ref, act_ref, wdn_ref, vec_ref, *refs):
    out_ref = refs[-1]
    group = start + pl.program_id(0)

    @pl.when(group * GROUP >= info[0])
    def _():
        out_ref[...] = jnp.zeros_like(out_ref)

    @pl.when(group * GROUP < info[0])
    def _():
        down = nn(wdn_ref[...], act_ref[...])
        for c in range(h_ref.shape[1] // LANES):
            image = group * GROUP + c * LANES // SEQ
            whole = down[:, cols(c)] + h_ref[:, cols(c)] + vec_ref[7]
            out_ref[cols(c), :] = jnp.where(image < info[0], whole, 0.0).T


def back_kernel(start, last, info, z_ref, qkv_ref, att_ref, dh_ref, wpn_ref, wq_ref, gp_ref, row_ref, *refs):
    if start:
        gq_in, rows_in, _ = refs[:3]
        refs = refs[3:]
    if last:
        dqkv_ref, keep_ref, send_ref, gq_ref, rows_ref, stage = refs[:6]
        refs = refs[6:]
    else:
        dqkv_ref, gq_ref, rows_ref = refs[:3]
        refs = refs[3:]
    da_scr, dqkv_scr, up_scr, ds_scr = refs
    width, lanes = z_ref.shape
    heads = width // HEAD_DIM
    step = pl.program_id(0)
    group = start + step

    @pl.when(step == 0)
    def _():
        if start == 0:
            gq_ref[...] = jnp.zeros_like(gq_ref)
            rows_ref[...] = jnp.zeros_like(rows_ref)
        else:
            gq_ref[...] = gq_in[...]
            rows_ref[...] = rows_in[...]

    @pl.when(group * GROUP < info[0])
    def _():
        da_scr[...] = nn(wpn_ref[...], dh_ref[...].astype(bf16)).astype(bf16)
        for image in range(lanes // SEQ):
            span = slice(image * SEQ, (image + 1) * SEQ)
            for head in range(heads):
                low = head * HEAD_DIM
                values = qkv_ref[2 * width + low : 2 * width + low + HEAD_DIM, span]
                up_scr[image * heads + head] = tn(values, da_scr[low : low + HEAD_DIM, span])
        for image in range(lanes // SEQ):
            span = slice(image * SEQ, (image + 1) * SEQ)
            for head in range(heads):
                low = head * HEAD_DIM
                high = low + HEAD_DIM
                slot = image * heads + head
                base = slot * SEQ
                for c in range(SEQ // LANES):
                    attend = att_ref[base : base + SEQ, cols(c)].astype(f32)
                    upstream = up_scr[slot, :, cols(c)]
                    delta = jnp.sum(attend * upstream, axis=0, keepdims=True)
                    ds_scr[slot, :, cols(c)] = (attend * (upstream - delta)).astype(bf16)
                query = qkv_ref[low:high, span]
                keys = qkv_ref[width + low : width + high, span]
                dscore = ds_scr[slot]
                dquery = nn(keys, dscore) * (1.0 / math.sqrt(HEAD_DIM))
                dkey = nt(query, dscore)
                dvalue = nt(da_scr[low:high, span], att_ref[base : base + SEQ, :])
                for part, value in enumerate((dquery, dkey, dvalue)):
                    rows = slice(part * width + low, part * width + high)
                    made = value.astype(bf16)
                    dqkv_scr[rows, span] = made
                    dqkv_ref[rows, span] = made
                    rows_ref[part, low:high, :] += value[:, :LANES] + value[:, LANES:]
        for part in range(3):
            rows = slice(part * width, (part + 1) * width)
            gq_ref[rows, :] += nt(dqkv_scr[rows, :], z_ref[...])

    if not last:
        return

    @pl.when(step == pl.num_programs(0) - 1)
    def _():
        count = 2 * keep_ref.shape[0]
        blocks = width // LANES
        sizes = (3 * width // count, width // count)
        rows = sum(sizes)
        stage[...] = jnp.zeros_like(stage)
        cross, plain = jnp.zeros((1, width), f32), jnp.zeros((1, width), f32)
        for part in range(3):
            rows_of = slice(part * width, (part + 1) * width)
            weight = wq_ref[rows_of, :].astype(f32)
            total = jnp.sum(rows_ref[part], axis=1, keepdims=True)
            cross += jnp.sum(weight * gq_ref[rows_of, :], axis=0, keepdims=True)
            plain += jnp.sum(weight * total, axis=0, keepdims=True)
        cross = (cross - row_ref[1:2, :] * plain) / row_ref[0:1, :]
        vector = [value[:, cols(c)] for value in (cross, plain) for c in range(blocks)]
        vector += lane_rows(rows_ref[0]) + lane_rows(rows_ref[2])
        for index, row in enumerate(vector):
            stage[blocks * rows + index : blocks * rows + index + 1, :] = rounded(row)
        for shard in range(count):
            for c in range(blocks):
                low = c * rows
                for piece, size in zip((gq_ref, gp_ref), sizes):
                    stage[low : low + size, :] = piece[shard * size : (shard + 1) * size, cols(c)]
                    low += size

            @pl.when(info[1] == shard % 2)
            def _():
                keep_ref[shard // 2] = stage[...]

            @pl.when(info[1] != shard % 2)
            def _():
                send_ref[shard // 2] = stage[...].astype(bf16)


def input_kernel(start, info, x_ref, dqkv_ref, dh_ref, wq_ref, vec_ref, *refs):
    out_ref, wqn_scr, s_scr, n_scr = refs[-4:]
    width, lanes = n_scr.shape
    step = pl.program_id(0)
    group = start + step

    @pl.when(step == 0)
    def _():
        for c in range(3):
            rows = slice(c * width, (c + 1) * width)
            wqn_scr[:, rows] = wq_ref[rows, :].T

    @pl.when(group * GROUP >= info[0])
    def _():
        out_ref[...] = jnp.zeros_like(out_ref)

    @pl.when(group * GROUP < info[0])
    def _():
        dz = nn(wqn_scr[...], dqkv_ref[...])
        for c in range(lanes // LANES):
            normed, scale = norm_parts(x_ref[cols(c), :].astype(f32).T)
            n_scr[:, cols(c)] = normed
            s_scr[:, cols(c)] = scale
        for c in range(lanes // LANES):
            inner = dz[:, cols(c)] * vec_ref[0]
            dx = norm_back(inner, n_scr[:, cols(c)], s_scr[:, cols(c)]) + dh_ref[:, cols(c)]
            out_ref[cols(c), :] = dx.T


def unpack_att(total, rows, width, vectors):
    blocks = width // LANES
    grad = jnp.concatenate([total[c * rows : (c + 1) * rows] for c in range(blocks)], axis=1)
    return grad, total[blocks * rows : blocks * rows + vectors]


def state_kernel(info, got_ref, ma_ref, mb_ref, ga_ref, gb_ref, sa_ref, sb_ref, spread_ref, state_ref, vec_ref):
    first, width = ma_ref.shape
    rows = first + mb_ref.shape[0]
    total = got_ref[0].astype(f32)
    for index in range(1, got_ref.shape[0]):
        total += got_ref[index].astype(f32)
    if got_ref.shape[2] == width:
        grad, vec_ref[...] = total[:rows], total[rows : rows + vec_ref.shape[0]]
    else:
        grad, vec_ref[...] = unpack_att(total, rows, width, vec_ref.shape[0])
    ga_ref[...] = grad[:first]
    gb_ref[...] = grad[first:]
    state = grad + momentum_decay * jnp.concatenate([ma_ref[...], mb_ref[...]], axis=0)
    sa_ref[...] = state[:first]
    sb_ref[...] = state[first:]
    state_ref[...] = state
    if got_ref.shape[2] == width:
        ours = info[0] == 0
        high, low = state[:first].astype(bf16), state[first:].astype(bf16)
        spread_ref[0] = jnp.where(ours, high, low)
        spread_ref[1] = jnp.where(ours, low, high)
    else:
        for index in range(spread_ref.shape[0]):
            spread_ref[index] = state.astype(bf16)


def store_parts(x, left_ref, right_ref):
    width = x.shape[0]
    high, low = split_parts(x)
    left_ref[:, :width] = high
    left_ref[:, width : 2 * width] = high
    left_ref[:, 2 * width :] = low
    right_ref[:, :width] = high
    right_ref[:, width : 2 * width] = low
    right_ref[:, 2 * width :] = high


def symmetric(left_ref, right_ref, out_ref):
    width = out_ref.shape[0]
    cut = (width // 256) * 256
    if cut in (0, width):
        out_ref[...] = nt(left_ref[...], right_ref[...])
        return
    made = nt(left_ref[...], right_ref[:cut, :])
    out_ref[:, :cut] = made
    out_ref[:cut, cut:] = made[cut:, :].T
    out_ref[cut:, cut:] = nt(left_ref[cut:, :], right_ref[cut:, :])


def newton_kernel(info, own_ref, other_ref, pool_ref, moved_ref, out_ref, whole, gram, poly, pa, pb, sa, sb):
    width = own_ref.shape[-1]
    eye = (
        lax.broadcasted_iota(jnp.int32, (width, width), 0)
        == lax.broadcasted_iota(jnp.int32, (width, width), 1)
    ).astype(f32)
    first = jnp.zeros((width, width), f32)
    for ref in (own_ref, other_ref):
        place = lax.broadcasted_iota(jnp.int32, ref.shape[1:], 0)
        mine = (place < info[1]) == (info[0] == 0)
        part = jnp.concatenate(
            [jnp.where(mine, ref[index].astype(f32), 0.0) for index in range(ref.shape[0])], axis=0
        ).astype(bf16)
        first += tn(part, part)
    second = tn(pool_ref[...], pool_ref[...]) + tn(moved_ref[...], moved_ref[...])
    for index, made in enumerate((first, second)):
        norm = lax.rsqrt(jnp.sum(made * eye) + norm_eps)
        out_ref[index, width:, :] = jnp.full((8, width), norm, f32)
        gram[index] = made * (norm * norm)
        whole[index] = eye

    def turn(step, carry):
        for k in range(2):
            store_parts(gram[k], sa.at[k], sb.at[k])
        for k in range(2):
            symmetric(sa.at[k], sb.at[k], poly.at[k])
        for k in range(2):
            made = newton_a * eye + newton_b * gram[k] + newton_c * poly[k]
            store_parts(made, pa.at[k], pb.at[k])
        for k in range(2):
            symmetric(pa.at[k], sb.at[k], poly.at[k])
        for k in range(2):
            store_parts(whole[k], sa.at[k], sb.at[k])
        for k in range(2):
            symmetric(pa.at[k], sb.at[k], whole.at[k])

        @pl.when(step < 4)
        def _():
            for k in range(2):
                store_parts(poly[k], sa.at[k], sb.at[k])
            for k in range(2):
                symmetric(sa.at[k], pb.at[k], gram.at[k])

        return carry

    lax.fori_loop(0, 5, turn, 0)
    for index in range(2):
        out_ref[index, :width, :] = whole[index]


def update_kernel(wide, info, mine_ref, theirs_ref, sa_ref, sb_ref, *refs):
    ours = info[0] == 0
    width = mine_ref.shape[2]
    for pair, state_ref in enumerate((sa_ref, sb_ref)):
        low = 0
        for side in range(2):
            w_ref, u_ref = refs[2 * pair + side], refs[4 + 2 * pair + side]
            high = low + w_ref.shape[0]
            pick = ours if side == 0 else jnp.logical_not(ours)
            whole = jnp.where(pick, mine_ref[pair, :width, :], theirs_ref[pair, :width, :])
            norm = jnp.where(
                pick, mine_ref[pair, width : width + 1, :], theirs_ref[pair, width : width + 1, :]
            )
            sh, sl = split_parts(state_ref[low:high, :] * norm)
            ph, pl_ = split_parts(whole)
            ortho = nt(sh, ph) + (nt(sl, ph) + nt(sh, pl_))
            rate = matrix_rate * 0.2 * math.sqrt(wide[2 * pair + side])
            u_ref[...] = w_ref[...] - rate * ortho
            low = high


def fixed(shape):
    return pl.BlockSpec(shape, lambda i, info: (0,) * len(shape))


ANY = pl.BlockSpec(memory_space=pl.ANY)


def params(grid=True):
    return pltpu.CompilerParams(
        dimension_semantics=("arbitrary",) if grid else None, vmem_limit_bytes=60 * 1024 * 1024
    )


def shape_of(shape, dtype):
    return jax.ShapeDtypeStruct(shape, dtype)


def cost(flops, read):
    return pl.CostEstimate(flops=int(flops), bytes_accessed=int(read), transcendentals=0)


def small_call(kernel, outs, name, scalars=0, scratch=()):
    vmem = pl.BlockSpec(memory_space=pltpu.VMEM)
    smem = pl.BlockSpec(memory_space=pltpu.SMEM)

    def call(*args):
        return pl.pallas_call(
            kernel,
            in_specs=[smem] * scalars + [vmem] * (len(args) - scalars),
            out_specs=[vmem] * len(outs),
            out_shape=[shape_of(*out) for out in outs],
            scratch_shapes=scratch,
            compiler_params=params(False),
            name=name,
        )(*args)

    return call


def group_specs(width, ff, start):
    heads = width // HEAD_DIM
    lanes = GROUP * SEQ
    deep = lambda i, info: (start + i, 0, 0)
    return (
        pl.BlockSpec((lanes, width), lambda i, info: (start + i, 0)),
        pl.BlockSpec((None, 3 * width, lanes), deep),
        pl.BlockSpec((None, GROUP * heads * SEQ, SEQ), deep),
        pl.BlockSpec((None, width, lanes), deep),
        pl.BlockSpec((None, ff, lanes), deep),
    )


def grid_call(kernel, info, start, stop, ins, outs, scratch, name, flops, before=()):
    return pl.pallas_call(
        kernel,
        grid_spec=pltpu.PrefetchScalarGridSpec(
            num_scalar_prefetch=1,
            grid=(stop - start,),
            in_specs=[spec or fixed(array.shape) for spec, array in ins] + [ANY] * len(before),
            out_specs=[spec or fixed(shape) for spec, shape, _ in outs],
            scratch_shapes=[pltpu.VMEM(*one) for one in scratch],
        ),
        out_shape=[shape_of(shape, dtype) for _, shape, dtype in outs],
        input_output_aliases={1 + len(ins) + i: i for i in range(len(before))},
        compiler_params=params(),
        cost_estimate=cost(flops * (stop - start), 4e6 * (stop - start)),
        name=name,
    )(info, *[array for _, array in ins], *before)


def order_ff(up_bias, par, half):
    parts = up_bias.reshape(half, 2, -1)
    return jnp.where(
        par == 0,
        jnp.concatenate([parts[:, 0], parts[:, 1]]),
        jnp.concatenate([parts[:, 1], parts[:, 0]]),
    ).reshape(-1)


def natural_ff(bias, half):
    return jnp.swapaxes(bias.reshape(2, half, -1), 0, 1).reshape(-1)


def spread_lanes(array):
    return jnp.broadcast_to(array[..., None], array.shape + (LANES,))


def body(
    block_in,
    out_grad,
    live_counts,
    qkv_weight,
    proj_weight,
    up_weight,
    down_weight,
    feature_vectors,
    up_bias,
    qkv_moment,
    proj_moment,
    up_moment,
    down_moment,
):
    devices = lax.axis_size("dp")
    half = devices // 2
    par = (lax.axis_index("dp") % 2).astype(jnp.int32)
    width = block_in.shape[1]
    groups = block_in.shape[0] // (GROUP * SEQ)
    ff = up_bias.shape[0]
    blocks = width // LANES
    turned = [w.T for w in (qkv_weight, proj_weight, up_weight, down_weight)]
    wq_s, wp_s, wu_s, wd_s = turned
    mq_s, mp_s, mu_s, md_s = [m.T for m in (qkv_moment, proj_moment, up_moment, down_moment)]
    cq, cp, cu, cd = (w.shape[0] for w in turned)
    pairs = [(i, i ^ 1) for i in range(devices)]
    planes = [[2 * i + c for i in range(half)] for c in range(2)]
    info = jnp.stack([live_counts[0], par])
    vec = spread_lanes(feature_vectors)
    ub = spread_lanes(order_ff(up_bias, par, half))

    def exchange(x):
        return lax.all_to_all(x, "dp", 0, 0, axis_index_groups=planes, tiled=True)

    def swap(x):
        return lax.ppermute(x, "dp", pairs)

    def after(x, *others):
        return lax.optimization_barrier((x,) + others)[0]

    first, second = small_call(
        prep_kernel,
        [((half, cq, width), bf16), ((half, -(-(cu + cd + cp) // 16) * 16, width), bf16)],
        "prep",
    )(wq_s, wp_s, wu_s, wd_s)
    lanes = GROUP * SEQ
    heads = width // HEAD_DIM
    tokens, qkv_spec, att_spec, deep_spec, ff_spec = group_specs(width, ff, 0)
    wide = (groups, width, lanes)
    z1 = grid_call(
        normal_kernel, info, 0, groups, [(tokens, block_in), (None, vec)], [(deep_spec, wide, bf16)], [],
        "normal", 1e9,
    )[0]
    wq_own = after(exchange(first), z1)
    wq_other = swap(wq_own)
    rest_own = exchange(after(second, wq_own))

    def attend(start, stop, weights, before=()):
        _, qkv_at, att_at, deep_at, _ = group_specs(width, ff, start)
        fresh = start == 0
        return grid_call(
            functools.partial(attend_kernel, start), info, start, stop,
            [(deep_at, z1), (None, vec)] + [(None, w) for w in weights],
            [
                (qkv_at, (groups, 3 * width, lanes), bf16),
                (att_at, (groups, GROUP * heads * SEQ, SEQ), bf16),
                (deep_at, wide, bf16),
            ] + [(None, (3 * width, width), bf16)] * fresh,
            [
                ((3 * width, lanes), bf16),
                ((GROUP * heads, SEQ, SEQ), f32),
                ((GROUP * heads, SEQ, SEQ), bf16),
            ] + [((3 * width, width), f32)] * fresh,
            "attend", 4e9, before,
        )

    early = groups - 2 if groups > 2 else groups
    qkv, att, attn, wq = attend(0, early, (wq_own, wq_other))
    rest_own = after(rest_own, attn)
    rest_other = swap(rest_own)
    if early < groups:
        qkv, att, attn = attend(early, groups, (wq,), (qkv, att, attn))

    block = 256
    rows_b = 2 * cu + 4 + ff // width
    h1, act, dh, gp, wpn, wdn, keep_b, send_b = grid_call(
        mlp_kernel, info, 0, groups,
        [(tokens, block_in), (tokens, out_grad), (deep_spec, attn)]
        + [(None, array) for array in (rest_own, rest_other, vec, ub)],
        [
            (deep_spec, wide, f32),
            (ff_spec, (groups, ff, lanes), bf16),
            (deep_spec, wide, f32),
            (None, (width, width), f32),
            (None, (width, width), bf16),
            (None, (width, ff), bf16),
            (None, (half, rows_b, width), f32),
            (None, (half, rows_b, width), bf16),
        ],
        [
            ((width, ff), bf16),
            ((width, width), bf16),
            ((ff, width), bf16),
            ((ff, width), bf16),
            ((ff, width), f32),
            ((ff, width), f32),
            ((4, width, LANES), f32),
            ((ff, LANES), f32),
            ((width, lanes), f32),
            ((width, lanes), bf16),
            ((width, lanes), bf16),
            ((ff, lanes), bf16),
            ((ff, lanes), bf16),
            ((width, lanes), bf16),
            ((1, lanes), f32),
            ((ff, width), f32),
            ((2, block, lanes), f32),
            ((2, block, lanes), f32),
        ],
        "mlp", 10e9,
    )

    def back(start, stop, before=(), info=info):
        _, qkv_at, att_at, deep_at, _ = group_specs(width, ff, start)
        last = stop == groups
        rows = -(-(blocks * (cq + cp) + 4 * blocks) // 16) * 16
        totals = [(3 * width, width), (3, width, LANES)]
        scratch = [
            ((width, lanes), bf16),
            ((3 * width, lanes), bf16),
            ((GROUP * heads, SEQ, SEQ), f32),
            ((GROUP * heads, SEQ, SEQ), bf16),
        ]
        ins = [
            (deep_at, z1), (qkv_at, qkv), (att_at, att), (deep_at, dh),
            (None, wpn), (None, wq), (None, gp), (None, feature_vectors),
        ]
        outs = [(qkv_at, (groups, 3 * width, lanes), bf16)]
        if last:
            outs += [(None, (half, rows, LANES), f32), (None, (half, rows, LANES), bf16)]
            scratch = [(shape, f32) for shape in totals + [(rows, LANES)]] + scratch
        else:
            outs += [(None, shape, f32) for shape in totals]
        kernel = functools.partial(back_kernel, start, last)
        if not before:
            return grid_call(kernel, info, start, stop, ins, outs, scratch, "back", 6e9)
        ins += [(None, array) for array in before[1:]]
        return grid_call(kernel, info, start, stop, ins, outs, scratch, "back", 6e9, before[:1])

    def out_part(start, stop, info, before=()):
        tokens, _, _, deep_at, ff_at = group_specs(width, ff, start)
        return grid_call(
            functools.partial(out_kernel, start), info, start, stop,
            [(deep_at, h1), (ff_at, act), (None, wdn), (None, vec)],
            [(tokens, block_in.shape, f32)], [], "out", 1.5e9, before,
        )

    def input_part(start, stop, dqkv, info, before=()):
        tokens, qkv_at, _, deep_at, _ = group_specs(width, ff, start)
        return grid_call(
            functools.partial(input_kernel, start), info, start, stop,
            [(tokens, block_in), (qkv_at, dqkv), (deep_at, dh), (None, wq), (None, vec)],
            [(tokens, block_in.shape, f32)],
            [((width, 3 * width), bf16), ((1, lanes), f32), ((width, lanes), f32)], "input", 2e9, before,
        )

    def fold(keep, received):
        return (keep + received.astype(f32)).astype(bf16)

    def sums(got, moment_a, moment_b, vectors, spread, name):
        rows = moment_a.shape[0] + moment_b.shape[0]
        return small_call(
            state_kernel,
            [
                (moment_a.shape, f32), (moment_b.shape, f32), (moment_a.shape, f32), (moment_b.shape, f32),
                (spread, bf16), ((rows, width), f32), (vectors, f32),
            ],
            name + "_state",
            scalars=1,
        )(par.reshape(1), got, moment_a, moment_b)

    swapped = swap(send_b)
    one = 1 if groups > 2 else groups
    done = back(0, one)
    summed_b = fold(keep_b, after(swapped, done[1]))
    got_b = exchange(summed_b)
    if one < groups:
        done = back(one, groups, done, after(info, summed_b))
    dqkv, keep_a, send_a = done
    send_a, got_b = lax.optimization_barrier((send_a, got_b))
    summed_a = fold(keep_a, swap(send_a))
    got_a = exchange(summed_a)
    gate = after(info, summed_a)
    gu, gd, su, sd, spread_b, state_b, vector_b = sums(
        after(got_b, summed_a), mu_s, md_s, (4 + ff // width, width), (2, cu, width), "mlp"
    )

    bits = [1 << k for k in range(1, devices.bit_length() - 1)][::-1]

    def gather_step(pool, bit):
        return lax.ppermute(pool, "dp", [(i, i ^ bit) for i in range(devices)])

    def joined(pool, moved):
        return jnp.concatenate([pool, moved], axis=0)

    mid = groups // 2
    pool = joined(spread_b[0], swap(spread_b[1]))
    moved = gather_step(pool, bits[0])
    out = out_part(0, mid, after(gate, pool))
    for bit in bits[1:-2]:
        pool = joined(pool, after(moved, out[0]))
        moved = gather_step(pool, bit)
    out = out_part(mid, groups, after(gate, pool), out)
    got_a = after(got_a, out[0])
    gq, gpr, sq, sp, spread_a, state_a, vector_a = sums(
        got_a, mq_s, mp_s, (4 * blocks, LANES), (half, cq + cp, width), "att"
    )
    own_a = exchange(spread_a)
    pool = joined(pool, after(moved, spread_a))
    moved = gather_step(pool, bits[-2])
    dx = input_part(0, mid, dqkv, after(info, pool))
    pool = joined(pool, after(moved, dx[0]))
    moved = gather_step(pool, bits[-1])
    dx = input_part(mid, groups, dqkv, after(info, pool), dx)
    own_a = after(own_a, dx[0])
    other_a = swap(own_a)
    square = pltpu.VMEM((2, width, width), f32)
    parts = pltpu.VMEM((2, width, 3 * width), bf16)
    mine = small_call(
        newton_kernel,
        [((2, width + 8, width), f32)],
        "newton",
        scalars=1,
        scratch=[square, square, square, parts, parts, parts, parts],
    )(jnp.stack([par, jnp.full((), cq, jnp.int32)]), own_a, other_a, pool, moved)[0]
    uq, up, uu, ud = small_call(
        functools.partial(update_kernel, tuple(w.shape[0] * devices for w in turned)),
        [(w.shape, f32) for w in turned],
        "update",
        scalars=1,
    )(par.reshape(1), mine, swap(mine), state_a, state_b, *turned)
    out, dx = out[0], dx[0]

    vector_grad = jnp.concatenate([vector_a.reshape(4, width), vector_b[:4]], axis=0)
    bias_grad = natural_ff(vector_b[4:].reshape(ff), half)

    def normalized_step(param, gradient):
        return param - vector_rate * gradient * lax.rsqrt(
            jnp.mean(gradient * gradient, axis=-1, keepdims=True) + norm_eps
        )

    return (
        out, dx, gq.T, gpr.T, gu.T, gd.T, vector_grad, bias_grad, uq.T, up.T, uu.T, ud.T,
        sq.T, sp.T, su.T, sd.T,
        normalized_step(feature_vectors, vector_grad),
        normalized_step(up_bias, bias_grad),
    )


def solution(mesh):
    rows, columns, whole = P("dp", None), P(None, "dp"), P()
    return jax.shard_map(
        body,
        mesh=mesh,
        in_specs=(rows, rows, P("dp")) + (columns,) * 4 + (whole,) * 2 + (columns,) * 4,
        out_specs=(rows, rows) + (columns,) * 4 + (whole,) * 2 + (columns,) * 8 + (whole,) * 2,
        check_vma=False,
    )
```

```python
import functools
import math

import jax
import jax.numpy as jnp
from jax import lax
from jax.experimental import pallas as pl
from jax.experimental.pallas import tpu as pltpu
from jax.sharding import PartitionSpec as P

HEAD_DIM = 64
SEQ = 256
GROUP = 2
LANES = 128

norm_eps = 1e-06
newton_a = 3.4445
newton_b = -4.775
newton_c = 2.0315
momentum_decay = 0.9
matrix_rate = 0.15
vector_rate = 0.2

f32 = jnp.float32
bf16 = jnp.bfloat16


def nn(a, b):
    return lax.dot_general(a, b, (((1,), (0,)), ((), ())), preferred_element_type=f32)


def nt(a, b):
    return lax.dot_general(a, b, (((1,), (1,)), ((), ())), preferred_element_type=f32)


def tn(a, b):
    return lax.dot_general(a, b, (((0,), (0,)), ((), ())), preferred_element_type=f32)


def cols(index):
    return slice(index * LANES, (index + 1) * LANES)


def norm_parts(chunk):
    width = chunk.shape[0]
    center = chunk - jnp.sum(chunk, axis=0, keepdims=True) * (1.0 / width)
    scale = lax.rsqrt(jnp.sum(center * center, axis=0, keepdims=True) * (1.0 / width) + norm_eps)
    return center * scale, scale


def norm_back(inner, normed, scale):
    width = inner.shape[0]
    mean = jnp.sum(inner, axis=0, keepdims=True) * (1.0 / width)
    cross = jnp.sum(inner * normed, axis=0, keepdims=True) * (1.0 / width)
    return scale * (inner - mean - normed * cross)


def split_parts(x):
    high = x.astype(bf16)
    return high, (x - high.astype(f32)).astype(bf16)


def shard_rows(par, shard, own_ref, other_ref, first, count):
    span = slice(first, first + count)
    return jnp.where(par == shard % 2, own_ref[shard // 2, span, :], other_ref[shard // 2, span, :])


def lane_rows(acc):
    return [jnp.sum(acc[cols(c), :].T, axis=0, keepdims=True) for c in range(acc.shape[0] // LANES)]


def wide_rows(acc, width):
    rows = lane_rows(acc)
    per = width // LANES
    return [jnp.concatenate(rows[i : i + per], axis=1) for i in range(0, len(rows), per)]


def rounded(x):
    return x.astype(bf16).astype(f32)


def prep_kernel(wq_ref, wp_ref, wu_ref, wd_ref, first_ref, second_ref):
    first = wq_ref[...].astype(bf16)
    second = jnp.concatenate([wu_ref[...], wd_ref[...], wp_ref[...]], axis=0).astype(bf16)
    for index in range(first_ref.shape[0]):
        first_ref[index] = first
        second_ref[index, : second.shape[0], :] = second
        second_ref[index, second.shape[0] :, :] = jnp.zeros_like(second_ref[index, second.shape[0] :, :])


def normal_kernel(info, x_ref, vec_ref, z_ref):
    @pl.when(pl.program_id(0) * GROUP < info[0])
    def _():
        for c in range(z_ref.shape[1] // LANES):
            normed, _ = norm_parts(x_ref[cols(c), :].astype(f32).T)
            z_ref[:, cols(c)] = (normed * vec_ref[0] + vec_ref[1]).astype(bf16)


def attend_kernel(start, info, z_ref, vec_ref, *refs):
    if start == 0:
        own_ref, other_ref, qkv_ref, att_ref, out_ref, wq_ref, qkv_scr, s_scr, p_scr, stage = refs
    else:
        wq_ref, _, _, _, qkv_ref, att_ref, out_ref, qkv_scr, s_scr, p_scr = refs
    width, lanes = z_ref.shape
    heads = width // HEAD_DIM
    group = start + pl.program_id(0)

    if start == 0:

        @pl.when(pl.program_id(0) == 0)
        def _():
            count = own_ref.shape[1]
            for shard in range(2 * own_ref.shape[0]):
                rows = shard_rows(info[1], shard, own_ref, other_ref, 0, count)
                stage[shard * count : (shard + 1) * count, :] = rows.astype(f32)
            wq_ref[...] = stage[...].astype(bf16)

    @pl.when(group * GROUP < info[0])
    def _():
        for part in range(3):
            rows = slice(part * width, (part + 1) * width)
            made = nn(wq_ref[rows, :], z_ref[...])
            for c in range(lanes // LANES):
                piece = made[:, cols(c)]
                if part == 0:
                    piece = (piece + vec_ref[2]) * (1.0 / math.sqrt(HEAD_DIM))
                elif part == 2:
                    piece = piece + vec_ref[3]
                piece = piece.astype(bf16)
                qkv_scr[rows, cols(c)] = piece
                qkv_ref[rows, cols(c)] = piece
        for image in range(lanes // SEQ):
            span = slice(image * SEQ, (image + 1) * SEQ)
            for head in range(heads):
                low = head * HEAD_DIM
                query = qkv_scr[low : low + HEAD_DIM, span]
                keys = qkv_scr[width + low : width + low + HEAD_DIM, span]
                s_scr[image * heads + head] = tn(keys, query)
        for image in range(lanes // SEQ):
            span = slice(image * SEQ, (image + 1) * SEQ)
            for head in range(heads):
                low = head * HEAD_DIM
                slot = image * heads + head
                for c in range(SEQ // LANES):
                    scores = s_scr[slot, :, cols(c)]
                    top = jnp.max(scores, axis=0, keepdims=True)
                    raised = jnp.exp(scores - top)
                    total = jnp.sum(raised, axis=0, keepdims=True)
                    attend = (raised * (1.0 / total)).astype(bf16)
                    p_scr[slot, :, cols(c)] = attend
                    att_ref[slot * SEQ : (slot + 1) * SEQ, cols(c)] = attend
                values = qkv_scr[2 * width + low : 2 * width + low + HEAD_DIM, span]
                out_ref[low : low + HEAD_DIM, span] = nn(values, p_scr[slot]).astype(bf16)


def mlp_kernel(
    info, x_ref, cot_ref, att_ref, own_ref, other_ref, vec_ref, ub_ref,
    h_ref, act_ref, dh_ref, gp_ref, wpn_ref, wdn_ref, keep_ref, send_ref,
    wun_scr, wp_scr, wu_scr, wd_scr, gu_scr, gd_scr, rows_scr, bias_scr,
    n_scr, z_scr, m_scr, act_scr, du_scr, dhb_scr, s_scr, stage, u_scr, d_scr,
):
    width, lanes = z_scr.shape
    ff = wu_scr.shape[0]
    half = own_ref.shape[0]
    part = ff // (2 * half)
    step = pl.program_id(0)
    block = u_scr.shape[1]

    @pl.when(step == 0)
    def _():
        gp_ref[...] = jnp.zeros_like(gp_ref)
        rows_scr[...] = jnp.zeros_like(rows_scr)

        def clear(index, carry):
            rows = pl.ds(pl.multiple_of(index * LANES, LANES), LANES)
            gu_scr[rows, :] = jnp.zeros((LANES, width), f32)
            gd_scr[rows, :] = jnp.zeros((LANES, width), f32)
            bias_scr[rows, :] = jnp.zeros((LANES, LANES), f32)
            return carry

        lax.fori_loop(0, ff // LANES, clear, 0)
        count = width // (2 * half)
        for shard in range(2 * half):
            rows = shard_rows(info[1], shard, own_ref, other_ref, 2 * part, count)
            stage[shard * count : (shard + 1) * count, :] = rows.astype(f32)
        wp_scr[...] = stage[:width, :].astype(bf16)
        wpn_ref[...] = stage[:width, :].T.astype(bf16)
        for low, wide_scr in ((0, wu_scr), (part, wd_scr)):
            if part % 16 == 0:
                for side, ref in enumerate((own_ref, other_ref)):
                    for index in range(half):
                        at = (side * half + index) * part
                        wide_scr[at : at + part, :] = ref[index, low : low + part, :]
            else:
                for side, ref in enumerate((own_ref, other_ref)):
                    for index in range(half):
                        at = (side * half + index) * part
                        stage[at : at + part, :] = ref[index, low : low + part, :].astype(f32)
                wide_scr[...] = stage[...].astype(bf16)

        def turn(index, carry):
            rows = pl.ds(pl.multiple_of(index * block, block), block)
            wun_scr[:, rows] = wu_scr[rows, :].T
            wdn_ref[:, rows] = wd_scr[rows, :].T
            return carry

        lax.fori_loop(0, ff // block, turn, 0)

    @pl.when(step * GROUP < info[0])
    def _():
        made = nn(wp_scr[...], att_ref[...])
        total7 = jnp.zeros((width, LANES), f32)
        for c in range(lanes // LANES):
            chunk = x_ref[cols(c), :].astype(f32).T + made[:, cols(c)] + vec_ref[4]
            h_ref[:, cols(c)] = chunk
            normed, scale = norm_parts(chunk)
            n_scr[:, cols(c)] = normed
            s_scr[:, cols(c)] = scale
            z_scr[:, cols(c)] = (normed * vec_ref[5] + vec_ref[6]).astype(bf16)
            image = step * GROUP + c * LANES // SEQ
            cot = jnp.where(image < info[0], cot_ref[cols(c), :].astype(f32), 0.0).T
            m_scr[:, cols(c)] = cot.astype(bf16)
            total7 += cot
        rows_scr[3] += total7

        def first(c):
            rows = slice(c * block, (c + 1) * block)
            u_scr[c % 2] = nn(wu_scr[rows, :], z_scr[...])
            d_scr[c % 2] = nn(wd_scr[rows, :], m_scr[...])

        def second(c):
            for low in range(c * block, (c + 1) * block, 128):
                rows = slice(low, low + 128)
                here = slice(low - c * block, low - c * block + 128)
                bias = jnp.zeros((128, LANES), f32)
                for k in range(lanes // LANES):
                    u = u_scr[c % 2, here, cols(k)] + ub_ref[rows, :]
                    v = u * (1.0 / math.sqrt(2.0))
                    cdf = 0.5 + 0.5 * lax.erf(v)
                    act = (u * cdf).astype(bf16)
                    act_scr[rows, cols(k)] = act
                    act_ref[rows, cols(k)] = act
                    slope = cdf + (v * (1.0 / math.sqrt(math.pi))) * jnp.exp(-(v * v))
                    du = d_scr[c % 2, here, cols(k)] * slope
                    du_scr[rows, cols(k)] = du.astype(bf16)
                    bias += du
                bias_scr[rows, :] += bias

        def third(c):
            rows = slice(c * block, (c + 1) * block)
            gu_scr[rows, :] += nt(du_scr[rows, :], z_scr[...])
            gd_scr[rows, :] += nt(act_scr[rows, :], m_scr[...])

        chunks = ff // block
        first(0)
        for c in range(chunks):
            if c + 1 < chunks:
                first(c + 1)
            second(c)
            third(c)
        dz = nn(wun_scr[...], du_scr[...])
        total4 = jnp.zeros((width, LANES), f32)
        total5 = jnp.zeros((width, LANES), f32)
        total6 = jnp.zeros((width, LANES), f32)
        for c in range(lanes // LANES):
            piece = dz[:, cols(c)]
            normed = n_scr[:, cols(c)]
            dh = norm_back(piece * vec_ref[5], normed, s_scr[:, cols(c)]) + m_scr[:, cols(c)].astype(f32)
            dh_ref[:, cols(c)] = dh
            dhb_scr[:, cols(c)] = dh.astype(bf16)
            total4 += dh
            total5 += piece * normed
            total6 += piece
        rows_scr[0] += total4
        rows_scr[1] += total5
        rows_scr[2] += total6
        gp_ref[...] += nt(dhb_scr[...], att_ref[...])

    @pl.when(step == pl.num_programs(0) - 1)
    def _():
        vector = []
        for index in range(4):
            vector += wide_rows(rows_scr[index], width)
        hidden = wide_rows(bias_scr, width)
        side = len(hidden) // 2
        for index in range(len(hidden)):
            swapped = hidden[(index + side) % len(hidden)]
            vector.append(jnp.where(info[1] == 0, hidden[index], swapped))
        vector = jnp.concatenate(vector, axis=0)
        total = 2 * part + vector.shape[0]
        for index in range(half):
            keep_ref[index, :part, :] = gu_scr[index * part : (index + 1) * part, :]
            keep_ref[index, part : 2 * part, :] = gd_scr[index * part : (index + 1) * part, :]
            keep_ref[index, 2 * part : total, :] = rounded(vector)
            at = half * part + index * part
            if part % 16 == 0:
                send_ref[index, :part, :] = gu_scr[at : at + part, :].astype(bf16)
                send_ref[index, part : 2 * part, :] = gd_scr[at : at + part, :].astype(bf16)
                send_ref[index, 2 * part : total, :] = vector.astype(bf16)
            else:
                stage[:part, :] = gu_scr[at : at + part, :]
                stage[part : 2 * part, :] = gd_scr[at : at + part, :]
                stage[2 * part : total, :] = vector
                send_ref[index] = stage[: send_ref.shape[1], :].astype(bf16)


def out_kernel(start, info, h_ref, act_ref, wdn_ref, vec_ref, *refs):
    out_ref = refs[-1]
    group = start + pl.program_id(0)

    @pl.when(group * GROUP >= info[0])
    def _():
        out_ref[...] = jnp.zeros_like(out_ref)

    @pl.when(group * GROUP < info[0])
    def _():
        down = nn(wdn_ref[...], act_ref[...])
        for c in range(h_ref.shape[1] // LANES):
            image = group * GROUP + c * LANES // SEQ
            whole = down[:, cols(c)] + h_ref[:, cols(c)] + vec_ref[7]
            out_ref[cols(c), :] = jnp.where(image < info[0], whole, 0.0).T


def back_kernel(start, last, info, z_ref, qkv_ref, att_ref, dh_ref, wpn_ref, wq_ref, gp_ref, row_ref, *refs):
    if start:
        gq_in, rows_in, _ = refs[:3]
        refs = refs[3:]
    if last:
        dqkv_ref, keep_ref, send_ref, gq_ref, rows_ref, stage = refs[:6]
        refs = refs[6:]
    else:
        dqkv_ref, gq_ref, rows_ref = refs[:3]
        refs = refs[3:]
    da_scr, dqkv_scr, up_scr, ds_scr = refs
    width, lanes = z_ref.shape
    heads = width // HEAD_DIM
    step = pl.program_id(0)
    group = start + step

    @pl.when(step == 0)
    def _():
        if start == 0:
            gq_ref[...] = jnp.zeros_like(gq_ref)
            rows_ref[...] = jnp.zeros_like(rows_ref)
        else:
            gq_ref[...] = gq_in[...]
            rows_ref[...] = rows_in[...]

    @pl.when(group * GROUP < info[0])
    def _():
        da_scr[...] = nn(wpn_ref[...], dh_ref[...].astype(bf16)).astype(bf16)
        for image in range(lanes // SEQ):
            span = slice(image * SEQ, (image + 1) * SEQ)
            for head in range(heads):
                low = head * HEAD_DIM
                values = qkv_ref[2 * width + low : 2 * width + low + HEAD_DIM, span]
                up_scr[image * heads + head] = tn(values, da_scr[low : low + HEAD_DIM, span])
        for image in range(lanes // SEQ):
            span = slice(image * SEQ, (image + 1) * SEQ)
            for head in range(heads):
                low = head * HEAD_DIM
                high = low + HEAD_DIM
                slot = image * heads + head
                base = slot * SEQ
                for c in range(SEQ // LANES):
                    attend = att_ref[base : base + SEQ, cols(c)].astype(f32)
                    upstream = up_scr[slot, :, cols(c)]
                    delta = jnp.sum(attend * upstream, axis=0, keepdims=True)
                    ds_scr[slot, :, cols(c)] = (attend * (upstream - delta)).astype(bf16)
                query = qkv_ref[low:high, span]
                keys = qkv_ref[width + low : width + high, span]
                dscore = ds_scr[slot]
                dquery = nn(keys, dscore) * (1.0 / math.sqrt(HEAD_DIM))
                dkey = nt(query, dscore)
                dvalue = nt(da_scr[low:high, span], att_ref[base : base + SEQ, :])
                for part, value in enumerate((dquery, dkey, dvalue)):
                    rows = slice(part * width + low, part * width + high)
                    made = value.astype(bf16)
                    dqkv_scr[rows, span] = made
                    dqkv_ref[rows, span] = made
                    rows_ref[part, low:high, :] += value[:, :LANES] + value[:, LANES:]
        for part in range(3):
            rows = slice(part * width, (part + 1) * width)
            gq_ref[rows, :] += nt(dqkv_scr[rows, :], z_ref[...])

    if not last:
        return

    @pl.when(step == pl.num_programs(0) - 1)
    def _():
        count = 2 * keep_ref.shape[0]
        blocks = width // LANES
        sizes = (3 * width // count, width // count)
        rows = sum(sizes)
        stage[...] = jnp.zeros_like(stage)
        cross, plain = jnp.zeros((1, width), f32), jnp.zeros((1, width), f32)
        for part in range(3):
            rows_of = slice(part * width, (part + 1) * width)
            weight = wq_ref[rows_of, :].astype(f32)
            total = jnp.sum(rows_ref[part], axis=1, keepdims=True)
            cross += jnp.sum(weight * gq_ref[rows_of, :], axis=0, keepdims=True)
            plain += jnp.sum(weight * total, axis=0, keepdims=True)
        cross = (cross - row_ref[1:2, :] * plain) / row_ref[0:1, :]
        vector = [value[:, cols(c)] for value in (cross, plain) for c in range(blocks)]
        vector += lane_rows(rows_ref[0]) + lane_rows(rows_ref[2])
        for index, row in enumerate(vector):
            stage[blocks * rows + index : blocks * rows + index + 1, :] = rounded(row)
        for shard in range(count):
            for c in range(blocks):
                low = c * rows
                for piece, size in zip((gq_ref, gp_ref), sizes):
                    stage[low : low + size, :] = piece[shard * size : (shard + 1) * size, cols(c)]
                    low += size

            @pl.when(info[1] == shard % 2)
            def _():
                keep_ref[shard // 2] = stage[...]

            @pl.when(info[1] != shard % 2)
            def _():
                send_ref[shard // 2] = stage[...].astype(bf16)


def input_kernel(start, info, x_ref, dqkv_ref, dh_ref, wq_ref, vec_ref, *refs):
    out_ref, wqn_scr, s_scr, n_scr = refs[-4:]
    width, lanes = n_scr.shape
    step = pl.program_id(0)
    group = start + step

    @pl.when(step == 0)
    def _():
        for c in range(3):
            rows = slice(c * width, (c + 1) * width)
            wqn_scr[:, rows] = wq_ref[rows, :].T

    @pl.when(group * GROUP >= info[0])
    def _():
        out_ref[...] = jnp.zeros_like(out_ref)

    @pl.when(group * GROUP < info[0])
    def _():
        dz = nn(wqn_scr[...], dqkv_ref[...])
        for c in range(lanes // LANES):
            normed, scale = norm_parts(x_ref[cols(c), :].astype(f32).T)
            n_scr[:, cols(c)] = normed
            s_scr[:, cols(c)] = scale
        for c in range(lanes // LANES):
            inner = dz[:, cols(c)] * vec_ref[0]
            dx = norm_back(inner, n_scr[:, cols(c)], s_scr[:, cols(c)]) + dh_ref[:, cols(c)]
            out_ref[cols(c), :] = dx.T


def unpack_att(total, rows, width, vectors):
    blocks = width // LANES
    grad = jnp.concatenate([total[c * rows : (c + 1) * rows] for c in range(blocks)], axis=1)
    return grad, total[blocks * rows : blocks * rows + vectors]


def state_kernel(info, got_ref, ma_ref, mb_ref, ga_ref, gb_ref, sa_ref, sb_ref, spread_ref, state_ref, vec_ref):
    first, width = ma_ref.shape
    rows = first + mb_ref.shape[0]
    total = got_ref[0].astype(f32)
    for index in range(1, got_ref.shape[0]):
        total += got_ref[index].astype(f32)
    if got_ref.shape[2] == width:
        grad, vec_ref[...] = total[:rows], total[rows : rows + vec_ref.shape[0]]
    else:
        grad, vec_ref[...] = unpack_att(total, rows, width, vec_ref.shape[0])
    ga_ref[...] = grad[:first]
    gb_ref[...] = grad[first:]
    state = grad + momentum_decay * jnp.concatenate([ma_ref[...], mb_ref[...]], axis=0)
    sa_ref[...] = state[:first]
    sb_ref[...] = state[first:]
    state_ref[...] = state
    if got_ref.shape[2] == width:
        ours = info[0] == 0
        high, low = state[:first].astype(bf16), state[first:].astype(bf16)
        spread_ref[0] = jnp.where(ours, high, low)
        spread_ref[1] = jnp.where(ours, low, high)
    else:
        for index in range(spread_ref.shape[0]):
            spread_ref[index] = state.astype(bf16)


def store_parts(x, left_ref, right_ref):
    width = x.shape[0]
    high, low = split_parts(x)
    left_ref[:, :width] = high
    left_ref[:, width : 2 * width] = high
    left_ref[:, 2 * width :] = low
    right_ref[:, :width] = high
    right_ref[:, width : 2 * width] = low
    right_ref[:, 2 * width :] = high


def symmetric(left_ref, right_ref, out_ref):
    width = out_ref.shape[0]
    cut = (width // 256) * 256
    if cut in (0, width):
        out_ref[...] = nt(left_ref[...], right_ref[...])
        return
    made = nt(left_ref[...], right_ref[:cut, :])
    out_ref[:, :cut] = made
    out_ref[:cut, cut:] = made[cut:, :].T
    out_ref[cut:, cut:] = nt(left_ref[cut:, :], right_ref[cut:, :])


def newton_kernel(info, own_ref, other_ref, pool_ref, moved_ref, out_ref, whole, gram, poly, pa, pb, sa, sb):
    width = own_ref.shape[-1]
    eye = (
        lax.broadcasted_iota(jnp.int32, (width, width), 0)
        == lax.broadcasted_iota(jnp.int32, (width, width), 1)
    ).astype(f32)
    first = jnp.zeros((width, width), f32)
    for ref in (own_ref, other_ref):
        place = lax.broadcasted_iota(jnp.int32, ref.shape[1:], 0)
        mine = (place < info[1]) == (info[0] == 0)
        part = jnp.concatenate(
            [jnp.where(mine, ref[index].astype(f32), 0.0) for index in range(ref.shape[0])], axis=0
        ).astype(bf16)
        first += tn(part, part)
    second = tn(pool_ref[...], pool_ref[...]) + tn(moved_ref[...], moved_ref[...])
    for index, made in enumerate((first, second)):
        norm = lax.rsqrt(jnp.sum(made * eye) + norm_eps)
        out_ref[index, width:, :] = jnp.full((8, width), norm, f32)
        gram[index] = made * (norm * norm)
        whole[index] = eye

    def turn(step, carry):
        for k in range(2):
            store_parts(gram[k], sa.at[k], sb.at[k])
        for k in range(2):
            symmetric(sa.at[k], sb.at[k], poly.at[k])
        for k in range(2):
            made = newton_a * eye + newton_b * gram[k] + newton_c * poly[k]
            store_parts(made, pa.at[k], pb.at[k])
        for k in range(2):
            symmetric(pa.at[k], sb.at[k], poly.at[k])
        for k in range(2):
            store_parts(whole[k], sa.at[k], sb.at[k])
        for k in range(2):
            symmetric(pa.at[k], sb.at[k], whole.at[k])

        @pl.when(step < 4)
        def _():
            for k in range(2):
                store_parts(poly[k], sa.at[k], sb.at[k])
            for k in range(2):
                symmetric(sa.at[k], pb.at[k], gram.at[k])

        return carry

    lax.fori_loop(0, 5, turn, 0)
    for index in range(2):
        out_ref[index, :width, :] = whole[index]


def update_kernel(wide, info, mine_ref, theirs_ref, sa_ref, sb_ref, *refs):
    ours = info[0] == 0
    width = mine_ref.shape[2]
    for pair, state_ref in enumerate((sa_ref, sb_ref)):
        low = 0
        for side in range(2):
            w_ref, u_ref = refs[2 * pair + side], refs[4 + 2 * pair + side]
            high = low + w_ref.shape[0]
            pick = ours if side == 0 else jnp.logical_not(ours)
            whole = jnp.where(pick, mine_ref[pair, :width, :], theirs_ref[pair, :width, :])
            norm = jnp.where(
                pick, mine_ref[pair, width : width + 1, :], theirs_ref[pair, width : width + 1, :]
            )
            sh, sl = split_parts(state_ref[low:high, :] * norm)
            ph, pl_ = split_parts(whole)
            ortho = nt(sh, ph) + (nt(sl, ph) + nt(sh, pl_))
            rate = matrix_rate * 0.2 * math.sqrt(wide[2 * pair + side])
            u_ref[...] = w_ref[...] - rate * ortho
            low = high


def fixed(shape):
    return pl.BlockSpec(shape, lambda i, info: (0,) * len(shape))


ANY = pl.BlockSpec(memory_space=pl.ANY)


def params(grid=True):
    return pltpu.CompilerParams(
        dimension_semantics=("arbitrary",) if grid else None, vmem_limit_bytes=60 * 1024 * 1024
    )


def shape_of(shape, dtype):
    return jax.ShapeDtypeStruct(shape, dtype)


def cost(flops, read):
    return pl.CostEstimate(flops=int(flops), bytes_accessed=int(read), transcendentals=0)


def small_call(kernel, outs, name, scalars=0, scratch=()):
    vmem = pl.BlockSpec(memory_space=pltpu.VMEM)
    smem = pl.BlockSpec(memory_space=pltpu.SMEM)

    def call(*args):
        return pl.pallas_call(
            kernel,
            in_specs=[smem] * scalars + [vmem] * (len(args) - scalars),
            out_specs=[vmem] * len(outs),
            out_shape=[shape_of(*out) for out in outs],
            scratch_shapes=scratch,
            compiler_params=params(False),
            name=name,
        )(*args)

    return call


def group_specs(width, ff, start):
    heads = width // HEAD_DIM
    lanes = GROUP * SEQ
    deep = lambda i, info: (start + i, 0, 0)
    return (
        pl.BlockSpec((lanes, width), lambda i, info: (start + i, 0)),
        pl.BlockSpec((None, 3 * width, lanes), deep),
        pl.BlockSpec((None, GROUP * heads * SEQ, SEQ), deep),
        pl.BlockSpec((None, width, lanes), deep),
        pl.BlockSpec((None, ff, lanes), deep),
    )


def grid_call(kernel, info, start, stop, ins, outs, scratch, name, flops, before=()):
    return pl.pallas_call(
        kernel,
        grid_spec=pltpu.PrefetchScalarGridSpec(
            num_scalar_prefetch=1,
            grid=(stop - start,),
            in_specs=[spec or fixed(array.shape) for spec, array in ins] + [ANY] * len(before),
            out_specs=[spec or fixed(shape) for spec, shape, _ in outs],
            scratch_shapes=[pltpu.VMEM(*one) for one in scratch],
        ),
        out_shape=[shape_of(shape, dtype) for _, shape, dtype in outs],
        input_output_aliases={1 + len(ins) + i: i for i in range(len(before))},
        compiler_params=params(),
        cost_estimate=cost(flops * (stop - start), 4e6 * (stop - start)),
        name=name,
    )(info, *[array for _, array in ins], *before)


def order_ff(up_bias, par, half):
    parts = up_bias.reshape(half, 2, -1)
    return jnp.where(
        par == 0,
        jnp.concatenate([parts[:, 0], parts[:, 1]]),
        jnp.concatenate([parts[:, 1], parts[:, 0]]),
    ).reshape(-1)


def natural_ff(bias, half):
    return jnp.swapaxes(bias.reshape(2, half, -1), 0, 1).reshape(-1)


def spread_lanes(array):
    return jnp.broadcast_to(array[..., None], array.shape + (LANES,))


def body(
    block_in,
    out_grad,
    live_counts,
    qkv_weight,
    proj_weight,
    up_weight,
    down_weight,
    feature_vectors,
    up_bias,
    qkv_moment,
    proj_moment,
    up_moment,
    down_moment,
):
    devices = lax.axis_size("dp")
    half = devices // 2
    par = (lax.axis_index("dp") % 2).astype(jnp.int32)
    width = block_in.shape[1]
    groups = block_in.shape[0] // (GROUP * SEQ)
    ff = up_bias.shape[0]
    blocks = width // LANES
    turned = [w.T for w in (qkv_weight, proj_weight, up_weight, down_weight)]
    wq_s, wp_s, wu_s, wd_s = turned
    mq_s, mp_s, mu_s, md_s = [m.T for m in (qkv_moment, proj_moment, up_moment, down_moment)]
    cq, cp, cu, cd = (w.shape[0] for w in turned)
    pairs = [(i, i ^ 1) for i in range(devices)]
    planes = [[2 * i + c for i in range(half)] for c in range(2)]
    info = jnp.stack([live_counts[0], par])
    vec = spread_lanes(feature_vectors)
    ub = spread_lanes(order_ff(up_bias, par, half))

    def exchange(x):
        return lax.all_to_all(x, "dp", 0, 0, axis_index_groups=planes, tiled=True)

    def swap(x):
        return lax.ppermute(x, "dp", pairs)

    def after(x, *others):
        return lax.optimization_barrier((x,) + others)[0]

    first, second = small_call(
        prep_kernel,
        [((half, cq, width), bf16), ((half, -(-(cu + cd + cp) // 16) * 16, width), bf16)],
        "prep",
    )(wq_s, wp_s, wu_s, wd_s)
    lanes = GROUP * SEQ
    heads = width // HEAD_DIM
    tokens, qkv_spec, att_spec, deep_spec, ff_spec = group_specs(width, ff, 0)
    wide = (groups, width, lanes)
    z1 = grid_call(
        normal_kernel, info, 0, groups, [(tokens, block_in), (None, vec)], [(deep_spec, wide, bf16)], [],
        "normal", 1e9,
    )[0]
    wq_own = after(exchange(first), z1)
    wq_other = swap(wq_own)
    rest_own = exchange(after(second, wq_own))

    def attend(start, stop, weights, before=()):
        _, qkv_at, att_at, deep_at, _ = group_specs(width, ff, start)
        fresh = start == 0
        return grid_call(
            functools.partial(attend_kernel, start), info, start, stop,
            [(deep_at, z1), (None, vec)] + [(None, w) for w in weights],
            [
                (qkv_at, (groups, 3 * width, lanes), bf16),
                (att_at, (groups, GROUP * heads * SEQ, SEQ), bf16),
                (deep_at, wide, bf16),
            ] + [(None, (3 * width, width), bf16)] * fresh,
            [
                ((3 * width, lanes), bf16),
                ((GROUP * heads, SEQ, SEQ), f32),
                ((GROUP * heads, SEQ, SEQ), bf16),
            ] + [((3 * width, width), f32)] * fresh,
            "attend", 4e9, before,
        )

    early = groups
    qkv, att, attn, wq = attend(0, early, (wq_own, wq_other))
    rest_own = after(rest_own, attn)
    rest_other = swap(rest_own)
    if early < groups:
        qkv, att, attn = attend(early, groups, (wq,), (qkv, att, attn))

    block = 256
    rows_b = 2 * cu + 4 + ff // width
    h1, act, dh, gp, wpn, wdn, keep_b, send_b = grid_call(
        mlp_kernel, info, 0, groups,
        [(tokens, block_in), (tokens, out_grad), (deep_spec, attn)]
        + [(None, array) for array in (rest_own, rest_other, vec, ub)],
        [
            (deep_spec, wide, f32),
            (ff_spec, (groups, ff, lanes), bf16),
            (deep_spec, wide, f32),
            (None, (width, width), f32),
            (None, (width, width), bf16),
            (None, (width, ff), bf16),
            (None, (half, rows_b, width), f32),
            (None, (half, rows_b, width), bf16),
        ],
        [
            ((width, ff), bf16),
            ((width, width), bf16),
            ((ff, width), bf16),
            ((ff, width), bf16),
            ((ff, width), f32),
            ((ff, width), f32),
            ((4, width, LANES), f32),
            ((ff, LANES), f32),
            ((width, lanes), f32),
            ((width, lanes), bf16),
            ((width, lanes), bf16),
            ((ff, lanes), bf16),
            ((ff, lanes), bf16),
            ((width, lanes), bf16),
            ((1, lanes), f32),
            ((ff, width), f32),
            ((2, block, lanes), f32),
            ((2, block, lanes), f32),
        ],
        "mlp", 10e9,
    )

    def back(start, stop, before=(), info=info):
        _, qkv_at, att_at, deep_at, _ = group_specs(width, ff, start)
        last = stop == groups
        rows = -(-(blocks * (cq + cp) + 4 * blocks) // 16) * 16
        totals = [(3 * width, width), (3, width, LANES)]
        scratch = [
            ((width, lanes), bf16),
            ((3 * width, lanes), bf16),
            ((GROUP * heads, SEQ, SEQ), f32),
            ((GROUP * heads, SEQ, SEQ), bf16),
        ]
        ins = [
            (deep_at, z1), (qkv_at, qkv), (att_at, att), (deep_at, dh),
            (None, wpn), (None, wq), (None, gp), (None, feature_vectors),
        ]
        outs = [(qkv_at, (groups, 3 * width, lanes), bf16)]
        if last:
            outs += [(None, (half, rows, LANES), f32), (None, (half, rows, LANES), bf16)]
            scratch = [(shape, f32) for shape in totals + [(rows, LANES)]] + scratch
        else:
            outs += [(None, shape, f32) for shape in totals]
        kernel = functools.partial(back_kernel, start, last)
        if not before:
            return grid_call(kernel, info, start, stop, ins, outs, scratch, "back", 6e9)
        ins += [(None, array) for array in before[1:]]
        return grid_call(kernel, info, start, stop, ins, outs, scratch, "back", 6e9, before[:1])

    def out_part(start, stop, info, before=()):
        tokens, _, _, deep_at, ff_at = group_specs(width, ff, start)
        return grid_call(
            functools.partial(out_kernel, start), info, start, stop,
            [(deep_at, h1), (ff_at, act), (None, wdn), (None, vec)],
            [(tokens, block_in.shape, f32)], [], "out", 1.5e9, before,
        )

    def input_part(start, stop, dqkv, info, before=()):
        tokens, qkv_at, _, deep_at, _ = group_specs(width, ff, start)
        return grid_call(
            functools.partial(input_kernel, start), info, start, stop,
            [(tokens, block_in), (qkv_at, dqkv), (deep_at, dh), (None, wq), (None, vec)],
            [(tokens, block_in.shape, f32)],
            [((width, 3 * width), bf16), ((1, lanes), f32), ((width, lanes), f32)], "input", 2e9, before,
        )

    def fold(keep, received):
        return (keep + received.astype(f32)).astype(bf16)

    def sums(got, moment_a, moment_b, vectors, spread, name):
        rows = moment_a.shape[0] + moment_b.shape[0]
        return small_call(
            state_kernel,
            [
                (moment_a.shape, f32), (moment_b.shape, f32), (moment_a.shape, f32), (moment_b.shape, f32),
                (spread, bf16), ((rows, width), f32), (vectors, f32),
            ],
            name + "_state",
            scalars=1,
        )(par.reshape(1), got, moment_a, moment_b)

    swapped = swap(send_b)
    one = 1 if groups > 2 else groups
    done = back(0, one)
    summed_b = fold(keep_b, after(swapped, done[1]))
    got_b = exchange(summed_b)
    if one < groups:
        done = back(one, groups, done, after(info, summed_b))
    dqkv, keep_a, send_a = done
    send_a, got_b = lax.optimization_barrier((send_a, got_b))
    summed_a = fold(keep_a, swap(send_a))
    got_a = exchange(summed_a)
    gate = after(info, summed_a)
    gu, gd, su, sd, spread_b, state_b, vector_b = sums(
        after(got_b, summed_a), mu_s, md_s, (4 + ff // width, width), (2, cu, width), "mlp"
    )

    bits = [1 << k for k in range(1, devices.bit_length() - 1)][::-1]

    def gather_step(pool, bit):
        return lax.ppermute(pool, "dp", [(i, i ^ bit) for i in range(devices)])

    def joined(pool, moved):
        return jnp.concatenate([pool, moved], axis=0)

    mid = groups // 2
    pool = joined(spread_b[0], swap(spread_b[1]))
    moved = gather_step(pool, bits[0])
    out = out_part(0, mid, after(gate, pool))
    for bit in bits[1:-2]:
        pool = joined(pool, after(moved, out[0]))
        moved = gather_step(pool, bit)
    out = out_part(mid, groups, after(gate, pool), out)
    got_a = after(got_a, out[0])
    gq, gpr, sq, sp, spread_a, state_a, vector_a = sums(
        got_a, mq_s, mp_s, (4 * blocks, LANES), (half, cq + cp, width), "att"
    )
    own_a = exchange(spread_a)
    pool = joined(pool, after(moved, spread_a))
    moved = gather_step(pool, bits[-2])
    dx = input_part(0, mid, dqkv, after(info, pool))
    pool = joined(pool, after(moved, dx[0]))
    moved = gather_step(pool, bits[-1])
    dx = input_part(mid, groups, dqkv, after(info, pool), dx)
    own_a = after(own_a, dx[0])
    other_a = swap(own_a)
    square = pltpu.VMEM((2, width, width), f32)
    parts = pltpu.VMEM((2, width, 3 * width), bf16)
    mine = small_call(
        newton_kernel,
        [((2, width + 8, width), f32)],
        "newton",
        scalars=1,
        scratch=[square, square, square, parts, parts, parts, parts],
    )(jnp.stack([par, jnp.full((), cq, jnp.int32)]), own_a, other_a, pool, moved)[0]
    uq, up, uu, ud = small_call(
        functools.partial(update_kernel, tuple(w.shape[0] * devices for w in turned)),
        [(w.shape, f32) for w in turned],
        "update",
        scalars=1,
    )(par.reshape(1), mine, swap(mine), state_a, state_b, *turned)
    out, dx = out[0], dx[0]

    vector_grad = jnp.concatenate([vector_a.reshape(4, width), vector_b[:4]], axis=0)
    bias_grad = natural_ff(vector_b[4:].reshape(ff), half)

    def normalized_step(param, gradient):
        return param - vector_rate * gradient * lax.rsqrt(
            jnp.mean(gradient * gradient, axis=-1, keepdims=True) + norm_eps
        )

    return (
        out, dx, gq.T, gpr.T, gu.T, gd.T, vector_grad, bias_grad, uq.T, up.T, uu.T, ud.T,
        sq.T, sp.T, su.T, sd.T,
        normalized_step(feature_vectors, vector_grad),
        normalized_step(up_bias, bias_grad),
    )


def solution(mesh):
    rows, columns, whole = P("dp", None), P(None, "dp"), P()
    return jax.shard_map(
        body,
        mesh=mesh,
        in_specs=(rows, rows, P("dp")) + (columns,) * 4 + (whole,) * 2 + (columns,) * 4,
        out_specs=(rows, rows) + (columns,) * 4 + (whole,) * 2 + (columns,) * 8 + (whole,) * 2,
        check_vma=False,
    )
```

```python
import functools
import math

import jax
import jax.numpy as jnp
from jax import lax
from jax.experimental import pallas as pl
from jax.experimental.pallas import tpu as pltpu
from jax.sharding import PartitionSpec as P

HEAD_DIM = 64
SEQ = 256
GROUP = 2
LANES = 128

norm_eps = 1e-06
newton_a = 3.4445
newton_b = -4.775
newton_c = 2.0315
momentum_decay = 0.9
matrix_rate = 0.15
vector_rate = 0.2

f32 = jnp.float32
bf16 = jnp.bfloat16


def nn(a, b):
    return lax.dot_general(a, b, (((1,), (0,)), ((), ())), preferred_element_type=f32)


def nt(a, b):
    return lax.dot_general(a, b, (((1,), (1,)), ((), ())), preferred_element_type=f32)


def tn(a, b):
    return lax.dot_general(a, b, (((0,), (0,)), ((), ())), preferred_element_type=f32)


def cols(index):
    return slice(index * LANES, (index + 1) * LANES)


def norm_parts(chunk):
    width = chunk.shape[0]
    center = chunk - jnp.sum(chunk, axis=0, keepdims=True) * (1.0 / width)
    scale = lax.rsqrt(jnp.sum(center * center, axis=0, keepdims=True) * (1.0 / width) + norm_eps)
    return center * scale, scale


def norm_back(inner, normed, scale):
    width = inner.shape[0]
    mean = jnp.sum(inner, axis=0, keepdims=True) * (1.0 / width)
    cross = jnp.sum(inner * normed, axis=0, keepdims=True) * (1.0 / width)
    return scale * (inner - mean - normed * cross)


def split_parts(x):
    high = x.astype(bf16)
    return high, (x - high.astype(f32)).astype(bf16)


def shard_rows(par, shard, own_ref, other_ref, first, count):
    span = slice(first, first + count)
    return jnp.where(par == shard % 2, own_ref[shard // 2, span, :], other_ref[shard // 2, span, :])


def lane_rows(acc):
    return [jnp.sum(acc[cols(c), :].T, axis=0, keepdims=True) for c in range(acc.shape[0] // LANES)]


def wide_rows(acc, width):
    rows = lane_rows(acc)
    per = width // LANES
    return [jnp.concatenate(rows[i : i + per], axis=1) for i in range(0, len(rows), per)]


def rounded(x):
    return x.astype(bf16).astype(f32)


def prep_kernel(wq_ref, wp_ref, wu_ref, wd_ref, first_ref, second_ref):
    first = wq_ref[...].astype(bf16)
    second = jnp.concatenate([wu_ref[...], wd_ref[...], wp_ref[...]], axis=0).astype(bf16)
    for index in range(first_ref.shape[0]):
        first_ref[index] = first
        second_ref[index, : second.shape[0], :] = second
        second_ref[index, second.shape[0] :, :] = jnp.zeros_like(second_ref[index, second.shape[0] :, :])


def normal_kernel(info, x_ref, vec_ref, z_ref):
    @pl.when(pl.program_id(0) * GROUP < info[0])
    def _():
        for c in range(z_ref.shape[1] // LANES):
            normed, _ = norm_parts(x_ref[cols(c), :].astype(f32).T)
            z_ref[:, cols(c)] = (normed * vec_ref[0] + vec_ref[1]).astype(bf16)


def attend_kernel(start, info, z_ref, vec_ref, *refs):
    if start == 0:
        own_ref, other_ref, qkv_ref, att_ref, out_ref, wq_ref, qkv_scr, s_scr, p_scr, stage = refs
    else:
        wq_ref, _, _, _, qkv_ref, att_ref, out_ref, qkv_scr, s_scr, p_scr = refs
    width, lanes = z_ref.shape
    heads = width // HEAD_DIM
    group = start + pl.program_id(0)

    if start == 0:

        @pl.when(pl.program_id(0) == 0)
        def _():
            count = own_ref.shape[1]
            for shard in range(2 * own_ref.shape[0]):
                rows = shard_rows(info[1], shard, own_ref, other_ref, 0, count)
                stage[shard * count : (shard + 1) * count, :] = rows.astype(f32)
            wq_ref[...] = stage[...].astype(bf16)

    @pl.when(group * GROUP < info[0])
    def _():
        for part in range(3):
            rows = slice(part * width, (part + 1) * width)
            made = nn(wq_ref[rows, :], z_ref[...])
            for c in range(lanes // LANES):
                piece = made[:, cols(c)]
                if part == 0:
                    piece = (piece + vec_ref[2]) * (1.0 / math.sqrt(HEAD_DIM))
                elif part == 2:
                    piece = piece + vec_ref[3]
                piece = piece.astype(bf16)
                qkv_scr[rows, cols(c)] = piece
                qkv_ref[rows, cols(c)] = piece
        for image in range(lanes // SEQ):
            span = slice(image * SEQ, (image + 1) * SEQ)
            for head in range(heads):
                low = head * HEAD_DIM
                query = qkv_scr[low : low + HEAD_DIM, span]
                keys = qkv_scr[width + low : width + low + HEAD_DIM, span]
                s_scr[image * heads + head] = tn(keys, query)
        for image in range(lanes // SEQ):
            span = slice(image * SEQ, (image + 1) * SEQ)
            for head in range(heads):
                low = head * HEAD_DIM
                slot = image * heads + head
                for c in range(SEQ // LANES):
                    scores = s_scr[slot, :, cols(c)]
                    top = jnp.max(scores, axis=0, keepdims=True)
                    raised = jnp.exp(scores - top)
                    total = jnp.sum(raised, axis=0, keepdims=True)
                    attend = (raised * (1.0 / total)).astype(bf16)
                    p_scr[slot, :, cols(c)] = attend
                    att_ref[slot * SEQ : (slot + 1) * SEQ, cols(c)] = attend
                values = qkv_scr[2 * width + low : 2 * width + low + HEAD_DIM, span]
                out_ref[low : low + HEAD_DIM, span] = nn(values, p_scr[slot]).astype(bf16)


def mlp_kernel(
    info, x_ref, cot_ref, att_ref, own_ref, other_ref, vec_ref, ub_ref,
    h_ref, act_ref, dh_ref, gp_ref, wpn_ref, wdn_ref, keep_ref, send_ref,
    wun_scr, wp_scr, wu_scr, wd_scr, gu_scr, gd_scr, rows_scr, bias_scr,
    n_scr, z_scr, m_scr, act_scr, du_scr, dhb_scr, s_scr, stage, u_scr, d_scr,
):
    width, lanes = z_scr.shape
    ff = wu_scr.shape[0]
    half = own_ref.shape[0]
    part = ff // (2 * half)
    step = pl.program_id(0)
    block = u_scr.shape[1]

    @pl.when(step == 0)
    def _():
        gp_ref[...] = jnp.zeros_like(gp_ref)
        rows_scr[...] = jnp.zeros_like(rows_scr)

        def clear(index, carry):
            rows = pl.ds(pl.multiple_of(index * LANES, LANES), LANES)
            gu_scr[rows, :] = jnp.zeros((LANES, width), f32)
            gd_scr[rows, :] = jnp.zeros((LANES, width), f32)
            bias_scr[rows, :] = jnp.zeros((LANES, LANES), f32)
            return carry

        lax.fori_loop(0, ff // LANES, clear, 0)
        count = width // (2 * half)
        for shard in range(2 * half):
            rows = shard_rows(info[1], shard, own_ref, other_ref, 2 * part, count)
            stage[shard * count : (shard + 1) * count, :] = rows.astype(f32)
        wp_scr[...] = stage[:width, :].astype(bf16)
        wpn_ref[...] = stage[:width, :].T.astype(bf16)
        for low, wide_scr in ((0, wu_scr), (part, wd_scr)):
            if part % 16 == 0:
                for side, ref in enumerate((own_ref, other_ref)):
                    for index in range(half):
                        at = (side * half + index) * part
                        wide_scr[at : at + part, :] = ref[index, low : low + part, :]
            else:
                for side, ref in enumerate((own_ref, other_ref)):
                    for index in range(half):
                        at = (side * half + index) * part
                        stage[at : at + part, :] = ref[index, low : low + part, :].astype(f32)
                wide_scr[...] = stage[...].astype(bf16)

        def turn(index, carry):
            rows = pl.ds(pl.multiple_of(index * block, block), block)
            wun_scr[:, rows] = wu_scr[rows, :].T
            wdn_ref[:, rows] = wd_scr[rows, :].T
            return carry

        lax.fori_loop(0, ff // block, turn, 0)

    @pl.when(step * GROUP < info[0])
    def _():
        made = nn(wp_scr[...], att_ref[...])
        total7 = jnp.zeros((width, LANES), f32)
        for c in range(lanes // LANES):
            chunk = x_ref[cols(c), :].astype(f32).T + made[:, cols(c)] + vec_ref[4]
            h_ref[:, cols(c)] = chunk
            normed, scale = norm_parts(chunk)
            n_scr[:, cols(c)] = normed
            s_scr[:, cols(c)] = scale
            z_scr[:, cols(c)] = (normed * vec_ref[5] + vec_ref[6]).astype(bf16)
            image = step * GROUP + c * LANES // SEQ
            cot = jnp.where(image < info[0], cot_ref[cols(c), :].astype(f32), 0.0).T
            m_scr[:, cols(c)] = cot.astype(bf16)
            total7 += cot
        rows_scr[3] += total7

        def first(c):
            rows = slice(c * block, (c + 1) * block)
            u_scr[c % 2] = nn(wu_scr[rows, :], z_scr[...])
            d_scr[c % 2] = nn(wd_scr[rows, :], m_scr[...])

        def second(c):
            for low in range(c * block, (c + 1) * block, 128):
                rows = slice(low, low + 128)
                here = slice(low - c * block, low - c * block + 128)
                bias = jnp.zeros((128, LANES), f32)
                for k in range(lanes // LANES):
                    u = u_scr[c % 2, here, cols(k)] + ub_ref[rows, :]
                    v = u * (1.0 / math.sqrt(2.0))
                    cdf = 0.5 + 0.5 * lax.erf(v)
                    act = (u * cdf).astype(bf16)
                    act_scr[rows, cols(k)] = act
                    act_ref[rows, cols(k)] = act
                    slope = cdf + (v * (1.0 / math.sqrt(math.pi))) * jnp.exp(-(v * v))
                    du = d_scr[c % 2, here, cols(k)] * slope
                    du_scr[rows, cols(k)] = du.astype(bf16)
                    bias += du
                bias_scr[rows, :] += bias

        def third(c):
            rows = slice(c * block, (c + 1) * block)
            gu_scr[rows, :] += nt(du_scr[rows, :], z_scr[...])
            gd_scr[rows, :] += nt(act_scr[rows, :], m_scr[...])

        chunks = ff // block
        first(0)
        for c in range(chunks):
            if c + 1 < chunks:
                first(c + 1)
            second(c)
            third(c)
        dz = nn(wun_scr[...], du_scr[...])
        total4 = jnp.zeros((width, LANES), f32)
        total5 = jnp.zeros((width, LANES), f32)
        total6 = jnp.zeros((width, LANES), f32)
        for c in range(lanes // LANES):
            piece = dz[:, cols(c)]
            normed = n_scr[:, cols(c)]
            dh = norm_back(piece * vec_ref[5], normed, s_scr[:, cols(c)]) + m_scr[:, cols(c)].astype(f32)
            dh_ref[:, cols(c)] = dh
            dhb_scr[:, cols(c)] = dh.astype(bf16)
            total4 += dh
            total5 += piece * normed
            total6 += piece
        rows_scr[0] += total4
        rows_scr[1] += total5
        rows_scr[2] += total6
        gp_ref[...] += nt(dhb_scr[...], att_ref[...])

    @pl.when(step == pl.num_programs(0) - 1)
    def _():
        vector = []
        for index in range(4):
            vector += wide_rows(rows_scr[index], width)
        hidden = wide_rows(bias_scr, width)
        side = len(hidden) // 2
        for index in range(len(hidden)):
            swapped = hidden[(index + side) % len(hidden)]
            vector.append(jnp.where(info[1] == 0, hidden[index], swapped))
        vector = jnp.concatenate(vector, axis=0)
        total = 2 * part + vector.shape[0]
        for index in range(half):
            keep_ref[index, :part, :] = gu_scr[index * part : (index + 1) * part, :]
            keep_ref[index, part : 2 * part, :] = gd_scr[index * part : (index + 1) * part, :]
            keep_ref[index, 2 * part : total, :] = rounded(vector)
            at = half * part + index * part
            if part % 16 == 0:
                send_ref[index, :part, :] = gu_scr[at : at + part, :].astype(bf16)
                send_ref[index, part : 2 * part, :] = gd_scr[at : at + part, :].astype(bf16)
                send_ref[index, 2 * part : total, :] = vector.astype(bf16)
            else:
                stage[:part, :] = gu_scr[at : at + part, :]
                stage[part : 2 * part, :] = gd_scr[at : at + part, :]
                stage[2 * part : total, :] = vector
                send_ref[index] = stage[: send_ref.shape[1], :].astype(bf16)


def out_kernel(start, info, h_ref, act_ref, wdn_ref, vec_ref, *refs):
    out_ref = refs[-1]
    group = start + pl.program_id(0)

    @pl.when(group * GROUP >= info[0])
    def _():
        out_ref[...] = jnp.zeros_like(out_ref)

    @pl.when(group * GROUP < info[0])
    def _():
        down = nn(wdn_ref[...], act_ref[...])
        for c in range(h_ref.shape[1] // LANES):
            image = group * GROUP + c * LANES // SEQ
            whole = down[:, cols(c)] + h_ref[:, cols(c)] + vec_ref[7]
            out_ref[cols(c), :] = jnp.where(image < info[0], whole, 0.0).T


def back_kernel(start, last, info, z_ref, qkv_ref, att_ref, dh_ref, wpn_ref, wq_ref, gp_ref, row_ref, *refs):
    if start:
        gq_in, rows_in, _ = refs[:3]
        refs = refs[3:]
    if last:
        dqkv_ref, keep_ref, send_ref, gq_ref, rows_ref, stage = refs[:6]
        refs = refs[6:]
    else:
        dqkv_ref, gq_ref, rows_ref = refs[:3]
        refs = refs[3:]
    da_scr, dqkv_scr, up_scr, ds_scr = refs
    width, lanes = z_ref.shape
    heads = width // HEAD_DIM
    step = pl.program_id(0)
    group = start + step

    @pl.when(step == 0)
    def _():
        if start == 0:
            gq_ref[...] = jnp.zeros_like(gq_ref)
            rows_ref[...] = jnp.zeros_like(rows_ref)
        else:
            gq_ref[...] = gq_in[...]
            rows_ref[...] = rows_in[...]

    @pl.when(group * GROUP < info[0])
    def _():
        da_scr[...] = nn(wpn_ref[...], dh_ref[...].astype(bf16)).astype(bf16)
        for image in range(lanes // SEQ):
            span = slice(image * SEQ, (image + 1) * SEQ)
            for head in range(heads):
                low = head * HEAD_DIM
                values = qkv_ref[2 * width + low : 2 * width + low + HEAD_DIM, span]
                up_scr[image * heads + head] = tn(values, da_scr[low : low + HEAD_DIM, span])
        for image in range(lanes // SEQ):
            span = slice(image * SEQ, (image + 1) * SEQ)
            for head in range(heads):
                low = head * HEAD_DIM
                high = low + HEAD_DIM
                slot = image * heads + head
                base = slot * SEQ
                for c in range(SEQ // LANES):
                    attend = att_ref[base : base + SEQ, cols(c)].astype(f32)
                    upstream = up_scr[slot, :, cols(c)]
                    delta = jnp.sum(attend * upstream, axis=0, keepdims=True)
                    ds_scr[slot, :, cols(c)] = (attend * (upstream - delta)).astype(bf16)
                query = qkv_ref[low:high, span]
                keys = qkv_ref[width + low : width + high, span]
                dscore = ds_scr[slot]
                dquery = nn(keys, dscore) * (1.0 / math.sqrt(HEAD_DIM))
                dkey = nt(query, dscore)
                dvalue = nt(da_scr[low:high, span], att_ref[base : base + SEQ, :])
                for part, value in enumerate((dquery, dkey, dvalue)):
                    rows = slice(part * width + low, part * width + high)
                    made = value.astype(bf16)
                    dqkv_scr[rows, span] = made
                    dqkv_ref[rows, span] = made
                    rows_ref[part, low:high, :] += value[:, :LANES] + value[:, LANES:]
        for part in range(3):
            rows = slice(part * width, (part + 1) * width)
            gq_ref[rows, :] += nt(dqkv_scr[rows, :], z_ref[...])

    if not last:
        return

    @pl.when(step == pl.num_programs(0) - 1)
    def _():
        count = 2 * keep_ref.shape[0]
        blocks = width // LANES
        sizes = (3 * width // count, width // count)
        rows = sum(sizes)
        stage[...] = jnp.zeros_like(stage)
        cross, plain = jnp.zeros((1, width), f32), jnp.zeros((1, width), f32)
        for part in range(3):
            rows_of = slice(part * width, (part + 1) * width)
            weight = wq_ref[rows_of, :].astype(f32)
            total = jnp.sum(rows_ref[part], axis=1, keepdims=True)
            cross += jnp.sum(weight * gq_ref[rows_of, :], axis=0, keepdims=True)
            plain += jnp.sum(weight * total, axis=0, keepdims=True)
        cross = (cross - row_ref[1:2, :] * plain) / row_ref[0:1, :]
        vector = [value[:, cols(c)] for value in (cross, plain) for c in range(blocks)]
        vector += lane_rows(rows_ref[0]) + lane_rows(rows_ref[2])
        for index, row in enumerate(vector):
            stage[blocks * rows + index : blocks * rows + index + 1, :] = rounded(row)
        for shard in range(count):
            for c in range(blocks):
                low = c * rows
                for piece, size in zip((gq_ref, gp_ref), sizes):
                    stage[low : low + size, :] = piece[shard * size : (shard + 1) * size, cols(c)]
                    low += size

            @pl.when(info[1] == shard % 2)
            def _():
                keep_ref[shard // 2] = stage[...]

            @pl.when(info[1] != shard % 2)
            def _():
                send_ref[shard // 2] = stage[...].astype(bf16)


def input_kernel(start, info, x_ref, dqkv_ref, dh_ref, wq_ref, vec_ref, *refs):
    out_ref, wqn_scr, s_scr, n_scr = refs[-4:]
    width, lanes = n_scr.shape
    step = pl.program_id(0)
    group = start + step

    @pl.when(step == 0)
    def _():
        for c in range(3):
            rows = slice(c * width, (c + 1) * width)
            wqn_scr[:, rows] = wq_ref[rows, :].T

    @pl.when(group * GROUP >= info[0])
    def _():
        out_ref[...] = jnp.zeros_like(out_ref)

    @pl.when(group * GROUP < info[0])
    def _():
        dz = nn(wqn_scr[...], dqkv_ref[...])
        for c in range(lanes // LANES):
            normed, scale = norm_parts(x_ref[cols(c), :].astype(f32).T)
            n_scr[:, cols(c)] = normed
            s_scr[:, cols(c)] = scale
        for c in range(lanes // LANES):
            inner = dz[:, cols(c)] * vec_ref[0]
            dx = norm_back(inner, n_scr[:, cols(c)], s_scr[:, cols(c)]) + dh_ref[:, cols(c)]
            out_ref[cols(c), :] = dx.T


def unpack_att(total, rows, width, vectors):
    blocks = width // LANES
    grad = jnp.concatenate([total[c * rows : (c + 1) * rows] for c in range(blocks)], axis=1)
    return grad, total[blocks * rows : blocks * rows + vectors]


def state_kernel(info, got_ref, ma_ref, mb_ref, ga_ref, gb_ref, sa_ref, sb_ref, spread_ref, state_ref, vec_ref):
    first, width = ma_ref.shape
    rows = first + mb_ref.shape[0]
    total = got_ref[0].astype(f32)
    for index in range(1, got_ref.shape[0]):
        total += got_ref[index].astype(f32)
    if got_ref.shape[2] == width:
        grad, vec_ref[...] = total[:rows], total[rows : rows + vec_ref.shape[0]]
    else:
        grad, vec_ref[...] = unpack_att(total, rows, width, vec_ref.shape[0])
    ga_ref[...] = grad[:first]
    gb_ref[...] = grad[first:]
    state = grad + momentum_decay * jnp.concatenate([ma_ref[...], mb_ref[...]], axis=0)
    sa_ref[...] = state[:first]
    sb_ref[...] = state[first:]
    state_ref[...] = state
    if got_ref.shape[2] == width:
        ours = info[0] == 0
        high, low = state[:first].astype(bf16), state[first:].astype(bf16)
        spread_ref[0] = jnp.where(ours, high, low)
        spread_ref[1] = jnp.where(ours, low, high)
    else:
        for index in range(spread_ref.shape[0]):
            spread_ref[index] = state.astype(bf16)


def store_parts(x, left_ref, right_ref):
    width = x.shape[0]
    high, low = split_parts(x)
    left_ref[:, :width] = high
    left_ref[:, width : 2 * width] = high
    left_ref[:, 2 * width :] = low
    right_ref[:, :width] = high
    right_ref[:, width : 2 * width] = low
    right_ref[:, 2 * width :] = high


def symmetric(left_ref, right_ref, out_ref):
    width = out_ref.shape[0]
    cut = (width // 256) * 256
    if cut in (0, width):
        out_ref[...] = nt(left_ref[...], right_ref[...])
        return
    made = nt(left_ref[...], right_ref[:cut, :])
    out_ref[:, :cut] = made
    out_ref[:cut, cut:] = made[cut:, :].T
    out_ref[cut:, cut:] = nt(left_ref[cut:, :], right_ref[cut:, :])


def newton_kernel(
    info, own_ref, other_ref, pool_ref, moved_ref, mine_a, theirs_a, mine_b, theirs_b,
    mine_ref, send_ref, whole, gram, poly, pa, pb, sa, sb,
):
    width = own_ref.shape[-1]
    eye = (
        lax.broadcasted_iota(jnp.int32, (width, width), 0)
        == lax.broadcasted_iota(jnp.int32, (width, width), 1)
    ).astype(f32)
    first = jnp.zeros((width, width), f32)
    for ref in (own_ref, other_ref):
        place = lax.broadcasted_iota(jnp.int32, ref.shape[1:], 0)
        mine = (place < info[1]) == (info[0] == 0)
        part = jnp.concatenate(
            [jnp.where(mine, ref[index].astype(f32), 0.0) for index in range(ref.shape[0])], axis=0
        ).astype(bf16)
        first += tn(part, part)
    second = tn(pool_ref[...], pool_ref[...]) + tn(moved_ref[...], moved_ref[...])
    norms = []
    for index, made in enumerate((first, second)):
        norm = lax.rsqrt(jnp.sum(made * eye) + norm_eps)
        norms.append(norm)
        gram[index] = made * (norm * norm)
        whole[index] = eye

    def turn(step, carry):
        for k in range(2):
            store_parts(gram[k], sa.at[k], sb.at[k])
        for k in range(2):
            symmetric(sa.at[k], sb.at[k], poly.at[k])
        for k in range(2):
            made = newton_a * eye + newton_b * gram[k] + newton_c * poly[k]
            store_parts(made, pa.at[k], pb.at[k])
        for k in range(2):
            symmetric(pa.at[k], sb.at[k], poly.at[k])
        for k in range(2):
            store_parts(whole[k], sa.at[k], sb.at[k])
        for k in range(2):
            symmetric(pa.at[k], sb.at[k], whole.at[k])

        @pl.when(step < 4)
        def _():
            for k in range(2):
                store_parts(poly[k], sa.at[k], sb.at[k])
            for k in range(2):
                symmetric(sa.at[k], pb.at[k], gram.at[k])

        return carry

    lax.fori_loop(0, 5, turn, 0)
    low = 0
    for k, pair in enumerate(((mine_a, theirs_a), (mine_b, theirs_b))):
        ph, pl_ = split_parts(whole[k])
        high = low + pair[0].shape[0]
        for state_ref, to_ref in zip(pair, (mine_ref, send_ref)):
            sh, sl = split_parts(state_ref[...] * norms[k])
            to_ref[low:high, :] = nt(sh, ph) + (nt(sl, ph) + nt(sh, pl_))
        low = high


def update_kernel(wide, info, mine_ref, got_ref, *refs):
    low = 0
    for index, (w_ref, u_ref) in enumerate(zip(refs[:4], refs[4:])):
        high = low + w_ref.shape[0]
        ortho = jnp.where(info[0] == index % 2, mine_ref[low:high, :], got_ref[low:high, :])
        u_ref[...] = w_ref[...] - (matrix_rate * 0.2 * math.sqrt(wide[index])) * ortho
        low = high


def fixed(shape):
    return pl.BlockSpec(shape, lambda i, info: (0,) * len(shape))


ANY = pl.BlockSpec(memory_space=pl.ANY)


def params(grid=True):
    return pltpu.CompilerParams(
        dimension_semantics=("arbitrary",) if grid else None, vmem_limit_bytes=60 * 1024 * 1024
    )


def shape_of(shape, dtype):
    return jax.ShapeDtypeStruct(shape, dtype)


def cost(flops, read):
    return pl.CostEstimate(flops=int(flops), bytes_accessed=int(read), transcendentals=0)


def small_call(kernel, outs, name, scalars=0, scratch=()):
    vmem = pl.BlockSpec(memory_space=pltpu.VMEM)
    smem = pl.BlockSpec(memory_space=pltpu.SMEM)

    def call(*args):
        return pl.pallas_call(
            kernel,
            in_specs=[smem] * scalars + [vmem] * (len(args) - scalars),
            out_specs=[vmem] * len(outs),
            out_shape=[shape_of(*out) for out in outs],
            scratch_shapes=scratch,
            compiler_params=params(False),
            name=name,
        )(*args)

    return call


def group_specs(width, ff, start):
    heads = width // HEAD_DIM
    lanes = GROUP * SEQ
    deep = lambda i, info: (start + i, 0, 0)
    return (
        pl.BlockSpec((lanes, width), lambda i, info: (start + i, 0)),
        pl.BlockSpec((None, 3 * width, lanes), deep),
        pl.BlockSpec((None, GROUP * heads * SEQ, SEQ), deep),
        pl.BlockSpec((None, width, lanes), deep),
        pl.BlockSpec((None, ff, lanes), deep),
    )


def grid_call(kernel, info, start, stop, ins, outs, scratch, name, flops, before=()):
    return pl.pallas_call(
        kernel,
        grid_spec=pltpu.PrefetchScalarGridSpec(
            num_scalar_prefetch=1,
            grid=(stop - start,),
            in_specs=[spec or fixed(array.shape) for spec, array in ins] + [ANY] * len(before),
            out_specs=[spec or fixed(shape) for spec, shape, _ in outs],
            scratch_shapes=[pltpu.VMEM(*one) for one in scratch],
        ),
        out_shape=[shape_of(shape, dtype) for _, shape, dtype in outs],
        input_output_aliases={1 + len(ins) + i: i for i in range(len(before))},
        compiler_params=params(),
        cost_estimate=cost(flops * (stop - start), 4e6 * (stop - start)),
        name=name,
    )(info, *[array for _, array in ins], *before)


def order_ff(up_bias, par, half):
    parts = up_bias.reshape(half, 2, -1)
    return jnp.where(
        par == 0,
        jnp.concatenate([parts[:, 0], parts[:, 1]]),
        jnp.concatenate([parts[:, 1], parts[:, 0]]),
    ).reshape(-1)


def natural_ff(bias, half):
    return jnp.swapaxes(bias.reshape(2, half, -1), 0, 1).reshape(-1)


def spread_lanes(array):
    return jnp.broadcast_to(array[..., None], array.shape + (LANES,))


def body(
    block_in,
    out_grad,
    live_counts,
    qkv_weight,
    proj_weight,
    up_weight,
    down_weight,
    feature_vectors,
    up_bias,
    qkv_moment,
    proj_moment,
    up_moment,
    down_moment,
):
    devices = lax.axis_size("dp")
    half = devices // 2
    par = (lax.axis_index("dp") % 2).astype(jnp.int32)
    width = block_in.shape[1]
    groups = block_in.shape[0] // (GROUP * SEQ)
    ff = up_bias.shape[0]
    blocks = width // LANES
    turned = [w.T for w in (qkv_weight, proj_weight, up_weight, down_weight)]
    wq_s, wp_s, wu_s, wd_s = turned
    mq_s, mp_s, mu_s, md_s = [m.T for m in (qkv_moment, proj_moment, up_moment, down_moment)]
    cq, cp, cu, cd = (w.shape[0] for w in turned)
    pairs = [(i, i ^ 1) for i in range(devices)]
    planes = [[2 * i + c for i in range(half)] for c in range(2)]
    info = jnp.stack([live_counts[0], par])
    vec = spread_lanes(feature_vectors)
    ub = spread_lanes(order_ff(up_bias, par, half))

    def exchange(x):
        return lax.all_to_all(x, "dp", 0, 0, axis_index_groups=planes, tiled=True)

    def swap(x):
        return lax.ppermute(x, "dp", pairs)

    def after(x, *others):
        return lax.optimization_barrier((x,) + others)[0]

    first, second = small_call(
        prep_kernel,
        [((half, cq, width), bf16), ((half, -(-(cu + cd + cp) // 16) * 16, width), bf16)],
        "prep",
    )(wq_s, wp_s, wu_s, wd_s)
    lanes = GROUP * SEQ
    heads = width // HEAD_DIM
    tokens, qkv_spec, att_spec, deep_spec, ff_spec = group_specs(width, ff, 0)
    wide = (groups, width, lanes)
    z1 = grid_call(
        normal_kernel, after(info, ub), 0, groups, [(tokens, block_in), (None, vec)], [(deep_spec, wide, bf16)], [],
        "normal", 1e9,
    )[0]
    wq_own = after(exchange(first), z1)
    wq_other = swap(wq_own)
    rest_own = exchange(after(second, wq_own))

    def attend(start, stop, weights, before=()):
        _, qkv_at, att_at, deep_at, _ = group_specs(width, ff, start)
        fresh = start == 0
        return grid_call(
            functools.partial(attend_kernel, start), info, start, stop,
            [(deep_at, z1), (None, vec)] + [(None, w) for w in weights],
            [
                (qkv_at, (groups, 3 * width, lanes), bf16),
                (att_at, (groups, GROUP * heads * SEQ, SEQ), bf16),
                (deep_at, wide, bf16),
            ] + [(None, (3 * width, width), bf16)] * fresh,
            [
                ((3 * width, lanes), bf16),
                ((GROUP * heads, SEQ, SEQ), f32),
                ((GROUP * heads, SEQ, SEQ), bf16),
            ] + [((3 * width, width), f32)] * fresh,
            "attend", 4e9, before,
        )

    early = groups
    qkv, att, attn, wq = attend(0, early, (wq_own, wq_other))
    rest_own = after(rest_own, attn)
    rest_other = swap(rest_own)
    if early < groups:
        qkv, att, attn = attend(early, groups, (wq,), (qkv, att, attn))

    block = 256
    rows_b = 2 * cu + 4 + ff // width
    h1, act, dh, gp, wpn, wdn, keep_b, send_b = grid_call(
        mlp_kernel, info, 0, groups,
        [(tokens, block_in), (tokens, out_grad), (deep_spec, attn)]
        + [(None, array) for array in (rest_own, rest_other, vec, ub)],
        [
            (deep_spec, wide, f32),
            (ff_spec, (groups, ff, lanes), bf16),
            (deep_spec, wide, f32),
            (None, (width, width), f32),
            (None, (width, width), bf16),
            (None, (width, ff), bf16),
            (None, (half, rows_b, width), f32),
            (None, (half, rows_b, width), bf16),
        ],
        [
            ((width, ff), bf16),
            ((width, width), bf16),
            ((ff, width), bf16),
            ((ff, width), bf16),
            ((ff, width), f32),
            ((ff, width), f32),
            ((4, width, LANES), f32),
            ((ff, LANES), f32),
            ((width, lanes), f32),
            ((width, lanes), bf16),
            ((width, lanes), bf16),
            ((ff, lanes), bf16),
            ((ff, lanes), bf16),
            ((width, lanes), bf16),
            ((1, lanes), f32),
            ((ff, width), f32),
            ((2, block, lanes), f32),
            ((2, block, lanes), f32),
        ],
        "mlp", 10e9,
    )

    def back(start, stop, before=(), info=info):
        _, qkv_at, att_at, deep_at, _ = group_specs(width, ff, start)
        last = stop == groups
        rows = -(-(blocks * (cq + cp) + 4 * blocks) // 16) * 16
        totals = [(3 * width, width), (3, width, LANES)]
        scratch = [
            ((width, lanes), bf16),
            ((3 * width, lanes), bf16),
            ((GROUP * heads, SEQ, SEQ), f32),
            ((GROUP * heads, SEQ, SEQ), bf16),
        ]
        ins = [
            (deep_at, z1), (qkv_at, qkv), (att_at, att), (deep_at, dh),
            (None, wpn), (None, wq), (None, gp), (None, feature_vectors),
        ]
        outs = [(qkv_at, (groups, 3 * width, lanes), bf16)]
        if last:
            outs += [(None, (half, rows, LANES), f32), (None, (half, rows, LANES), bf16)]
            scratch = [(shape, f32) for shape in totals + [(rows, LANES)]] + scratch
        else:
            outs += [(None, shape, f32) for shape in totals]
        kernel = functools.partial(back_kernel, start, last)
        if not before:
            return grid_call(kernel, info, start, stop, ins, outs, scratch, "back", 6e9)
        ins += [(None, array) for array in before[1:]]
        return grid_call(kernel, info, start, stop, ins, outs, scratch, "back", 6e9, before[:1])

    def out_part(start, stop, info, before=()):
        tokens, _, _, deep_at, ff_at = group_specs(width, ff, start)
        return grid_call(
            functools.partial(out_kernel, start), info, start, stop,
            [(deep_at, h1), (ff_at, act), (None, wdn), (None, vec)],
            [(tokens, block_in.shape, f32)], [], "out", 1.5e9, before,
        )

    def input_part(start, stop, dqkv, info, before=()):
        tokens, qkv_at, _, deep_at, _ = group_specs(width, ff, start)
        return grid_call(
            functools.partial(input_kernel, start), info, start, stop,
            [(tokens, block_in), (qkv_at, dqkv), (deep_at, dh), (None, wq), (None, vec)],
            [(tokens, block_in.shape, f32)],
            [((width, 3 * width), bf16), ((1, lanes), f32), ((width, lanes), f32)], "input", 2e9, before,
        )

    def fold(keep, received):
        return (keep + received.astype(f32)).astype(bf16)

    def sums(got, moment_a, moment_b, vectors, spread, name):
        rows = moment_a.shape[0] + moment_b.shape[0]
        return small_call(
            state_kernel,
            [
                (moment_a.shape, f32), (moment_b.shape, f32), (moment_a.shape, f32), (moment_b.shape, f32),
                (spread, bf16), ((rows, width), f32), (vectors, f32),
            ],
            name + "_state",
            scalars=1,
        )(par.reshape(1), got, moment_a, moment_b)

    swapped = swap(send_b)
    one = 1 if groups > 2 else groups
    done = back(0, one)
    summed_b = fold(keep_b, after(swapped, done[1]))
    got_b = exchange(summed_b)
    if one < groups:
        done = back(one, groups, done, after(info, summed_b))
    dqkv, keep_a, send_a = done
    send_a, got_b = lax.optimization_barrier((send_a, got_b))
    summed_a = fold(keep_a, swap(send_a))
    got_a = exchange(summed_a)
    gate = after(info, summed_a)
    gu, gd, su, sd, spread_b, state_b, vector_b = sums(
        after(got_b, summed_a), mu_s, md_s, (4 + ff // width, width), (2, cu, width), "mlp"
    )

    bits = [1 << k for k in range(1, devices.bit_length() - 1)][::-1]

    def gather_step(pool, bit):
        return lax.ppermute(pool, "dp", [(i, i ^ bit) for i in range(devices)])

    def joined(pool, moved):
        return jnp.concatenate([pool, moved], axis=0)

    mid = groups // 2
    pool = joined(spread_b[0], swap(spread_b[1]))
    moved = gather_step(pool, bits[0])
    out = out_part(0, mid, after(gate, pool))
    for bit in bits[1:-2]:
        pool = joined(pool, after(moved, out[0]))
        moved = gather_step(pool, bit)
    out = out_part(mid, groups, after(gate, pool), out)
    got_a = after(got_a, out[0])
    gq, gpr, sq, sp, spread_a, state_a, vector_a = sums(
        got_a, mq_s, mp_s, (4 * blocks, LANES), (half, cq + cp, width), "att"
    )
    others_b = swap(state_b)
    own_a = exchange(spread_a)
    others_a = swap(state_a)
    pool = joined(pool, after(moved, spread_a))
    moved = gather_step(pool, bits[-2])
    dx = input_part(0, mid, dqkv, after(info, pool))
    pool = joined(pool, after(moved, dx[0]))
    moved = gather_step(pool, bits[-1])
    dx = input_part(mid, groups, dqkv, after(info, pool, others_a, others_b), dx)
    own_a = after(own_a, dx[0])
    other_a = swap(own_a)
    square = pltpu.VMEM((2, width, width), f32)
    parts = pltpu.VMEM((2, width, 3 * width), bf16)
    total = cq + cp + cu + cd
    mine, send = small_call(
        newton_kernel,
        [((total, width), f32), ((total, width), f32)],
        "newton",
        scalars=1,
        scratch=[square, square, square, parts, parts, parts, parts],
    )(
        jnp.stack([par, jnp.full((), cq, jnp.int32)]),
        own_a, other_a, pool, moved, state_a, others_a, state_b, others_b,
    )
    uq, up, uu, ud = small_call(
        functools.partial(update_kernel, tuple(w.shape[0] * devices for w in turned)),
        [(w.shape, f32) for w in turned],
        "update",
        scalars=1,
    )(par.reshape(1), mine, swap(send), *turned)
    out, dx = out[0], dx[0]

    vector_grad = jnp.concatenate([vector_a.reshape(4, width), vector_b[:4]], axis=0)
    bias_grad = natural_ff(vector_b[4:].reshape(ff), half)

    def normalized_step(param, gradient):
        return param - vector_rate * gradient * lax.rsqrt(
            jnp.mean(gradient * gradient, axis=-1, keepdims=True) + norm_eps
        )

    return (
        out, dx, gq.T, gpr.T, gu.T, gd.T, vector_grad, bias_grad, uq.T, up.T, uu.T, ud.T,
        sq.T, sp.T, su.T, sd.T,
        normalized_step(feature_vectors, vector_grad),
        normalized_step(up_bias, bias_grad),
    )


def solution(mesh):
    rows, columns, whole = P("dp", None), P(None, "dp"), P()
    return jax.shard_map(
        body,
        mesh=mesh,
        in_specs=(rows, rows, P("dp")) + (columns,) * 4 + (whole,) * 2 + (columns,) * 4,
        out_specs=(rows, rows) + (columns,) * 4 + (whole,) * 2 + (columns,) * 8 + (whole,) * 2,
        check_vma=False,
    )
```
